256 devices in a mesh: space: 32 (over z, y), exp: 8 (over x, core).
Axes of the slice: x: 4, y: 4, z: 8, core: 2. Of those that a mesh axis runs over, the one named last changes fastest.
Arguments:
- offsets: float32 [3, 8192, 128], P(None, ('space', 'exp')), may hold values from -1 to 1
- strength: float32 [3, 8192, 128], P(None, ('space', 'exp')), may hold values from -1.3 to 1.3
- leaf_cell: int32 [8192], P(('space', 'exp')), may hold values from 0 to 255, as said below
- leaf_count: int32 [32], P('space'), may hold values from 64 to 256, as said below
- leaf_fill: int32 [8192], P(('space', 'exp')), may hold values from 0 to 128, as said below
- near_list: int32 [18, 8192], P(None, ('space', 'exp')), may hold values from 0 to 8191, as said below
- near_count: int32 [8192], P(('space', 'exp')), may hold values from 0 to 18, as said below
Outputs:
- stream: float32 [3, 8192, 128], P(None, ('space', 'exp'))
The draws below stay inside these ranges and needn't reach their ends.
Inputs may be any that keep to these rules, and one draw needn't show every extreme that they name: `leaf_cell`: within each segment a permutation of the 256 cells of its slab; live slots hold the occupied cells in ascending order, dead slots the other cells in ascending order. `leaf_count`: two neighbouring segments are full in every draw, and some other segment holds exactly 64 live slots. `leaf_fill`: 0 for dead slots. `near_list`: the first near_count[g] entries of column g are the global slots of the live leaves whose cells differ from g's by at most 1 along every coordinate, g included, in ascending order of the offset (first coordinate slowest); the other entries equal g. `near_count`: 0 for dead slots.
All inputs are finite; a program needn't handle non-finite values.
Results may differ from the reference program's by a relative error of at most 0.0003.
Values sent between devices are 32-bit elements; how exact they have to be, the bound alone decides.
A program may use at most 128 MiB of HBM per device.

```python
import math
import jax
import jax.numpy as jnp
from jax import lax

LEAF_SIZE = 128
NEAR_MAX = 18
LEAF_SEG = 256
LEAVES = 8192
N_SPACE = 32


def geometry(key):
    segments = LEAVES // LEAF_SEG
    count_key = jax.random.fold_in(key, 11)
    counts = jax.random.randint(count_key, (segments,), LEAF_SEG // 4, LEAF_SEG + 1)
    first_full = jax.random.randint(jax.random.fold_in(count_key, 1), (), 0, segments - 1)
    seg_ids = jnp.arange(segments)
    counts = jnp.where(seg_ids == (first_full + 2) % segments, LEAF_SEG // 4, counts)
    counts = jnp.where((seg_ids == first_full) | (seg_ids == first_full + 1), LEAF_SEG, counts).astype(jnp.int32)
    scores = jax.random.randint(jax.random.fold_in(key, 12), (segments, LEAF_SEG), 0, 1 << 20) * LEAF_SEG + jnp.arange(LEAF_SEG)[None, :]
    ranks = jnp.argsort(jnp.argsort(scores, axis=1), axis=1)
    occupied = ranks < counts[:, None]
    order_key = jnp.where(occupied, 0, LEAF_SEG) + jnp.arange(LEAF_SEG)[None, :]
    cells = jnp.argsort(order_key, axis=1).astype(jnp.int32)
    return (counts, cells)


def near_lists(key):
    counts, cells = geometry(key)
    segments = LEAVES // LEAF_SEG
    span = LEAF_SEG // 4
    slot_ids = jnp.arange(LEAVES).astype(jnp.int32)
    seg_of = slot_ids // LEAF_SEG
    flat_cells = cells.reshape(LEAVES)
    live = slot_ids % LEAF_SEG < counts[seg_of]
    inverse = jnp.zeros((segments, LEAF_SEG), jnp.int32).at[seg_of, flat_cells].set(slot_ids)
    coord_first = 2 * seg_of + flat_cells // 2 % 2
    coord_second = flat_cells // 4
    coord_third = flat_cells % 2
    moves = jnp.arange(27)
    next_first = coord_first[:, None] + (moves // 9 - 1)[None, :]
    next_second = coord_second[:, None] + (moves // 3 % 3 - 1)[None, :]
    next_third = coord_third[:, None] + (moves % 3 - 1)[None, :]
    inside = (next_first >= 0) & (next_first < 2 * segments) & (next_second >= 0) & (next_second < span) & (next_third >= 0) & (next_third < 2)
    next_seg = jnp.clip(next_first // 2, 0, segments - 1)
    next_cell = jnp.clip(next_second, 0, span - 1) * 4 + next_first % 2 * 2 + jnp.clip(next_third, 0, 1)
    next_slot = inverse[next_seg, next_cell]
    next_live = next_slot % LEAF_SEG < counts[next_seg]
    valid = inside & next_live & live[:, None]
    order = jnp.argsort(jnp.where(valid, 0, 1) * 32 + moves[None, :], axis=1)
    picked = jnp.take_along_axis(next_slot, order, axis=1)[:, :NEAR_MAX]
    picked_valid = jnp.take_along_axis(valid, order, axis=1)[:, :NEAR_MAX]
    listing = jnp.where(picked_valid, picked, slot_ids[:, None])
    return (listing.T.astype(jnp.int32), jnp.sum(valid.astype(jnp.int32), axis=1).astype(jnp.int32))


def draw_leaf_count(key, part):
    return geometry(key)[0]


def draw_leaf_cell(key, part):
    return geometry(key)[1].reshape(LEAVES)


def draw_leaf_fill(key, part):
    counts, cells = geometry(key)
    raw = jax.random.randint(jax.random.fold_in(key, 13), (LEAVES,), LEAF_SIZE // 4, LEAF_SIZE + LEAF_SIZE // 4 + 1)
    raw = jnp.minimum(raw, LEAF_SIZE)
    slot_ids = jnp.arange(LEAVES)
    live = slot_ids % LEAF_SEG < counts[slot_ids // LEAF_SEG]
    return jnp.where(live, raw, 0).astype(jnp.int32)


def draw_near_list(key, part):
    return near_lists(key)[0]


def draw_near_count(key, part):
    return near_lists(key)[1]


def draw_strength(key, part):
    shape = (3, LEAVES, LEAF_SIZE)
    return jnp.clip(0.2 * jax.random.normal(jax.random.fold_in(key, 1), shape, jnp.float32), -1.3, 1.3)


def shard_levels(key, extent, shards, least, largest):
    def one(axis_at, blocks):
        steps = jax.random.uniform(jax.random.fold_in(jax.random.fold_in(key, 6), axis_at), (blocks,), jnp.float32, least / len(shards), largest / len(shards))
        return jnp.repeat(jnp.exp(steps), extent[axis_at] // blocks).reshape((-1,) + (1,) * (len(extent) - axis_at - 1))

    gain = one(*shards[0])
    for cut in shards[1:]:
        gain = gain * one(*cut)
    return gain


def setup_inputs(seed: int = 0) -> dict:
    key_list = jax.random.split(jax.random.key(seed), 8)
    return {
        "offsets": jnp.clip(jax.random.uniform(key_list[0], (3, LEAVES, LEAF_SIZE), jnp.float32, -1.0, 1.0) * shard_levels(key_list[0], (3, LEAVES, LEAF_SIZE), ((1, 256),), -0.4, 0.0), -1.0, 1.0),
        "strength": draw_strength(jax.random.fold_in(key_list[7], 71), 0),
        "leaf_cell": draw_leaf_cell(jax.random.fold_in(key_list[7], 71), 0),
        "leaf_count": draw_leaf_count(jax.random.fold_in(key_list[7], 71), 0),
        "leaf_fill": draw_leaf_fill(jax.random.fold_in(key_list[7], 71), 0),
        "near_list": draw_near_list(jax.random.fold_in(key_list[7], 71), 0),
        "near_count": draw_near_count(jax.random.fold_in(key_list[7], 71), 0),
    }


cheb_points = 4
smoothing_sq = 0.01
four_pi = 4.0 * math.pi
highest = lax.Precision.HIGHEST

def cheb_nodes():
    orders = jnp.arange(cheb_points, dtype=jnp.float32)
    return jnp.cos((2.0 * orders + 1.0) * math.pi / (2.0 * cheb_points))

def cheb_poly(values):
    quadratic = 2.0 * values * values - 1.0
    third_term = 4.0 * values * values * values - 3.0 * values
    return jnp.stack([values, quadratic, third_term])

def interp_weights(points):
    node_values = cheb_nodes()
    node_poly = cheb_poly(node_values)
    factors = []
    for axis_num in range(3):
        polynomials = cheb_poly(points[axis_num])
        factors.append(0.25 + 0.5 * jnp.einsum('mk,mn->kn', node_poly, polynomials, precision=highest))
    weights = factors[0][:, None, None, :] * factors[1][None, :, None, :] * factors[2][None, None, :, :]
    return weights.reshape(64, points.shape[-1])

def node_grid():
    node_values = cheb_nodes()
    node_index = jnp.arange(64)
    return jnp.stack([node_values[node_index // 16], node_values[node_index // 4 % 4], node_values[node_index % 4]])

def kernel(first_diff, second_diff, third_diff):
    return lax.rsqrt(first_diff * first_diff + second_diff * second_diff + third_diff * third_diff + smoothing_sq) / four_pi

def child_table():
    nodes_xyz = node_grid()
    child_ids = jnp.arange(8)
    child_bits = jnp.stack([child_ids // 2 % 2, child_ids // 4, child_ids % 2]).astype(jnp.float32)
    points = child_bits[:, :, None] - 0.5 + 0.5 * nodes_xyz[:, None, :]
    weights = interp_weights(points.reshape(3, 8 * 64))
    return weights.reshape(64, 8, 64).transpose(1, 2, 0)

def shell_table():
    nodes_xyz = node_grid()
    child_ids = jnp.arange(8)
    first_bit = (child_ids // 2 % 2).astype(jnp.float32)
    second_bit = (child_ids // 4).astype(jnp.float32)
    third_bit = (child_ids % 2).astype(jnp.float32)
    window_ids = jnp.arange(72)
    block_pos = (window_ids // 24).astype(jnp.float32)
    height_pos = (window_ids // 4 % 6).astype(jnp.float32)
    first_src = (window_ids // 2 % 2).astype(jnp.float32)
    third_src = (window_ids % 2).astype(jnp.float32)
    first_step = 2.0 * block_pos[None, :] - 2.0 + first_src[None, :] - first_bit[:, None]
    second_step = height_pos[None, :] - 2.0 - second_bit[:, None]
    third_step = third_src[None, :] - third_bit[:, None]
    apart = jnp.maximum(jnp.maximum(jnp.abs(first_step), jnp.abs(second_step)), jnp.abs(third_step)) > 1.5
    halves = 0.5 * (nodes_xyz[:, :, None] - nodes_xyz[:, None, :])
    values = kernel(halves[0] - first_step[:, :, None, None], halves[1] - second_step[:, :, None, None], halves[2] - third_step[:, :, None, None])
    return jnp.where(apart[:, :, None, None], values, 0.0)

def far_block(target_first, target_second, source_first, source_second):
    nodes_xyz = node_grid()
    spread = nodes_xyz[:, :, None] - nodes_xyz[:, None, :]
    first_step = 2.0 * (target_first[:, None] - source_first[None, :])
    second_step = 2.0 * (target_second[:, None] - source_second[None, :])
    far_mask = (jnp.abs(first_step) > 3.0) | (jnp.abs(second_step) > 3.0)
    values = kernel(first_step[:, :, None, None] + spread[0], second_step[:, :, None, None] + spread[1], spread[2])
    return jnp.where(far_mask[:, :, None, None], values, 0.0)

def near_sum(target_position, source_position, source_charge):
    differences = target_position[None, :, None, :] - source_position[:, :, :, None]
    values = kernel(differences[:, 0], differences[:, 1], differences[:, 2])
    return jnp.einsum('kcm,kmn->cn', source_charge, values, precision=highest)

def reference(offsets, strength, leaf_cell, leaf_count, leaf_fill, near_list, near_count):
    leaf_total = offsets.shape[1]
    leaf_size = offsets.shape[2]
    seg_leaves = leaf_total // N_SPACE
    cells_along = seg_leaves // 4
    seg_parents = seg_leaves // 8
    slot_ids = jnp.arange(leaf_total).astype(jnp.int32)
    segment_of = (slot_ids // seg_leaves).astype(jnp.int32)
    live_leaf = slot_ids % seg_leaves < leaf_count[segment_of]
    particle_live = (jnp.arange(leaf_size)[None, :] < leaf_fill[:, None]) & live_leaf[:, None]
    live_float = particle_live.astype(jnp.float32)
    charges = strength * live_float[None]
    weights = interp_weights(offsets.reshape(3, leaf_total * leaf_size)).reshape(64, leaf_total, leaf_size)
    multipole = jnp.einsum('cli,ali->lca', charges, weights, precision=highest)
    first_cell = 2 * segment_of + leaf_cell // 2 % 2
    centers = jnp.stack([first_cell, leaf_cell // 4, leaf_cell % 2]).astype(jnp.float32) + 0.5
    positions = centers[:, :, None] + 0.5 * offsets
    cell_grid = jnp.zeros((N_SPACE + 2, cells_along + 4, 2, 2, 192), jnp.float32)
    cell_grid = cell_grid.at[segment_of + 1, leaf_cell // 4 + 2, leaf_cell // 2 % 2, leaf_cell % 2].add(multipole.reshape(leaf_total, 192))
    inner = cell_grid[1:N_SPACE + 1, 2:cells_along + 2].reshape(N_SPACE * seg_parents, 8, 3, 64)
    children = child_table()
    parent_multipole = jnp.einsum('pkca,kab->pcb', inner, children, precision=highest)
    parent_ids = jnp.arange(N_SPACE * seg_parents).astype(jnp.int32)
    parent_first = (parent_ids // seg_parents).astype(jnp.float32)
    parent_second = (parent_ids % seg_parents).astype(jnp.float32)

    def far_local(target):
        values = far_block(parent_first[target][None], parent_second[target][None], parent_first, parent_second)[0]
        return jnp.einsum('qab,qcb->ca', values, parent_multipole, precision=highest)
    parent_local = lax.map(far_local, parent_ids)
    shells = shell_table()
    zero_index = jnp.zeros((), jnp.int32)

    def leaf_value(slot_index):
        segment = segment_of[slot_index]
        target_cell = leaf_cell[slot_index]
        target_position = positions[:, slot_index]
        near_ids = near_list[:, slot_index]
        listed = (jnp.arange(near_ids.shape[0]) < near_count[slot_index]).astype(jnp.float32)
        source_position = positions[:, near_ids].transpose(1, 0, 2)
        source_charge = charges[:, near_ids].transpose(1, 0, 2) * listed[:, None, None]
        near_part = near_sum(target_position, source_position, source_charge)
        parent_row = (target_cell // 8).astype(jnp.int32)
        child_index = target_cell % 8
        window_block = lax.dynamic_slice(cell_grid, (segment.astype(jnp.int32), (2 * parent_row).astype(jnp.int32), zero_index, zero_index, zero_index), (3, 6, 2, 2, 192)).reshape(72, 3, 64)
        expansion = jnp.einsum('wab,wcb->ca', shells[child_index], window_block, precision=highest)
        expansion = expansion + jnp.einsum('cb,ab->ca', parent_local[segment * seg_parents + parent_row], children[child_index], precision=highest)
        far_part = jnp.einsum('ca,an->cn', expansion, interp_weights(offsets[:, slot_index]), precision=highest)
        return (near_part + far_part) * live_float[slot_index][None, :]
    stream = lax.map(leaf_value, slot_ids)
    return stream.transpose(1, 0, 2)
```

```python
import math

import jax
import jax.numpy as jnp
from jax import lax
from jax.experimental import pallas as pl
from jax.experimental.pallas import tpu as pltpu
from jax.sharding import PartitionSpec as P

NODES = [math.cos((2 * k + 1) * math.pi / 8) for k in range(4)]
SMOOTH = 0.01
SCALE = 1.0 / (4.0 * math.pi)
F32 = jnp.float32
BF16 = jnp.bfloat16
VMEM = pl.BlockSpec(memory_space=pltpu.VMEM)
SMEM = pl.BlockSpec(memory_space=pltpu.SMEM)
ANY = pl.BlockSpec(memory_space=pl.ANY)
BIG = 60 * 1024 * 1024
NN = (((1,), (0,)), ((), ()))
NT = (((1,), (1,)), ((), ()))


def iota(shape, axis):
    return lax.broadcasted_iota(jnp.int32, shape, axis)


def split2(x):
    hi = x.astype(BF16)
    return hi, (x - hi.astype(F32)).astype(BF16)


def bdot(a, b, dims=NN):
    return lax.dot_general(a, b, dims, preferred_element_type=F32)


def dot3(a, b, dims=NN):
    ah, al = a if isinstance(a, tuple) else split2(a)
    bh, bl = b if isinstance(b, tuple) else split2(b)
    return bdot(ah, bh, dims) + (bdot(al, bh, dims) + bdot(ah, bl, dims))


def pick_exact(one_hot, x):
    hi = x.astype(BF16)
    rest = x - hi.astype(F32)
    mid = rest.astype(BF16)
    low = (rest - mid.astype(F32)).astype(BF16)
    return bdot(one_hot, hi) + (bdot(one_hot, mid) + bdot(one_hot, low))


def node(k):
    return jnp.where(
        k == 0, NODES[0], jnp.where(k == 1, NODES[1], jnp.where(k == 2, NODES[2], NODES[3]))
    ).astype(F32)


def cheb(u):
    return u, 2.0 * u * u - 1.0, (4.0 * u * u - 3.0) * u


def factors(u):
    t1, t2, t3 = cheb(u)
    out = []
    for t in NODES:
        out.append(0.25 + t1 * (0.5 * t) + t2 * (0.5 * (2 * t * t - 1)) + t3 * (0.5 * (4 * t**3 - 3 * t)))
    return out


def cheb_pair(u, t):
    u1, u2, u3 = cheb(u)
    t1, t2, t3 = cheb(t)
    return 0.25 + 0.5 * (u1 * t1 + u2 * t2 + u3 * t3)


def column(row, count):
    spread = jnp.where(iota((count, count), 0) == iota((count, count), 1), row.astype(F32), 0.0)
    return jnp.sum(spread, axis=1, keepdims=True)


def weights_loop(offs, visit):
    fx, fy, fz = (factors(o) for o in offs)
    for i in range(4):
        for j in range(4):
            fxy = fx[i] * fy[j]
            for k in range(4):
                visit(16 * i + 4 * j + k, fxy * fz[k])


def particle_kernel(off_ref, str_ref, cell_ref, count_ref, fill_ref, rec_ref):
    leaf, size = off_ref.shape[1], off_ref.shape[2]
    seg, ex = lax.axis_index("space"), lax.axis_index("exp")
    cell_f = column(cell_ref[...], leaf)
    fill = column(fill_ref[...], leaf)
    cell = cell_f.astype(jnp.int32)
    slot = ex * leaf + iota((leaf, size), 0)
    alive = (slot < count_ref[0]) & (iota((leaf, size), 1).astype(F32) < fill)
    centre = (
        2 * seg + ((cell >> 1) & 1),
        cell >> 2,
        cell & 1,
    )
    offs = [off_ref[a] for a in range(3)]
    charge = []
    for a in range(3):
        pos = (centre[a].astype(F32) + 0.5) + 0.5 * offs[a]
        rec_ref[pl.ds(a, leaf, 8), :] = pos
        q = jnp.where(alive, str_ref[a], 0.0)
        rec_ref[pl.ds(3 + a, leaf, 8), :] = q
        charge.append(q)
    lane = iota((leaf, size), 1)
    acc = [jnp.zeros((leaf, size), F32), jnp.where(lane >= 64, cell_f, 0.0)]

    def visit(a, w):
        for c in range(3):
            total = jnp.sum(charge[c] * w, axis=1, keepdims=True)
            at = a + 64 * (c % 2)
            acc[c // 2] = jnp.where(lane == at, total, acc[c // 2])

    weights_loop(offs, visit)
    rec_ref[pl.ds(6, leaf, 8), :] = acc[0]
    rec_ref[pl.ds(7, leaf, 8), :] = acc[1]


def mesh_at(seg, ex):
    return {"space": seg, "exp": ex}


def remote(src, dst, send, recv, seg, ex):
    return pltpu.make_async_remote_copy(
        src_ref=src, dst_ref=dst, send_sem=send, recv_sem=recv,
        device_id=mesh_at(seg, ex), device_id_type=pl.DeviceIdType.MESH,
    )


def greet(devices):
    barrier = pltpu.get_barrier_semaphore()
    for seg, ex in devices:
        pl.semaphore_signal(barrier, 1, device_id=mesh_at(seg, ex), device_id_type=pl.DeviceIdType.MESH)
    pl.semaphore_wait(barrier, len(devices))


def gather_kernel(n_seg, n_x, rec_ref, out_ref, send, recv, own_sem):
    seg, ex = lax.axis_index("space"), lax.axis_index("exp")
    x, core = ex // 2, ex % 2
    prev, after = (seg + n_seg - 1) % n_seg, (seg + 1) % n_seg
    ring = [((x + d) % n_x) * 2 + core for d in range(n_x)]
    order = [1, n_x - 1] + list(range(2, n_x - 1))
    mate = x * 2 + 1 - core
    mates = [((x + d) % n_x) * 2 + 1 - core for d in range(n_x)]
    greet([(seg, ring[d]) for d in order] + [(seg, mate), (prev, ex), (after, ex)])
    sent = []

    def push(src, part, who, to_seg, to_ex):
        copy = remote(src, out_ref.at[part, who], send.at[len(sent)], recv.at[part, who], to_seg, to_ex)
        copy.start()
        sent.append(copy)

    def arrived(part, who):
        remote(rec_ref, out_ref.at[part, who], send.at[0], recv.at[part, who], seg, mate).wait_recv()

    push(rec_ref, 0, ex, after, ex)
    push(rec_ref, 2, ex, prev, ex)
    for d in order:
        push(rec_ref, 1, ex, seg, ring[d])
    push(rec_ref, 1, ex, seg, mate)
    keep = pltpu.make_async_copy(rec_ref, out_ref.at[1, ex], own_sem)
    keep.start()
    for d in order:
        arrived(1, ring[d])
        push(out_ref.at[1, ring[d]], 0, ring[d], after, ex)
        push(out_ref.at[1, ring[d]], 2, ring[d], prev, ex)
        push(out_ref.at[1, ring[d]], 1, ring[d], seg, mate)
    for d in [0] + order:
        for part in (0, 2):
            arrived(part, ring[d])
            push(out_ref.at[part, ring[d]], part, ring[d], seg, mate)
    for d in range(n_x):
        for part in range(3):
            arrived(part, mates[d])
    keep.wait()
    for copy in sent:
        copy.wait_send()


def sorted_block(win_ref, base, slots, guard):
    m01 = win_ref[pl.ds(base + 6, slots, 8), :]
    m2c = win_ref[pl.ds(base + 7, slots, 8), :]
    cells = jnp.swapaxes(m2c, 0, 1)[64:65, :]
    row = iota((slots, slots), 0)
    wanted = ((row % (slots // 8)) * 8 + row // (slots // 8)).astype(F32)
    one_hot = jnp.where((wanted == cells) & guard, 1.0, 0.0).astype(BF16)
    return pick_exact(one_hot, m01), pick_exact(one_hot, m2c)


def parent_kernel(win_ref, out_ref):
    slots = win_ref.shape[0] // 8
    par = slots // 8
    g01, g2 = sorted_block(win_ref, 0, slots, True)
    total = jnp.zeros((2 * par, 128), F32)
    lane_b = iota((128, 128), 1)
    row_a = iota((128, 128), 0)
    bx, by, bz = (node((lane_b // w) % 4) for w in (16, 4, 1))
    ax, ay, az = (node((row_a // w) % 4) for w in (16, 4, 1))
    sx, sy, sz = ([cheb_pair(bit - 0.5 + 0.5 * a, b) for bit in (0, 1)] for a, b in ((ax, bx), (ay, by), (az, bz)))
    same = (lane_b // 64) == (row_a // 64)
    for h in range(8):
        table = jnp.where(same, sx[(h // 2) % 2] * sy[h // 4] * sz[h % 2], 0.0)
        lhs = jnp.concatenate([g01[h * par : (h + 1) * par], g2[h * par : (h + 1) * par]], axis=0)
        total = total + dot3(lhs, table)
    out_ref[...] = total


def swap_kernel(per, pm_ref, out_ref, send, recv, own_sem):
    seg, ex = lax.axis_index("space"), lax.axis_index("exp")
    there = seg // per
    mine = ex == there
    barrier = pltpu.get_barrier_semaphore()

    def copy(i):
        return remote(pm_ref, out_ref.at[seg % per], send.at[i], recv.at[seg % per], ex * per + i, there)

    def local():
        return pltpu.make_async_copy(pm_ref, out_ref.at[seg % per], own_sem)

    for i in range(per):
        here = mine & (seg % per == i)

        @pl.when(jnp.logical_not(here))
        def _():
            pl.semaphore_signal(barrier, 1, device_id=mesh_at(ex * per + i, there), device_id_type=pl.DeviceIdType.MESH)

    pl.semaphore_wait(barrier, jnp.where(mine, per - 1, per))
    for i in range(per):
        here = mine & (seg % per == i)

        @pl.when(jnp.logical_not(here))
        def _():
            copy(i).start()

        @pl.when(here)
        def _():
            local().start()

    for i in range(per):
        here = mine & (seg % per == i)

        @pl.when(jnp.logical_not(here))
        def _():
            remote(pm_ref, out_ref.at[i], send.at[i], recv.at[i], ex * per + i, there).wait_recv()
            copy(i).wait_send()

        @pl.when(here)
        def _():
            local().wait()


def far_kernel(n_seg, pq_ref, out_ref, base_ref):
    per = pq_ref.shape[0]
    par = pq_ref.shape[1] // 2
    wide = per * 64
    seg, ex = lax.axis_index("space"), lax.axis_index("exp")
    rows = []
    for c in range(3):
        r0, l0 = par * (c // 2), 64 * (c % 2)
        rows.append(jnp.concatenate([pq_ref[q, r0 : r0 + par, l0 : l0 + 64] for q in range(per)], axis=1))
    rows.append(jnp.zeros((128 - 3 * par, wide), F32))
    ph, plo = split2(jnp.concatenate(rows, axis=0))
    lane, row = iota((64, wide), 1), iota((64, wide), 0)
    step = (seg - ex * per - lane // 64).astype(F32)
    dx = 2.0 * step + node(row // 16) - node((lane // 16) % 4)
    dz = node(row % 4) - node(lane % 4)
    base_ref[0] = dx * dx + (dz * dz + SMOOTH)
    base_ref[1] = node((row // 4) % 4) - node((lane // 4) % 4)
    base_ref[2] = jnp.where(jnp.abs(step) < 1.5, jnp.inf, 0.0)
    to = iota((64, 128), 1)
    p_to = to % par
    acc = jnp.zeros((64, 128), F32)

    def one(delta, acc):
        dy = base_ref[1] + 2.0 * delta.astype(F32)
        gap = jnp.where(jnp.abs(delta) <= 1, jnp.inf, 0.0)
        g = lax.rsqrt(dy * dy + base_ref[0] + jnp.minimum(base_ref[2], gap))
        gh, gl = split2(g)
        got = bdot(gh, ph, NT) + (bdot(gl, ph, NT) + bdot(gh, plo, NT))
        moved = pltpu.roll(got, (delta + 128) % 128, 1)
        source = p_to - delta
        return acc + jnp.where((source >= 0) & (source < par), moved, 0.0)

    def some(i, acc):
        for u in range(3):
            acc = one(i * 3 + u - (par - 1), acc)
        return acc

    out_ref[...] = lax.fori_loop(0, (2 * par - 1) // 3, some, acc)


def share_kernel(n_ex, part_ref, out_ref, send, recv, own_sem):
    seg, ex = lax.axis_index("space"), lax.axis_index("exp")
    others = [(ex + d) % n_ex for d in range(1, n_ex)]
    greet([(seg, o) for o in others])
    copies = [remote(part_ref, out_ref.at[ex], send.at[i], recv.at[ex], seg, o) for i, o in enumerate(others)]
    for copy in copies:
        copy.start()
    keep = pltpu.make_async_copy(part_ref, out_ref.at[ex], own_sem)
    keep.start()
    for i, o in enumerate(others):
        remote(part_ref, out_ref.at[o], send.at[i], recv.at[o], seg, o).wait_recv()
    keep.wait()
    for copy in copies:
        copy.wait_send()


def final_kernel(
    n_seg, fill_ref, near_ref, many_ref, count_ref, off_ref, cell_ref, win_ref, part_ref, out_ref,
    grid_ref, base_ref, near_x_ref, loc_ref, xb_ref,
):
    leaf, size = off_ref.shape[1], off_ref.shape[2]
    seg, ex = lax.axis_index("space"), lax.axis_index("exp")
    slots = win_ref.shape[0] // 3
    win_rows = win_ref.reshape(3 * slots * 8, size)
    par = slots // 8
    grid_ref[...] = jnp.zeros(grid_ref.shape, F32)
    for j in range(3):
        guard = True if j == 1 else ((seg > 0) if j == 0 else (seg < n_seg - 1))
        g01, g2 = sorted_block(win_rows, j * slots * 8, slots, guard)
        for odd in range(2):
            for c in range(3):
                src = g01 if c < 2 else g2
                lo = 64 * (c % 2)
                block = jnp.concatenate(
                    [src[(4 * odd + r) * par : (4 * odd + r + 1) * par, lo : lo + 64] for r in range(4)], axis=1
                )
                grid_ref[j * 2 + odd, c, 8 : 8 + par, :] = block
    parent = part_ref[0]
    for i in range(1, part_ref.shape[0]):
        parent = parent + part_ref[i]
    parent = jnp.swapaxes(parent, 0, 1)[: 3 * par, :]
    lane, row = iota((64, 512), 1), iota((64, 512), 0)
    table = 1.0
    for bit, w in (((lane // 128) % 2, 16), (lane // 256, 4), ((lane // 64) % 2, 1)):
        table = table * cheb_pair(bit.astype(F32) - 0.5 + 0.5 * node((lane // w) % 4), node((row // w) % 4))
    loc_ref[...] = dot3(parent, table)
    lane, row = iota((256, 512), 1), iota((256, 512), 0)
    ux = ((lane // 128) % 2).astype(F32) + 0.5 * node((lane // 16) % 4)
    vx = (row // 128).astype(F32) + 0.5 * node((row // 16) % 4)
    uz = ((lane // 64) % 2).astype(F32) + 0.5 * node(lane % 4)
    vz = ((row // 64) % 2).astype(F32) + 0.5 * node(row % 4)
    base_ref[1] = (uz - vz) * (uz - vz) + SMOOTH
    base_ref[2] = ux - vx
    near_x_ref[1] = ((row // 128) - (lane // 128) % 2).astype(F32)
    lane1 = iota((1, 512), 1)
    uy = (lane1 // 256).astype(F32) + 0.5 * node((lane1 // 4) % 4)
    up1 = (lane1 // 256).astype(F32)
    vy = 0.5 * node((iota((256, 1), 0) // 4) % 4)

    def m2l_seg(j, carry):
        shift = 2.0 * j.astype(F32) - 2.0
        dx = base_ref[2] - shift
        base_ref[0] = dx * dx + base_ref[1]
        near_x_ref[0] = jnp.where(jnp.abs(near_x_ref[1] + shift) < 1.5, jnp.inf, 0.0)
        for odd in range(2):
            for i in range(3):
                height = 2 * i + odd - 2
                lhs = jnp.concatenate([grid_ref[j * 2 + odd, c, 7 + i : 7 + i + par, :] for c in range(3)], axis=0)
                near_y = jnp.where(jnp.abs(height - up1) < 1.5, jnp.inf, 0.0)
                dy = (uy - height) - vy
                g = lax.rsqrt(dy * dy + base_ref[0] + jnp.minimum(near_x_ref[0], near_y))
                loc_ref[...] += dot3(lhs, g)
        return carry

    lax.fori_loop(0, 3, m2l_seg, 0)
    cell = column(cell_ref[...], leaf).astype(jnp.int32)
    chosen = jnp.where((cell >> 3) == iota((leaf, par), 1), 1.0, 0.0).astype(BF16)
    child = cell & 7
    lane = iota((leaf, 128), 1)
    expansion = []
    for c in range(3):
        wide = pick_exact(chosen, loc_ref[c * par : (c + 1) * par, :])
        kept = jnp.zeros((leaf, 128), F32)
        for i in range(4):
            kept = kept + jnp.where(lane // 64 + 2 * i == child, wide[:, 128 * i : 128 * i + 128], 0.0)
        expansion.append(kept + pltpu.roll(kept, 64, 1))
    far = [jnp.zeros((leaf, size), F32) for _ in range(3)]

    def visit(a, w):
        for c in range(3):
            far[c] = far[c] + expansion[c][:, a : a + 1] * w

    weights_loop([off_ref[a] for a in range(3)], visit)
    for c in range(3):
        out_ref[c] = far[c]
    start = (seg - 1) * slots
    block = 64
    zeros = jnp.zeros((block, size), F32)

    def target(t, carry):
        fill = fill_ref[t]
        many = many_ref[t]
        turned = jnp.swapaxes(win_ref[slots + ex * leaf + t], 0, 1)
        for a in range(3):
            xb_ref[a] = jnp.broadcast_to(turned[:, a : a + 1], (size, size))
            xb_ref[3 + a] = jnp.zeros((size, size), F32)

        def rows(n, carry):
            at = pl.multiple_of(n * block, block)

            def step(k3, acc):
                acc = list(acc)
                for u in range(3):
                    k = k3 * 3 + u
                    m = near_ref[k, t] - start
                    on = jnp.where(k < many, 1.0, 0.0).astype(F32)
                    dx = xb_ref[0, pl.ds(at, block), :] - win_ref[m, 0:1, :]
                    dy = xb_ref[1, pl.ds(at, block), :] - win_ref[m, 1:2, :]
                    dz = xb_ref[2, pl.ds(at, block), :] - win_ref[m, 2:3, :]
                    g = lax.rsqrt(dx * dx + (dy * dy + (dz * dz + SMOOTH)))
                    for c in range(3):
                        acc[c] = acc[c] + g * (win_ref[m, 3 + c : 4 + c, :] * on)
                return tuple(acc)

            acc = lax.fori_loop(0, (many + 2) // 3, step, (zeros, zeros, zeros))
            for c in range(3):
                xb_ref[3 + c, pl.ds(at, block), :] = acc[c]
            return carry

        lax.fori_loop(0, (fill + block - 1) // block, rows, 0)
        lane = iota((size, size), 1)
        cols = jnp.zeros((size, size), F32)
        for c in range(3):
            cols = jnp.where(lane == c, jnp.sum(xb_ref[3 + c], axis=1, keepdims=True), cols)
        result = jnp.swapaxes(cols, 0, 1)
        live = iota((1, size), 1) < fill
        for c in range(3):
            total = (result[c : c + 1, :] + out_ref[c, pl.ds(t, 1), :]) * SCALE
            out_ref[c, pl.ds(t, 1), :] = jnp.where(live, total, 0.0)
        return carry

    turns = jnp.clip(count_ref[0] - ex * leaf, 0, leaf)
    lax.fori_loop(0, turns, target, 0)

    def blank(t, carry):
        for c in range(3):
            out_ref[c, pl.ds(t, 1), :] = jnp.zeros((1, size), F32)
        return carry

    lax.fori_loop(turns, leaf, blank, 0)


def shape(*dims):
    return jax.ShapeDtypeStruct(dims, F32)


def particle_call(offsets, strength, cell_row, leaf_count, fill_row):
    leaf, size = offsets.shape[1], offsets.shape[2]
    return pl.pallas_call(
        particle_kernel,
        out_shape=shape(leaf * 8, size),
        in_specs=[VMEM, VMEM, VMEM, SMEM, VMEM],
        out_specs=VMEM,
    )(offsets, strength, cell_row, leaf_count, fill_row)


def parent_call(window):
    slots = window.shape[0] // 3
    return pl.pallas_call(
        parent_kernel,
        grid=(1,),
        out_shape=shape(slots // 4, 128),
        in_specs=[pl.BlockSpec((slots * 8, 128), lambda i: (1, 0))],
        out_specs=pl.BlockSpec((slots // 4, 128), lambda i: (0, 0)),
    )(window.reshape(3 * slots * 8, 128))


def far_call(n_seg, pq):
    per = pq.shape[0]
    return pl.pallas_call(
        lambda *refs: far_kernel(n_seg, *refs),
        out_shape=shape(64, 128),
        in_specs=[VMEM],
        out_specs=VMEM,
        scratch_shapes=[pltpu.VMEM((3, 64, per * 64), F32)],
    )(pq)


def final_call(n_seg, fill, near, many, count, offsets, cell_row, window, parts):
    leaf, size = offsets.shape[1], offsets.shape[2]
    slots = window.shape[0] // 3
    par = slots // 8
    return pl.pallas_call(
        lambda *refs: final_kernel(n_seg, *refs),
        out_shape=shape(3, leaf, size),
        in_specs=[SMEM, SMEM, SMEM, SMEM, VMEM, VMEM, VMEM, VMEM],
        out_specs=VMEM,
        scratch_shapes=[
            pltpu.VMEM((6, 3, par + 16, 256), F32),
            pltpu.VMEM((3, 256, 512), F32),
            pltpu.VMEM((2, 256, 512), F32),
            pltpu.VMEM((3 * par, 512), F32),
            pltpu.VMEM((6, size, size), F32),
        ],
        compiler_params=pltpu.CompilerParams(vmem_limit_bytes=BIG),
    )(fill, near, many, count, offsets, cell_row, window, parts)


def solution(mesh):
    n_seg, n_ex = mesh.shape["space"], mesh.shape["exp"]
    per = n_seg // n_ex
    n_x = n_ex // 2
    dma = pltpu.SemaphoreType.DMA

    def body(offsets, strength, leaf_cell, leaf_count, leaf_fill, near_list, near_count):
        leaf, size = offsets.shape[1], offsets.shape[2]
        slots = leaf * n_ex
        cell_row = leaf_cell.reshape(1, leaf)
        fill_row = leaf_fill.reshape(1, leaf)
        record = particle_call(offsets, strength, cell_row, leaf_count, fill_row).reshape(leaf, 8, size)
        window = pl.pallas_call(
            lambda *refs: gather_kernel(n_seg, n_x, *refs),
            out_shape=shape(3, n_ex, leaf, 8, size),
            in_specs=[VMEM],
            out_specs=ANY,
            scratch_shapes=[dma((6 * n_x - 1,)), dma((3, n_ex)), dma],
            compiler_params=pltpu.CompilerParams(collective_id=0, has_side_effects=True),
        )(record).reshape(3 * slots, 8, size)
        pm = parent_call(window)
        pq = pl.pallas_call(
            lambda *refs: swap_kernel(per, *refs),
            out_shape=shape(per, *pm.shape),
            in_specs=[VMEM],
            out_specs=ANY,
            scratch_shapes=[dma((per,)), dma((per,)), dma],
            compiler_params=pltpu.CompilerParams(collective_id=1, has_side_effects=True),
        )(pm)
        part = far_call(n_seg, pq)
        parts = pl.pallas_call(
            lambda *refs: share_kernel(n_ex, *refs),
            out_shape=shape(n_ex, *part.shape),
            in_specs=[VMEM],
            out_specs=ANY,
            scratch_shapes=[dma((n_ex - 1,)), dma((n_ex,)), dma],
            compiler_params=pltpu.CompilerParams(collective_id=2, has_side_effects=True),
        )(part)
        return final_call(n_seg, leaf_fill, near_list, near_count, leaf_count, offsets, cell_row, window, parts)

    in_specs = (
        P(None, ("space", "exp"), None),
        P(None, ("space", "exp"), None),
        P(("space", "exp")),
        P("space"),
        P(("space", "exp")),
        P(None, ("space", "exp")),
        P(("space", "exp")),
    )
    out_specs = P(None, ("space", "exp"), None)
    return jax.shard_map(body, mesh=mesh, in_specs=in_specs, out_specs=out_specs, check_vma=False)
```

```python
import math

import jax
import jax.numpy as jnp
from jax import lax
from jax.experimental import pallas as pl
from jax.experimental.pallas import tpu as pltpu
from jax.sharding import PartitionSpec as P

NODES = [math.cos((2 * k + 1) * math.pi / 8) for k in range(4)]
SMOOTH = 0.01
SCALE = 1.0 / (4.0 * math.pi)
F32 = jnp.float32
BF16 = jnp.bfloat16
VMEM = pl.BlockSpec(memory_space=pltpu.VMEM)
SMEM = pl.BlockSpec(memory_space=pltpu.SMEM)
ANY = pl.BlockSpec(memory_space=pl.ANY)
BIG = 60 * 1024 * 1024
NN = (((1,), (0,)), ((), ()))
NT = (((1,), (1,)), ((), ()))


def iota(shape, axis):
    return lax.broadcasted_iota(jnp.int32, shape, axis)


def split2(x):
    hi = x.astype(BF16)
    return hi, (x - hi.astype(F32)).astype(BF16)


def bdot(a, b, dims=NN):
    return lax.dot_general(a, b, dims, preferred_element_type=F32)


def dot3(a, b, dims=NN):
    ah, al = a if isinstance(a, tuple) else split2(a)
    bh, bl = b if isinstance(b, tuple) else split2(b)
    return bdot(ah, bh, dims) + (bdot(al, bh, dims) + bdot(ah, bl, dims))


def pick_exact(one_hot, x):
    hi = x.astype(BF16)
    rest = x - hi.astype(F32)
    mid = rest.astype(BF16)
    low = (rest - mid.astype(F32)).astype(BF16)
    return bdot(one_hot, hi) + (bdot(one_hot, mid) + bdot(one_hot, low))


def node(k):
    return jnp.where(
        k == 0, NODES[0], jnp.where(k == 1, NODES[1], jnp.where(k == 2, NODES[2], NODES[3]))
    ).astype(F32)


def cheb(u):
    return u, 2.0 * u * u - 1.0, (4.0 * u * u - 3.0) * u


def factors(u):
    t1, t2, t3 = cheb(u)
    out = []
    for t in NODES:
        out.append(0.25 + t1 * (0.5 * t) + t2 * (0.5 * (2 * t * t - 1)) + t3 * (0.5 * (4 * t**3 - 3 * t)))
    return out


def cheb_pair(u, t):
    u1, u2, u3 = cheb(u)
    t1, t2, t3 = cheb(t)
    return 0.25 + 0.5 * (u1 * t1 + u2 * t2 + u3 * t3)


def column(row, count):
    spread = jnp.where(iota((count, count), 0) == iota((count, count), 1), row.astype(F32), 0.0)
    return jnp.sum(spread, axis=1, keepdims=True)


def weights_loop(offs, visit):
    fx, fy, fz = (factors(o) for o in offs)
    for i in range(4):
        for j in range(4):
            fxy = fx[i] * fy[j]
            for k in range(4):
                visit(16 * i + 4 * j + k, fxy * fz[k])


def particle_kernel(off_ref, str_ref, cell_ref, count_ref, fill_ref, rec_ref, mul_ref):
    leaf, size = off_ref.shape[1], off_ref.shape[2]
    seg, ex = lax.axis_index("space"), lax.axis_index("exp")
    cell_f = column(cell_ref[...], leaf)
    fill = column(fill_ref[...], leaf)
    cell = cell_f.astype(jnp.int32)
    slot = ex * leaf + iota((leaf, size), 0)
    alive = (slot < count_ref[0]) & (iota((leaf, size), 1).astype(F32) < fill)
    centre = (
        2 * seg + ((cell >> 1) & 1),
        cell >> 2,
        cell & 1,
    )
    offs = [off_ref[a] for a in range(3)]
    charge = []
    for a in range(3):
        pos = (centre[a].astype(F32) + 0.5) + 0.5 * offs[a]
        rec_ref[pl.ds(a, leaf, 6), :] = pos
        q = jnp.where(alive, str_ref[a], 0.0)
        rec_ref[pl.ds(3 + a, leaf, 6), :] = q
        charge.append(q)
    lane = iota((leaf, size), 1)
    acc = [jnp.zeros((leaf, size), F32), jnp.where(lane >= 64, cell_f, 0.0)]

    def visit(a, w):
        for c in range(3):
            total = jnp.sum(charge[c] * w, axis=1, keepdims=True)
            at = a + 64 * (c % 2)
            acc[c // 2] = jnp.where(lane == at, total, acc[c // 2])

    weights_loop(offs, visit)
    mul_ref[0:leaf, :] = acc[0]
    mul_ref[leaf : 2 * leaf, :] = acc[1]


def mesh_at(seg, ex):
    return {"space": seg, "exp": ex}


def remote(src, dst, send, recv, seg, ex):
    return pltpu.make_async_remote_copy(
        src_ref=src, dst_ref=dst, send_sem=send, recv_sem=recv,
        device_id=mesh_at(seg, ex), device_id_type=pl.DeviceIdType.MESH,
    )


def sorted_block(mul_ref, part, guard):
    n_ex, leaf = mul_ref.shape[1], mul_ref.shape[2] // 2
    slots = n_ex * leaf
    par = slots // 8
    m01 = mul_ref[part, :, 0:leaf, :].reshape(slots, 128)
    m2c = mul_ref[part, :, leaf : 2 * leaf, :].reshape(slots, 128)
    cells = jnp.swapaxes(m2c, 0, 1)[64:65, :]
    row = iota((slots, slots), 0)
    wanted = ((row % par) * 8 + row // par).astype(F32)
    one_hot = jnp.where((wanted == cells) & guard, 1.0, 0.0).astype(BF16)
    return pick_exact(one_hot, m01), pick_exact(one_hot, m2c)


def parent_moments(g01, g2):
    par = g01.shape[0] // 8
    total = jnp.zeros((2 * par, 128), F32)
    lane_b = iota((128, 128), 1)
    row_a = iota((128, 128), 0)
    bx, by, bz = (node((lane_b // w) % 4) for w in (16, 4, 1))
    ax, ay, az = (node((row_a // w) % 4) for w in (16, 4, 1))
    sx, sy, sz = ([cheb_pair(bit - 0.5 + 0.5 * a, b) for bit in (0, 1)] for a, b in ((ax, bx), (ay, by), (az, bz)))
    same = (lane_b // 64) == (row_a // 64)
    for h in range(8):
        table = jnp.where(same, sx[(h // 2) % 2] * sy[h // 4] * sz[h % 2], 0.0)
        lhs = jnp.concatenate([g01[h * par : (h + 1) * par], g2[h * par : (h + 1) * par]], axis=0)
        total = total + dot3(lhs, table)
    return total


def store_rows(grid_ref, j, g01, g2):
    par = g01.shape[0] // 8
    for odd in range(2):
        for c in range(3):
            src = g01 if c < 2 else g2
            lo = 64 * (c % 2)
            grid_ref[j * 2 + odd, c, 8 : 8 + par, :] = jnp.concatenate(
                [src[(4 * odd + r) * par : (4 * odd + r + 1) * par, lo : lo + 64] for r in range(4)], axis=1
            )


def m2l_tables(base_ref, near_x_ref):
    lane, row = iota((256, 512), 1), iota((256, 512), 0)
    ux = ((lane // 128) % 2).astype(F32) + 0.5 * node((lane // 16) % 4)
    vx = (row // 128).astype(F32) + 0.5 * node((row // 16) % 4)
    uz = ((lane // 64) % 2).astype(F32) + 0.5 * node(lane % 4)
    vz = ((row // 64) % 2).astype(F32) + 0.5 * node(row % 4)
    base_ref[1] = (uz - vz) * (uz - vz) + SMOOTH
    base_ref[2] = ux - vx
    near_x_ref[1] = ((row // 128) - (lane // 128) % 2).astype(F32)


def m2l_segment(j, par, grid_ref, base_ref, near_x_ref, loc_ref):
    lane1 = iota((1, 512), 1)
    up1 = (lane1 // 256).astype(F32)
    uy = up1 + 0.5 * node((lane1 // 4) % 4)
    vy = 0.5 * node((iota((256, 1), 0) // 4) % 4)
    shift = 2.0 * jnp.asarray(j, jnp.int32).astype(F32) - 2.0
    dx = base_ref[2] - shift
    base_ref[0] = dx * dx + base_ref[1]
    near_x_ref[0] = jnp.where(jnp.abs(near_x_ref[1] + shift) < 1.5, jnp.inf, 0.0)
    for odd in range(2):
        for i in range(3):
            height = 2 * i + odd - 2
            lhs = jnp.concatenate([grid_ref[j * 2 + odd, c, 7 + i : 7 + i + par, :] for c in range(3)], axis=0)
            near_y = jnp.where(jnp.abs(height - up1) < 1.5, jnp.inf, 0.0)
            dy = (uy - height) - vy
            g = lax.rsqrt(dy * dy + base_ref[0] + jnp.minimum(near_x_ref[0], near_y))
            loc_ref[...] += dot3(lhs, g)


def far_sum(seg, ex, pq_ref, far_ref):
    per = pq_ref.shape[0]
    par = pq_ref.shape[1] // 2
    wide = per * 64
    rows = []
    for c in range(3):
        r0, l0 = par * (c // 2), 64 * (c % 2)
        rows.append(jnp.concatenate([pq_ref[q, r0 : r0 + par, l0 : l0 + 64] for q in range(per)], axis=1))
    rows.append(jnp.zeros((128 - 3 * par, wide), F32))
    ph, plo = split2(jnp.swapaxes(jnp.concatenate(rows, axis=0), 0, 1))
    lane, row = iota((64, wide), 1), iota((64, wide), 0)
    step = (seg - ex * per - lane // 64).astype(F32)
    dx = 2.0 * step + node(row // 16) - node((lane // 16) % 4)
    dz = node(row % 4) - node(lane % 4)
    far_ref[0] = dx * dx + (dz * dz + SMOOTH)
    far_ref[1] = node((row // 4) % 4) - node((lane // 4) % 4)
    far_ref[2] = jnp.where(jnp.abs(step) < 1.5, jnp.inf, 0.0)
    p_to = iota((64, 128), 1) % par

    def some(i, acc):
        high, low = [], []
        for u in range(3):
            delta = i * 3 + u - (par - 1)
            dy = far_ref[1] + 2.0 * delta.astype(F32)
            gap = jnp.where(jnp.abs(delta) <= 1, jnp.inf, 0.0)
            gh, gl = split2(lax.rsqrt(dy * dy + far_ref[0] + jnp.minimum(far_ref[2], gap)))
            high.append(gh)
            low.append(gl)
        gh = jnp.concatenate(high, axis=0)
        got = bdot(gh, ph) + (bdot(jnp.concatenate(low, axis=0), ph) + bdot(gh, plo))
        for u in range(3):
            delta = i * 3 + u - (par - 1)
            moved = pltpu.roll(got[64 * u : 64 * u + 64], (delta + 128) % 128, 1)
            source = p_to - delta
            acc = acc + jnp.where((source >= 0) & (source < par), moved, 0.0)
        return acc

    return lax.fori_loop(0, (2 * par - 1) // 3, some, jnp.zeros((64, 128), F32))


def parent_to_child(parent):
    lane, row = iota((64, 512), 1), iota((64, 512), 0)
    table = 1.0
    for bit, w in (((lane // 128) % 2, 16), (lane // 256, 4), ((lane // 64) % 2, 1)):
        table = table * cheb_pair(bit.astype(F32) - 0.5 + 0.5 * node((lane // w) % 4), node((row // w) % 4))
    return dot3(parent, table)


def tree_kernel(
    n_seg, n_x, per, rec_ref, mul_ref, win_ref, loc_ref,
    mwin_ref, pm_ref, pq_ref, part_ref, share_ref, grid_ref, base_ref, near_x_ref, far_ref,
    send, mrecv, precv, swap_send, swap_recv, share_recv, own_sem,
):
    n_ex = 2 * n_x
    seg, ex = lax.axis_index("space"), lax.axis_index("exp")
    x, core = ex // 2, ex % 2
    prev, after = (seg + n_seg - 1) % n_seg, (seg + 1) % n_seg
    ring = [((x + d) % n_x) * 2 + core for d in range(n_x)]
    mates = [((x + d) % n_x) * 2 + 1 - core for d in range(n_x)]
    order = [1, n_x - 1] + list(range(2, n_x - 1))
    mate = mates[0]
    others = [ring[d] for d in order] + [mates[d] for d in [0] + order]
    there = seg // per
    mine = ex == there
    par = mul_ref.shape[0] // 2 * n_ex // 8
    barrier = pltpu.get_barrier_semaphore()
    sent = []

    def hello(to_seg, to_ex):
        pl.semaphore_signal(barrier, 1, device_id=mesh_at(to_seg, to_ex), device_id_type=pl.DeviceIdType.MESH)

    def not_self(i):
        return jnp.logical_not(mine & (seg % per == i))

    for o in others:
        hello(seg, o)
    hello(prev, ex)
    hello(after, ex)
    for i in range(per):

        @pl.when(not_self(i))
        def _():
            hello(ex * per + i, there)

    pl.semaphore_wait(barrier, len(others) + 2 + jnp.where(mine, per - 1, per))

    def push(src, dst, recv, to_seg, to_ex):
        copy = remote(src, dst, send.at[len(sent)], recv, to_seg, to_ex)
        copy.start()
        sent.append(copy)

    def push_m(src, part, who, to_seg, to_ex):
        push(src, mwin_ref.at[part, who], mrecv.at[part, who], to_seg, to_ex)

    def push_p(src, part, who, to_seg, to_ex):
        push(src, win_ref.at[part, who], precv.at[part, who], to_seg, to_ex)

    def got_m(part, who):
        remote(mul_ref, mwin_ref.at[part, who], send.at[0], mrecv.at[part, who], seg, mate).wait_recv()

    def got_p(part, who):
        remote(rec_ref, win_ref.at[part, who], send.at[0], precv.at[part, who], seg, mate).wait_recv()

    for o in others:
        push_m(mul_ref, 1, ex, seg, o)
    push_m(mul_ref, 0, ex, after, ex)
    push_m(mul_ref, 2, ex, prev, ex)
    for d in order:
        push_p(rec_ref, 1, ex, seg, ring[d])
    push_p(rec_ref, 0, ex, after, ex)
    push_p(rec_ref, 2, ex, prev, ex)
    push_p(rec_ref, 1, ex, seg, mate)
    keep = pltpu.make_async_copy(rec_ref, win_ref.at[1, ex], own_sem)
    keep.start()
    mwin_ref[1, ex] = mul_ref[...]
    grid_ref[...] = jnp.zeros(grid_ref.shape, F32)
    m2l_tables(base_ref, near_x_ref)
    for d in order:
        got_m(1, ring[d])
        push_m(mwin_ref.at[1, ring[d]], 0, ring[d], after, ex)
        push_m(mwin_ref.at[1, ring[d]], 2, ring[d], prev, ex)
    for d in range(n_x):
        got_m(1, mates[d])
    g01, g2 = sorted_block(mwin_ref, 1, True)
    pm_ref[...] = parent_moments(g01, g2)
    store_rows(grid_ref, 1, g01, g2)

    def pass_on(d):
        got_p(1, ring[d])
        push_p(win_ref.at[1, ring[d]], 0, ring[d], after, ex)
        push_p(win_ref.at[1, ring[d]], 2, ring[d], prev, ex)
        push_p(win_ref.at[1, ring[d]], 1, ring[d], seg, mate)

    pass_on(order[0])
    pass_on(order[1])

    def swap(i):
        return remote(pm_ref, pq_ref.at[seg % per], swap_send.at[i], swap_recv.at[seg % per], ex * per + i, there)

    for i in range(per):

        @pl.when(not_self(i))
        def _():
            swap(i).start()

    @pl.when(mine)
    def _():
        pq_ref[seg % per] = pm_ref[...]

    for d in order[2:]:
        pass_on(d)
    loc_ref[...] = jnp.zeros(loc_ref.shape, F32)
    m2l_segment(1, par, grid_ref, base_ref, near_x_ref, loc_ref)
    for d in [0] + order:
        for part in (0, 2):
            got_m(part, ring[d])
            push_m(mwin_ref.at[part, ring[d]], part, ring[d], seg, mate)

    def pass_mate(d):
        for part in (0, 2):
            got_p(part, ring[d])
            push_p(win_ref.at[part, ring[d]], part, ring[d], seg, mate)

    pass_mate(0)
    for d in range(n_x):
        for part in (0, 2):
            got_m(part, mates[d])
    for part, guard in ((0, seg > 0), (2, seg < n_seg - 1)):
        g01, g2 = sorted_block(mwin_ref, part, guard)
        store_rows(grid_ref, part, g01, g2)

    def sides(i, carry):
        m2l_segment(2 * i, par, grid_ref, base_ref, near_x_ref, loc_ref)
        return carry

    lax.fori_loop(0, 2, sides, 0)
    pass_mate(order[0])
    pass_mate(order[1])
    for i in range(per):

        @pl.when(not_self(i))
        def _():
            remote(pm_ref, pq_ref.at[i], swap_send.at[i], swap_recv.at[i], ex * per + i, there).wait_recv()
            swap(i).wait_send()

    part_ref[...] = far_sum(seg, ex, pq_ref, far_ref)
    for d in order[2:]:
        pass_mate(d)
    for o in others:
        push(part_ref, share_ref.at[ex], share_recv.at[ex], seg, o)
    share_ref[ex] = part_ref[...]
    for d in range(n_x):
        for part in range(3):
            got_p(part, mates[d])
    for o in others:
        remote(part_ref, share_ref.at[o], send.at[0], share_recv.at[o], seg, o).wait_recv()
    parent = share_ref[0]
    for i in range(1, n_ex):
        parent = parent + share_ref[i]
    loc_ref[...] += parent_to_child(jnp.swapaxes(parent, 0, 1)[: 3 * par, :])
    keep.wait()
    for copy in sent:
        copy.wait_send()


def final_kernel(
    fill_ref, near_ref, many_ref, count_ref, off_ref, cell_ref, win_ref, loc_ref, out_ref, xb_ref,
):
    leaf, size = off_ref.shape[1], off_ref.shape[2]
    seg, ex = lax.axis_index("space"), lax.axis_index("exp")
    slots = win_ref.shape[0] // 18
    par = slots // 8
    cell = column(cell_ref[...], leaf).astype(jnp.int32)
    chosen = jnp.where((cell >> 3) == iota((leaf, par), 1), 1.0, 0.0).astype(BF16)
    child = cell & 7
    lane = iota((leaf, 128), 1)
    expansion = []
    for c in range(3):
        wide = pick_exact(chosen, loc_ref[c * par : (c + 1) * par, :])
        kept = jnp.zeros((leaf, 128), F32)
        for i in range(4):
            kept = kept + jnp.where(lane // 64 + 2 * i == child, wide[:, 128 * i : 128 * i + 128], 0.0)
        expansion.append(kept + pltpu.roll(kept, 64, 1))
    far = [jnp.zeros((leaf, size), F32) for _ in range(3)]

    def visit(a, w):
        for c in range(3):
            far[c] = far[c] + expansion[c][:, a : a + 1] * w

    weights_loop([off_ref[a] for a in range(3)], visit)
    for c in range(3):
        out_ref[c] = far[c]
    start = (seg - 1) * slots
    block = 64
    zeros = jnp.zeros((block, size), F32)

    def target(t, carry):
        fill = fill_ref[t]
        many = many_ref[t]
        own = (slots + ex * leaf + t) * 6
        spare = jnp.zeros((5, size), F32)
        turned = jnp.swapaxes(jnp.concatenate([win_ref[pl.ds(own + a, 1), :] for a in range(3)] + [spare], axis=0), 0, 1)
        for a in range(3):
            xb_ref[a] = jnp.broadcast_to(turned[:, a : a + 1], (size, size))
            xb_ref[3 + a] = jnp.zeros((size, size), F32)

        def rows(n, carry):
            at = pl.multiple_of(n * block, block)

            def step(k3, acc):
                acc = list(acc)
                for u in range(3):
                    k = k3 * 3 + u
                    m = (near_ref[k, t] - start) * 6
                    on = jnp.where(k < many, 1.0, 0.0).astype(F32)
                    dx = xb_ref[0, pl.ds(at, block), :] - win_ref[pl.ds(m + 0, 1), :]
                    dy = xb_ref[1, pl.ds(at, block), :] - win_ref[pl.ds(m + 1, 1), :]
                    dz = xb_ref[2, pl.ds(at, block), :] - win_ref[pl.ds(m + 2, 1), :]
                    g = lax.rsqrt(dx * dx + (dy * dy + (dz * dz + SMOOTH)))
                    for c in range(3):
                        acc[c] = acc[c] + g * (win_ref[pl.ds(m + 3 + c, 1), :] * on)
                return tuple(acc)

            acc = lax.fori_loop(0, (many + 2) // 3, step, (zeros, zeros, zeros))
            for c in range(3):
                xb_ref[3 + c, pl.ds(at, block), :] = acc[c]
            return carry

        lax.fori_loop(0, (fill + block - 1) // block, rows, 0)
        lane = iota((size, size), 1)
        cols = jnp.zeros((size, size), F32)
        for c in range(3):
            cols = jnp.where(lane == c, jnp.sum(xb_ref[3 + c], axis=1, keepdims=True), cols)
        result = jnp.swapaxes(cols, 0, 1)
        live = iota((1, size), 1) < fill
        for c in range(3):
            total = (result[c : c + 1, :] + out_ref[c, pl.ds(t, 1), :]) * SCALE
            out_ref[c, pl.ds(t, 1), :] = jnp.where(live, total, 0.0)
        return carry

    turns = jnp.clip(count_ref[0] - ex * leaf, 0, leaf)
    lax.fori_loop(0, turns, target, 0)

    def blank(t, carry):
        for c in range(3):
            out_ref[c, pl.ds(t, 1), :] = jnp.zeros((1, size), F32)
        return carry

    lax.fori_loop(turns, leaf, blank, 0)


def shape(*dims):
    return jax.ShapeDtypeStruct(dims, F32)


def particle_call(offsets, strength, cell_row, leaf_count, fill_row):
    leaf, size = offsets.shape[1], offsets.shape[2]
    return pl.pallas_call(
        particle_kernel,
        out_shape=(shape(leaf * 6, size), shape(leaf * 2, size)),
        in_specs=[VMEM, VMEM, VMEM, SMEM, VMEM],
        out_specs=(VMEM, VMEM),
    )(offsets, strength, cell_row, leaf_count, fill_row)


def tree_call(n_seg, n_ex, record, moments):
    n_x, per = n_ex // 2, n_seg // n_ex
    par = moments.shape[0] // 2 * n_ex // 8
    dma = pltpu.SemaphoreType.DMA
    return pl.pallas_call(
        lambda *refs: tree_kernel(n_seg, n_x, per, *refs),
        out_shape=(shape(3, n_ex, *record.shape), shape(3 * par, 512)),
        in_specs=[VMEM, VMEM],
        out_specs=(ANY, VMEM),
        scratch_shapes=[
            pltpu.VMEM((3, n_ex, *moments.shape), F32),
            pltpu.VMEM((2 * par, 128), F32),
            pltpu.VMEM((per, 2 * par, 128), F32),
            pltpu.VMEM((64, 128), F32),
            pltpu.VMEM((n_ex, 64, 128), F32),
            pltpu.VMEM((6, 3, par + 16, 256), F32),
            pltpu.VMEM((3, 256, 512), F32),
            pltpu.VMEM((2, 256, 512), F32),
            pltpu.VMEM((3, 64, per * 64), F32),
            dma((14 * n_x + 5,)),
            dma((3, n_ex)),
            dma((3, n_ex)),
            dma((per,)),
            dma((per,)),
            dma((n_ex,)),
            dma,
        ],
        compiler_params=pltpu.CompilerParams(collective_id=0, has_side_effects=True, vmem_limit_bytes=BIG),
    )(record, moments)


def final_call(fill, near, many, count, offsets, cell_row, window, loc):
    leaf, size = offsets.shape[1], offsets.shape[2]
    return pl.pallas_call(
        final_kernel,
        out_shape=shape(3, leaf, size),
        in_specs=[SMEM, SMEM, SMEM, SMEM, VMEM, VMEM, VMEM, VMEM],
        out_specs=VMEM,
        scratch_shapes=[pltpu.VMEM((6, size, size), F32)],
        compiler_params=pltpu.CompilerParams(vmem_limit_bytes=BIG),
    )(fill, near, many, count, offsets, cell_row, window, loc)


def solution(mesh):
    n_seg, n_ex = mesh.shape["space"], mesh.shape["exp"]

    def body(offsets, strength, leaf_cell, leaf_count, leaf_fill, near_list, near_count):
        leaf, size = offsets.shape[1], offsets.shape[2]
        cell_row = leaf_cell.reshape(1, leaf)
        fill_row = leaf_fill.reshape(1, leaf)
        record, moments = particle_call(offsets, strength, cell_row, leaf_count, fill_row)
        window, loc = tree_call(n_seg, n_ex, record, moments)
        window = window.reshape(3 * n_ex * leaf * 6, size)
        return final_call(leaf_fill, near_list, near_count, leaf_count, offsets, cell_row, window, loc)

    in_specs = (
        P(None, ("space", "exp"), None),
        P(None, ("space", "exp"), None),
        P(("space", "exp")),
        P("space"),
        P(("space", "exp")),
        P(None, ("space", "exp")),
        P(("space", "exp")),
    )
    out_specs = P(None, ("space", "exp"), None)
    return jax.shard_map(body, mesh=mesh, in_specs=in_specs, out_specs=out_specs, check_vma=False)
```

```python
import math

import jax
import jax.numpy as jnp
from jax import lax
from jax.experimental import pallas as pl
from jax.experimental.pallas import tpu as pltpu
from jax.sharding import PartitionSpec as P

NODES = [math.cos((2 * k + 1) * math.pi / 8) for k in range(4)]
SMOOTH = 0.01
SCALE = 1.0 / (4.0 * math.pi)
F32 = jnp.float32
BF16 = jnp.bfloat16
VMEM = pl.BlockSpec(memory_space=pltpu.VMEM)
SMEM = pl.BlockSpec(memory_space=pltpu.SMEM)
ANY = pl.BlockSpec(memory_space=pl.ANY)
BIG = 60 * 1024 * 1024
NN = (((1,), (0,)), ((), ()))
NT = (((1,), (1,)), ((), ()))


def iota(shape, axis):
    return lax.broadcasted_iota(jnp.int32, shape, axis)


def split2(x):
    hi = x.astype(BF16)
    return hi, (x - hi.astype(F32)).astype(BF16)


def split3(x):
    hi = x.astype(BF16).astype(F32)
    rest = x - hi
    mid = rest.astype(BF16).astype(F32)
    return hi, mid, rest - mid


def bdot(a, b, dims=NN):
    return lax.dot_general(a, b, dims, preferred_element_type=F32)


def dot3(a, b, dims=NN):
    ah, al = a if isinstance(a, tuple) else split2(a)
    bh, bl = b if isinstance(b, tuple) else split2(b)
    return bdot(ah, bh, dims) + (bdot(al, bh, dims) + bdot(ah, bl, dims))


def pick_exact(one_hot, x):
    hi = x.astype(BF16)
    rest = x - hi.astype(F32)
    mid = rest.astype(BF16)
    low = (rest - mid.astype(F32)).astype(BF16)
    return bdot(one_hot, hi) + (bdot(one_hot, mid) + bdot(one_hot, low))


def node(k):
    return jnp.where(
        k == 0, NODES[0], jnp.where(k == 1, NODES[1], jnp.where(k == 2, NODES[2], NODES[3]))
    ).astype(F32)


def cheb(u):
    return u, 2.0 * u * u - 1.0, (4.0 * u * u - 3.0) * u


def factors(u):
    t1, t2, t3 = cheb(u)
    out = []
    for t in NODES:
        out.append(0.25 + t1 * (0.5 * t) + t2 * (0.5 * (2 * t * t - 1)) + t3 * (0.5 * (4 * t**3 - 3 * t)))
    return out


def cheb_pair(u, t):
    u1, u2, u3 = cheb(u)
    t1, t2, t3 = cheb(t)
    return 0.25 + 0.5 * (u1 * t1 + u2 * t2 + u3 * t3)


def column(row, count):
    spread = jnp.where(iota((count, count), 0) == iota((count, count), 1), row.astype(F32), 0.0)
    return jnp.sum(spread, axis=1, keepdims=True)


def weights_loop(offs, visit):
    fx, fy, fz = (factors(o) for o in offs)
    for i in range(4):
        for j in range(4):
            fxy = fx[i] * fy[j]
            for k in range(4):
                visit(16 * i + 4 * j + k, fxy * fz[k])


def particles(seg, ex, off_ref, str_ref, cell_ref, count_ref, fill_ref, rec_ref, mul_ref):
    leaf, size = off_ref.shape[1], off_ref.shape[2]
    cell_f = column(cell_ref[...], leaf)
    fill = column(fill_ref[...], leaf)
    cell = cell_f.astype(jnp.int32)
    slot = ex * leaf + iota((leaf, size), 0)
    alive = (slot < count_ref[0]) & (iota((leaf, size), 1).astype(F32) < fill)
    centre = (
        2 * seg + ((cell >> 1) & 1),
        cell >> 2,
        cell & 1,
    )
    offs = [off_ref[a] for a in range(3)]
    charge = []
    for a in range(3):
        pos = (centre[a].astype(F32) + 0.5) + 0.5 * offs[a]
        rec_ref[pl.ds(a, leaf, 6), :] = pos
        q = jnp.where(alive, str_ref[a], 0.0)
        rec_ref[pl.ds(3 + a, leaf, 6), :] = q
        charge.append(q)
    lane = iota((leaf, size), 1)
    acc = [jnp.zeros((leaf, size), F32), jnp.where(lane >= 64, cell_f, 0.0)]

    def visit(a, w):
        for c in range(3):
            total = jnp.sum(charge[c] * w, axis=1, keepdims=True)
            at = a + 64 * (c % 2)
            acc[c // 2] = jnp.where(lane == at, total, acc[c // 2])

    weights_loop(offs, visit)
    mul_ref[0:leaf, :] = acc[0]
    mul_ref[leaf : 2 * leaf, :] = acc[1]


def mesh_at(seg, ex):
    return {"space": seg, "exp": ex}


def remote(src, dst, send, recv, seg, ex):
    return pltpu.make_async_remote_copy(
        src_ref=src, dst_ref=dst, send_sem=send, recv_sem=recv,
        device_id=mesh_at(seg, ex), device_id_type=pl.DeviceIdType.MESH,
    )


def sorted_block(mul_ref, part, guard):
    n_ex, leaf = mul_ref.shape[1], mul_ref.shape[2] // 2
    slots = n_ex * leaf
    par = slots // 8
    m01 = mul_ref[part, :, 0:leaf, :].reshape(slots, 128)
    m2c = mul_ref[part, :, leaf : 2 * leaf, :].reshape(slots, 128)
    cells = jnp.swapaxes(m2c, 0, 1)[64:65, :]
    row = iota((slots, slots), 0)
    wanted = ((row % par) * 8 + row // par).astype(F32)
    one_hot = jnp.where((wanted == cells) & guard, 1.0, 0.0).astype(BF16)
    return pick_exact(one_hot, m01), pick_exact(one_hot, m2c)


def parent_moments(g01, g2):
    par = g01.shape[0] // 8
    total = jnp.zeros((2 * par, 128), F32)
    lane_b = iota((128, 128), 1)
    row_a = iota((128, 128), 0)
    bx, by, bz = (node((lane_b // w) % 4) for w in (16, 4, 1))
    ax, ay, az = (node((row_a // w) % 4) for w in (16, 4, 1))
    sx, sy, sz = ([cheb_pair(bit - 0.5 + 0.5 * a, b) for bit in (0, 1)] for a, b in ((ax, bx), (ay, by), (az, bz)))
    same = (lane_b // 64) == (row_a // 64)
    for h in range(8):
        table = jnp.where(same, sx[(h // 2) % 2] * sy[h // 4] * sz[h % 2], 0.0)
        lhs = jnp.concatenate([g01[h * par : (h + 1) * par], g2[h * par : (h + 1) * par]], axis=0)
        total = total + dot3(lhs, table)
    return total


def store_rows(grid_ref, j, g01, g2):
    par = g01.shape[0] // 8
    for odd in range(2):
        for c in range(3):
            src = g01 if c < 2 else g2
            lo = 64 * (c % 2)
            grid_ref[j * 2 + odd, c, 8 : 8 + par, :] = jnp.concatenate(
                [src[(4 * odd + r) * par : (4 * odd + r + 1) * par, lo : lo + 64] for r in range(4)], axis=1
            )


def m2l_tables(base_ref, near_x_ref):
    lane, row = iota((256, 512), 1), iota((256, 512), 0)
    ux = ((lane // 128) % 2).astype(F32) + 0.5 * node((lane // 16) % 4)
    vx = (row // 128).astype(F32) + 0.5 * node((row // 16) % 4)
    uz = ((lane // 64) % 2).astype(F32) + 0.5 * node(lane % 4)
    vz = ((row // 64) % 2).astype(F32) + 0.5 * node(row % 4)
    base_ref[1] = (uz - vz) * (uz - vz) + SMOOTH
    base_ref[2] = ux - vx
    near_x_ref[1] = ((row // 128) - (lane // 128) % 2).astype(F32)


def m2l_segment(j, par, grid_ref, base_ref, near_x_ref, loc_ref):
    lane1 = iota((1, 512), 1)
    up1 = (lane1 // 256).astype(F32)
    uy = up1 + 0.5 * node((lane1 // 4) % 4)
    vy = 0.5 * node((iota((256, 1), 0) // 4) % 4)
    shift = 2.0 * jnp.asarray(j, jnp.int32).astype(F32) - 2.0
    dx = base_ref[2] - shift
    base_ref[0] = dx * dx + base_ref[1]
    near_x_ref[0] = jnp.where(jnp.abs(near_x_ref[1] + shift) < 1.5, jnp.inf, 0.0)
    for odd in range(2):
        for i in range(3):
            height = 2 * i + odd - 2
            lhs = jnp.concatenate([grid_ref[j * 2 + odd, c, 7 + i : 7 + i + par, :] for c in range(3)], axis=0)
            near_y = jnp.where(jnp.abs(height - up1) < 1.5, jnp.inf, 0.0)
            dy = (uy - height) - vy
            g = lax.rsqrt(dy * dy + base_ref[0] + jnp.minimum(near_x_ref[0], near_y))
            loc_ref[...] += dot3(lhs, g)


def far_tables(seg, ex, per, far_ref):
    wide = per * 64
    lane, row = iota((64, wide), 1), iota((64, wide), 0)
    step = (seg - ex * per - lane // 64).astype(F32)
    dx = 2.0 * step + node(row // 16) - node((lane // 16) % 4)
    dz = node(row % 4) - node(lane % 4)
    far_ref[0] = dx * dx + (dz * dz + SMOOTH)
    far_ref[1] = node((row // 4) % 4) - node((lane // 4) % 4)
    far_ref[2] = jnp.where(jnp.abs(step) < 1.5, jnp.inf, 0.0)


def far_sum(pq_ref, far_ref):
    per = pq_ref.shape[0]
    par = pq_ref.shape[1] // 2
    wide = per * 64
    turn = 7 if (2 * par - 1) % 7 == 0 else 1
    rows = []
    for c in range(3):
        r0, l0 = par * (c // 2), 64 * (c % 2)
        rows.append(jnp.concatenate([pq_ref[q, r0 : r0 + par, l0 : l0 + 64] for q in range(per)], axis=1))
    rows.append(jnp.zeros((128 - 3 * par, wide), F32))
    ph, plo = split2(jnp.swapaxes(jnp.concatenate(rows, axis=0), 0, 1))
    p_to = iota((64, 128), 1) % par

    def some(i, acc):
        high, low = [], []
        for u in range(turn):
            delta = i * turn + u - (par - 1)
            dy = far_ref[1] + 2.0 * delta.astype(F32)
            gap = jnp.where(jnp.abs(delta) <= 1, jnp.inf, 0.0)
            gh, gl = split2(lax.rsqrt(dy * dy + far_ref[0] + jnp.minimum(far_ref[2], gap)))
            high.append(gh)
            low.append(gl)
        gh = jnp.concatenate(high, axis=0)
        got = bdot(gh, ph) + (bdot(jnp.concatenate(low, axis=0), ph) + bdot(gh, plo))
        for u in range(turn):
            delta = i * turn + u - (par - 1)
            moved = pltpu.roll(got[64 * u : 64 * u + 64], (delta + 128) % 128, 1)
            source = p_to - delta
            acc = acc + jnp.where((source >= 0) & (source < par), moved, 0.0)
        return acc

    return lax.fori_loop(0, (2 * par - 1) // turn, some, jnp.zeros((64, 128), F32))


def child_table(table_ref):
    lane, row = iota((64, 512), 1), iota((64, 512), 0)
    table = 1.0
    for bit, w in (((lane // 128) % 2, 16), (lane // 256, 4), ((lane // 64) % 2, 1)):
        table = table * cheb_pair(bit.astype(F32) - 0.5 + 0.5 * node((lane // w) % 4), node((row // w) % 4))
    table_ref[...] = table


def tree_kernel(
    n_seg, n_x, per, off_ref, str_ref, cell_ref, count_ref, fill_ref, win_ref, loc_ref,
    rec_ref, mul_ref, table_ref, mwin_ref, pm_ref, pq_ref, part_ref, share_ref, grid_ref, base_ref, near_x_ref, far_ref,
    send, mrecv, precv, swap_send, swap_recv, share_recv, own_sem,
):
    n_ex = 2 * n_x
    seg, ex = lax.axis_index("space"), lax.axis_index("exp")
    x, core = ex // 2, ex % 2
    prev, after = (seg + n_seg - 1) % n_seg, (seg + 1) % n_seg
    ring = [((x + d) % n_x) * 2 + core for d in range(n_x)]
    mates = [((x + d) % n_x) * 2 + 1 - core for d in range(n_x)]
    order = [1, n_x - 1] + list(range(2, n_x - 1))
    mate = mates[0]
    others = [ring[d] for d in order] + [mates[d] for d in [0] + order]
    there = seg // per
    mine = ex == there
    par = mul_ref.shape[0] // 2 * n_ex // 8
    barrier = pltpu.get_barrier_semaphore()
    sent = []

    def hello(to_seg, to_ex):
        pl.semaphore_signal(barrier, 1, device_id=mesh_at(to_seg, to_ex), device_id_type=pl.DeviceIdType.MESH)

    def not_self(i):
        return jnp.logical_not(mine & (seg % per == i))

    for o in others:
        hello(seg, o)
    hello(prev, ex)
    hello(after, ex)
    for i in range(per):

        @pl.when(not_self(i))
        def _():
            hello(ex * per + i, there)

    particles(seg, ex, off_ref, str_ref, cell_ref, count_ref, fill_ref, rec_ref, mul_ref)
    grid_ref[...] = jnp.zeros(grid_ref.shape, F32)
    loc_ref[...] = jnp.zeros(loc_ref.shape, F32)
    m2l_tables(base_ref, near_x_ref)
    far_tables(seg, ex, per, far_ref)
    child_table(table_ref)
    pl.semaphore_wait(barrier, len(others) + 2 + jnp.where(mine, per - 1, per))

    def push(src, dst, recv, to_seg, to_ex):
        copy = remote(src, dst, send.at[len(sent)], recv, to_seg, to_ex)
        copy.start()
        sent.append(copy)

    def push_m(src, part, who, to_seg, to_ex):
        push(src, mwin_ref.at[part, who], mrecv.at[part, who], to_seg, to_ex)

    def push_p(src, part, who, to_seg, to_ex):
        push(src, win_ref.at[part, who], precv.at[part, who], to_seg, to_ex)

    def got_m(part, who):
        remote(mul_ref, mwin_ref.at[part, who], send.at[0], mrecv.at[part, who], seg, mate).wait_recv()

    def got_p(part, who):
        remote(rec_ref, win_ref.at[part, who], send.at[0], precv.at[part, who], seg, mate).wait_recv()

    for o in others:
        push_m(mul_ref, 1, ex, seg, o)
    push_m(mul_ref, 0, ex, after, ex)
    push_m(mul_ref, 2, ex, prev, ex)
    for d in order:
        push_p(rec_ref, 1, ex, seg, ring[d])
    push_p(rec_ref, 0, ex, after, ex)
    push_p(rec_ref, 2, ex, prev, ex)
    push_p(rec_ref, 1, ex, seg, mate)
    keep = pltpu.make_async_copy(rec_ref, win_ref.at[1, ex], own_sem)
    keep.start()
    mwin_ref[1, ex] = mul_ref[...]
    for d in order:
        got_m(1, ring[d])
        push_m(mwin_ref.at[1, ring[d]], 0, ring[d], after, ex)
        push_m(mwin_ref.at[1, ring[d]], 2, ring[d], prev, ex)
    for d in range(n_x):
        got_m(1, mates[d])
    g01, g2 = sorted_block(mwin_ref, 1, True)
    pm_ref[...] = parent_moments(g01, g2)
    store_rows(grid_ref, 1, g01, g2)

    def pass_on(d):
        got_p(1, ring[d])
        push_p(win_ref.at[1, ring[d]], 0, ring[d], after, ex)
        push_p(win_ref.at[1, ring[d]], 2, ring[d], prev, ex)
        push_p(win_ref.at[1, ring[d]], 1, ring[d], seg, mate)

    def swap(i):
        return remote(pm_ref, pq_ref.at[seg % per], swap_send.at[i], swap_recv.at[seg % per], ex * per + i, there)

    for i in range(per):

        @pl.when(not_self(i))
        def _():
            swap(i).start()

    @pl.when(mine)
    def _():
        pq_ref[seg % per] = pm_ref[...]

    for d in order:
        pass_on(d)
    m2l_segment(1, par, grid_ref, base_ref, near_x_ref, loc_ref)
    for d in [0] + order:
        for part in (0, 2):
            got_m(part, ring[d])
            push_m(mwin_ref.at[part, ring[d]], part, ring[d], seg, mate)

    def pass_mate(d):
        for part in (0, 2):
            got_p(part, ring[d])
            push_p(win_ref.at[part, ring[d]], part, ring[d], seg, mate)

    pass_mate(0)
    for d in range(n_x):
        for part in (0, 2):
            got_m(part, mates[d])
    for part, guard in ((0, seg > 0), (2, seg < n_seg - 1)):
        g01, g2 = sorted_block(mwin_ref, part, guard)
        store_rows(grid_ref, part, g01, g2)

    def sides(i, carry):
        m2l_segment(2 * i, par, grid_ref, base_ref, near_x_ref, loc_ref)
        return carry

    lax.fori_loop(0, 2, sides, 0)
    pass_mate(order[0])
    pass_mate(order[1])
    for i in range(per):

        @pl.when(not_self(i))
        def _():
            remote(pm_ref, pq_ref.at[i], swap_send.at[i], swap_recv.at[i], ex * per + i, there).wait_recv()
            swap(i).wait_send()

    part_ref[...] = far_sum(pq_ref, far_ref)
    for d in order[2:]:
        pass_mate(d)
    for o in others:
        push(part_ref, share_ref.at[ex], share_recv.at[ex], seg, o)
    share_ref[ex] = part_ref[...]
    for d in range(n_x):
        for part in range(3):
            got_p(part, mates[d])
    for o in others:
        remote(part_ref, share_ref.at[o], send.at[0], share_recv.at[o], seg, o).wait_recv()
    parent = share_ref[0]
    for i in range(1, n_ex):
        parent = parent + share_ref[i]
    loc_ref[...] += dot3(jnp.swapaxes(parent, 0, 1)[: 3 * par, :], table_ref[...])
    keep.wait()
    for copy in sent:
        copy.wait_send()


def final_kernel(
    fill_ref, near_ref, many_ref, count_ref, spot_ref, off_ref, cell_ref, win_ref, loc_ref, out_ref,
    box_ref, feat_ref, load_ref, side_ref, sum_ref, sem,
):
    leaf, size = off_ref.shape[1], off_ref.shape[2]
    seg, ex = lax.axis_index("space"), lax.axis_index("exp")
    slots = win_ref.shape[0] // 18
    fetch = pltpu.make_async_copy(win_ref, box_ref.at[0 : slots * 18], sem)
    fetch.start()
    box_ref[slots * 18 :, :] = jnp.zeros((8, size), F32)
    par = slots // 8
    cell = column(cell_ref[...], leaf).astype(jnp.int32)
    chosen = jnp.where((cell >> 3) == iota((leaf, par), 1), 1.0, 0.0).astype(BF16)
    child = cell & 7
    lane = iota((leaf, 128), 1)
    expansion = []
    for c in range(3):
        wide = pick_exact(chosen, loc_ref[c * par : (c + 1) * par, :])
        kept = jnp.zeros((leaf, 128), F32)
        for i in range(4):
            kept = kept + jnp.where(lane // 64 + 2 * i == child, wide[:, 128 * i : 128 * i + 128], 0.0)
        expansion.append(kept + pltpu.roll(kept, 64, 1))
    far = [jnp.zeros((leaf, size), F32) for _ in range(3)]

    def visit(a, w):
        for c in range(3):
            far[c] = far[c] + expansion[c][:, a : a + 1] * w

    weights_loop([off_ref[a] for a in range(3)], visit)
    for c in range(3):
        out_ref[c] = far[c]
    start = (seg - 1) * slots
    row8 = iota((8, size), 0)
    first, second = row8 < 3, (row8 >= 3) & (row8 < 6)
    none = jnp.zeros((8, size), F32)
    count = near_ref.shape[0]
    block = 64
    lane = iota((size, size), 1)
    sum_ref[...] = jnp.zeros(sum_ref.shape, F32)
    fetch.wait()

    def target(t, carry):
        fill = fill_ref[t]
        many = many_ref[t]
        c = spot_ref[t]
        middle = (2 * seg + ((c >> 1) & 1), c >> 2, c & 1)
        mx, my, mz = (jnp.where(row8 == a, m.astype(F32) + 0.5, 0.0) for a, m in enumerate(middle))
        middle = mx + my + mz

        def local(rows):
            near = jnp.where(first, rows - middle, 0.0)
            return near + pltpu.roll(near, 3, 0)

        here = local(box_ref[pl.ds((slots + ex * leaf + t) * 6, 8), :])
        xh, xm, xl = split3(-2.0 * here)
        length = 0.5 * jnp.sum(here * here, axis=0, keepdims=True) + SMOOTH
        nh, nm, nl = split3(length)
        norm = jnp.where(row8 == 3, nh, jnp.where(row8 == 4, nm, nl))
        keep = jnp.where(row8 < 6, 1.0, 0.0)
        cross = jnp.where(first, xh, jnp.where(second, xm, 0.0))
        last = jnp.where(first, xh, jnp.where(second, xl, 0.0))
        tail = jnp.where(first, 1.0, jnp.where(second, norm, 0.0))
        side = jnp.concatenate([cross, cross, last, keep, tail] + [none] * 11, axis=0)
        side_ref[...] = jnp.swapaxes(side, 0, 1).astype(BF16)
        for k in range(count):
            rows = box_ref[pl.ds((near_ref[k, t] - start) * 6, 8), :]
            y = local(rows)
            yh, ym, yl = split3(y)
            sh, sm, sl = split3(y * y)
            feat = [yh, ym, jnp.where(first, yl, yh), jnp.where(first, sh, sm), jnp.where(first, sl, 1.0), none]
            feat_ref[:, size * k : size * k + size] = jnp.concatenate(feat, axis=0).astype(BF16)
            load_ref[k] = rows * jnp.where(k < many, 1.0, 0.0).astype(F32)

        def rows(n, carry):
            at = pl.multiple_of(n * block, block)
            side = side_ref[pl.ds(at, block), 0:48]
            acc = [jnp.zeros((block, size), F32) for _ in range(3)]
            for k in range(0, count, 2):
                g = lax.rsqrt(bdot(side, feat_ref[:, size * k : size * k + 2 * size]))
                for u in range(2):
                    for c in range(3):
                        acc[c] = acc[c] + g[:, size * u : size * u + size] * load_ref[k + u, 3 + c : 4 + c, :]
            for c in range(3):
                sum_ref[c, pl.ds(at, block), :] = acc[c]
            return carry

        lax.fori_loop(0, (fill + block - 1) // block, rows, 0)
        cols = jnp.zeros((size, size), F32)
        for c in range(3):
            cols = jnp.where(lane == c, jnp.sum(sum_ref[c], axis=1, keepdims=True), cols)
        result = jnp.swapaxes(cols, 0, 1)
        live = iota((1, size), 1) < fill
        for c in range(3):
            total = (result[c : c + 1, :] + out_ref[c, pl.ds(t, 1), :]) * SCALE
            out_ref[c, pl.ds(t, 1), :] = jnp.where(live, total, 0.0)
        return carry

    turns = jnp.clip(count_ref[0] - ex * leaf, 0, leaf)
    lax.fori_loop(0, turns, target, 0)

    def blank(t, carry):
        for c in range(3):
            out_ref[c, pl.ds(t, 1), :] = jnp.zeros((1, size), F32)
        return carry

    lax.fori_loop(turns, leaf, blank, 0)


def shape(*dims):
    return jax.ShapeDtypeStruct(dims, F32)


def tree_call(n_seg, n_ex, offsets, strength, cell_row, count, fill_row):
    n_x, per = n_ex // 2, n_seg // n_ex
    leaf, size = offsets.shape[1], offsets.shape[2]
    par = leaf * n_ex // 8
    dma = pltpu.SemaphoreType.DMA
    return pl.pallas_call(
        lambda *refs: tree_kernel(n_seg, n_x, per, *refs),
        out_shape=(shape(3, n_ex, leaf * 6, size), shape(3 * par, 512)),
        in_specs=[VMEM, VMEM, VMEM, SMEM, VMEM],
        out_specs=(ANY, VMEM),
        scratch_shapes=[
            pltpu.VMEM((leaf * 6, size), F32),
            pltpu.VMEM((leaf * 2, size), F32),
            pltpu.VMEM((64, 512), F32),
            pltpu.VMEM((3, n_ex, leaf * 2, size), F32),
            pltpu.VMEM((2 * par, 128), F32),
            pltpu.VMEM((per, 2 * par, 128), F32),
            pltpu.VMEM((64, 128), F32),
            pltpu.VMEM((n_ex, 64, 128), F32),
            pltpu.VMEM((6, 3, par + 16, 256), F32),
            pltpu.VMEM((3, 256, 512), F32),
            pltpu.VMEM((2, 256, 512), F32),
            pltpu.VMEM((3, 64, per * 64), F32),
            dma((14 * n_x + 5,)),
            dma((3, n_ex)),
            dma((3, n_ex)),
            dma((per,)),
            dma((per,)),
            dma((n_ex,)),
            dma,
        ],
        compiler_params=pltpu.CompilerParams(collective_id=0, has_side_effects=True, vmem_limit_bytes=BIG),
    )(offsets, strength, cell_row, count, fill_row)


def final_call(fill, near, many, count, spot, offsets, cell_row, window, loc):
    leaf, size = offsets.shape[1], offsets.shape[2]
    return pl.pallas_call(
        final_kernel,
        out_shape=shape(3, leaf, size),
        in_specs=[SMEM, SMEM, SMEM, SMEM, SMEM, VMEM, VMEM, ANY, VMEM],
        out_specs=VMEM,
        scratch_shapes=[
            pltpu.VMEM((window.shape[0] + 8, size), F32),
            pltpu.VMEM((48, near.shape[0] * size), BF16),
            pltpu.VMEM((near.shape[0], 8, size), F32),
            pltpu.VMEM((size, size), BF16),
            pltpu.VMEM((3, size, size), F32),
            pltpu.SemaphoreType.DMA,
        ],
        compiler_params=pltpu.CompilerParams(vmem_limit_bytes=BIG),
    )(fill, near, many, count, spot, offsets, cell_row, window, loc)


def solution(mesh):
    n_seg, n_ex = mesh.shape["space"], mesh.shape["exp"]

    def body(offsets, strength, leaf_cell, leaf_count, leaf_fill, near_list, near_count):
        leaf, size = offsets.shape[1], offsets.shape[2]
        cell_row = leaf_cell.reshape(1, leaf)
        fill_row = leaf_fill.reshape(1, leaf)
        window, loc = tree_call(n_seg, n_ex, offsets, strength, cell_row, leaf_count, fill_row)
        window = window.reshape(3 * n_ex * leaf * 6, size)
        return final_call(leaf_fill, near_list, near_count, leaf_count, leaf_cell, offsets, cell_row, window, loc)

    in_specs = (
        P(None, ("space", "exp"), None),
        P(None, ("space", "exp"), None),
        P(("space", "exp")),
        P("space"),
        P(("space", "exp")),
        P(None, ("space", "exp")),
        P(("space", "exp")),
    )
    out_specs = P(None, ("space", "exp"), None)
    return jax.shard_map(body, mesh=mesh, in_specs=in_specs, out_specs=out_specs, check_vma=False)
```

```python
import math

import jax
import jax.numpy as jnp
from jax import lax
from jax.experimental import pallas as pl
from jax.experimental.pallas import tpu as pltpu
from jax.sharding import PartitionSpec as P

NODES = [math.cos((2 * k + 1) * math.pi / 8) for k in range(4)]
SMOOTH = 0.01
SCALE = 1.0 / (4.0 * math.pi)
F32 = jnp.float32
BF16 = jnp.bfloat16
VMEM = pl.BlockSpec(memory_space=pltpu.VMEM)
SMEM = pl.BlockSpec(memory_space=pltpu.SMEM)
ANY = pl.BlockSpec(memory_space=pl.ANY)
BIG = 60 * 1024 * 1024
NN = (((1,), (0,)), ((), ()))
NT = (((1,), (1,)), ((), ()))


def iota(shape, axis):
    return lax.broadcasted_iota(jnp.int32, shape, axis)


def split2(x):
    hi = x.astype(BF16)
    return hi, (x - hi.astype(F32)).astype(BF16)


def split3(x):
    hi = x.astype(BF16).astype(F32)
    rest = x - hi
    mid = rest.astype(BF16).astype(F32)
    return hi, mid, rest - mid


def bdot(a, b, dims=NN):
    return lax.dot_general(a, b, dims, preferred_element_type=F32)


def dot3(a, b, dims=NN):
    ah, al = a if isinstance(a, tuple) else split2(a)
    bh, bl = b if isinstance(b, tuple) else split2(b)
    return bdot(ah, bh, dims) + (bdot(al, bh, dims) + bdot(ah, bl, dims))


def pick_exact(one_hot, x):
    hi = x.astype(BF16)
    rest = x - hi.astype(F32)
    mid = rest.astype(BF16)
    low = (rest - mid.astype(F32)).astype(BF16)
    return bdot(one_hot, hi) + (bdot(one_hot, mid) + bdot(one_hot, low))


def node(k):
    return jnp.where(
        k == 0, NODES[0], jnp.where(k == 1, NODES[1], jnp.where(k == 2, NODES[2], NODES[3]))
    ).astype(F32)


def cheb(u):
    return u, 2.0 * u * u - 1.0, (4.0 * u * u - 3.0) * u


def factors(u):
    t1, t2, t3 = cheb(u)
    out = []
    for t in NODES:
        out.append(0.25 + t1 * (0.5 * t) + t2 * (0.5 * (2 * t * t - 1)) + t3 * (0.5 * (4 * t**3 - 3 * t)))
    return out


def cheb_pair(u, t):
    u1, u2, u3 = cheb(u)
    t1, t2, t3 = cheb(t)
    return 0.25 + 0.5 * (u1 * t1 + u2 * t2 + u3 * t3)


def column(row, count):
    spread = jnp.where(iota((count, count), 0) == iota((count, count), 1), row.astype(F32), 0.0)
    return jnp.sum(spread, axis=1, keepdims=True)


def weights_loop(offs, visit):
    fx, fy, fz = (factors(o) for o in offs)
    for i in range(4):
        for j in range(4):
            fxy = fx[i] * fy[j]
            for k in range(4):
                visit(16 * i + 4 * j + k, fxy * fz[k])


def particles(seg, ex, off_ref, str_ref, cell_ref, count_ref, fill_ref, rec_ref, mul_ref):
    leaf, size = off_ref.shape[1], off_ref.shape[2]
    cell_f = column(cell_ref[...], leaf)
    fill = column(fill_ref[...], leaf)
    cell = cell_f.astype(jnp.int32)
    slot = ex * leaf + iota((leaf, size), 0)
    alive = (slot < count_ref[0]) & (iota((leaf, size), 1).astype(F32) < fill)
    centre = (
        2 * seg + ((cell >> 1) & 1),
        cell >> 2,
        cell & 1,
    )
    offs = [off_ref[a] for a in range(3)]
    charge = []
    for a in range(3):
        pos = (centre[a].astype(F32) + 0.5) + 0.5 * offs[a]
        rec_ref[pl.ds(a, leaf, 6), :] = pos
        q = jnp.where(alive, str_ref[a], 0.0)
        rec_ref[pl.ds(3 + a, leaf, 6), :] = q
        charge.append(q)
    lane = iota((leaf, size), 1)
    acc = [jnp.zeros((leaf, size), F32), jnp.where(lane >= 64, cell_f, 0.0)]

    def visit(a, w):
        for c in range(3):
            total = jnp.sum(charge[c] * w, axis=1, keepdims=True)
            at = a + 64 * (c % 2)
            acc[c // 2] = jnp.where(lane == at, total, acc[c // 2])

    weights_loop(offs, visit)
    mul_ref[0:leaf, :] = acc[0]
    mul_ref[leaf : 2 * leaf, :] = acc[1]


def mesh_at(seg, ex):
    return {"space": seg, "exp": ex}


def remote(src, dst, send, recv, seg, ex):
    return pltpu.make_async_remote_copy(
        src_ref=src, dst_ref=dst, send_sem=send, recv_sem=recv,
        device_id=mesh_at(seg, ex), device_id_type=pl.DeviceIdType.MESH,
    )


def sorted_block(mul_ref, part, guard):
    n_ex, leaf = mul_ref.shape[1], mul_ref.shape[2] // 2
    slots = n_ex * leaf
    par = slots // 8
    m01 = mul_ref[part, :, 0:leaf, :].reshape(slots, 128)
    m2c = mul_ref[part, :, leaf : 2 * leaf, :].reshape(slots, 128)
    cells = jnp.swapaxes(m2c, 0, 1)[64:65, :]
    row = iota((slots, slots), 0)
    wanted = ((row % par) * 8 + row // par).astype(F32)
    one_hot = jnp.where((wanted == cells) & guard, 1.0, 0.0).astype(BF16)
    return pick_exact(one_hot, m01), pick_exact(one_hot, m2c)


def parent_moments(g01, g2):
    par = g01.shape[0] // 8
    total = jnp.zeros((2 * par, 128), F32)
    lane_b = iota((128, 128), 1)
    row_a = iota((128, 128), 0)
    bx, by, bz = (node((lane_b // w) % 4) for w in (16, 4, 1))
    ax, ay, az = (node((row_a // w) % 4) for w in (16, 4, 1))
    sx, sy, sz = ([cheb_pair(bit - 0.5 + 0.5 * a, b) for bit in (0, 1)] for a, b in ((ax, bx), (ay, by), (az, bz)))
    same = (lane_b // 64) == (row_a // 64)
    for h in range(8):
        table = jnp.where(same, sx[(h // 2) % 2] * sy[h // 4] * sz[h % 2], 0.0)
        lhs = jnp.concatenate([g01[h * par : (h + 1) * par], g2[h * par : (h + 1) * par]], axis=0)
        total = total + dot3(lhs, table)
    return total


def store_rows(grid_ref, j, g01, g2):
    par = g01.shape[0] // 8
    for odd in range(2):
        for c in range(3):
            src = g01 if c < 2 else g2
            lo = 64 * (c % 2)
            grid_ref[j * 2 + odd, c, 8 : 8 + par, :] = jnp.concatenate(
                [src[(4 * odd + r) * par : (4 * odd + r + 1) * par, lo : lo + 64] for r in range(4)], axis=1
            )


def m2l_tables(base_ref, near_x_ref):
    lane, row = iota((256, 512), 1), iota((256, 512), 0)
    ux = ((lane // 128) % 2).astype(F32) + 0.5 * node((lane // 16) % 4)
    vx = (row // 128).astype(F32) + 0.5 * node((row // 16) % 4)
    uz = ((lane // 64) % 2).astype(F32) + 0.5 * node(lane % 4)
    vz = ((row // 64) % 2).astype(F32) + 0.5 * node(row % 4)
    base_ref[1] = (uz - vz) * (uz - vz) + SMOOTH
    base_ref[2] = ux - vx
    near_x_ref[1] = ((row // 128) - (lane // 128) % 2).astype(F32)


def m2l_segment(j, par, grid_ref, base_ref, near_x_ref, loc_ref):
    lane1 = iota((1, 512), 1)
    up1 = (lane1 // 256).astype(F32)
    uy = up1 + 0.5 * node((lane1 // 4) % 4)
    vy = 0.5 * node((iota((256, 1), 0) // 4) % 4)
    shift = 2.0 * jnp.asarray(j, jnp.int32).astype(F32) - 2.0
    dx = base_ref[2] - shift
    base_ref[0] = dx * dx + base_ref[1]
    near_x_ref[0] = jnp.where(jnp.abs(near_x_ref[1] + shift) < 1.5, jnp.inf, 0.0)
    for odd in range(2):
        for i in range(3):
            height = 2 * i + odd - 2
            lhs = jnp.concatenate([grid_ref[j * 2 + odd, c, 7 + i : 7 + i + par, :] for c in range(3)], axis=0)
            near_y = jnp.where(jnp.abs(height - up1) < 1.5, jnp.inf, 0.0)
            dy = (uy - height) - vy
            g = lax.rsqrt(dy * dy + base_ref[0] + jnp.minimum(near_x_ref[0], near_y))
            loc_ref[...] += dot3(lhs, g)


def far_tables(seg, ex, per, far_ref):
    wide = per * 64
    lane, row = iota((64, wide), 1), iota((64, wide), 0)
    step = (seg - ex * per - lane // 64).astype(F32)
    dx = 2.0 * step + node(row // 16) - node((lane // 16) % 4)
    dz = node(row % 4) - node(lane % 4)
    far_ref[0] = dx * dx + (dz * dz + SMOOTH)
    far_ref[1] = node((row // 4) % 4) - node((lane // 4) % 4)
    far_ref[2] = jnp.where(jnp.abs(step) < 1.5, jnp.inf, 0.0)


def far_sum(pq_ref, far_ref):
    per = pq_ref.shape[0]
    par = pq_ref.shape[1] // 2
    wide = per * 64
    turn = 7 if (2 * par - 1) % 7 == 0 else 1
    rows = []
    for c in range(3):
        r0, l0 = par * (c // 2), 64 * (c % 2)
        rows.append(jnp.concatenate([pq_ref[q, r0 : r0 + par, l0 : l0 + 64] for q in range(per)], axis=1))
    rows.append(jnp.zeros((128 - 3 * par, wide), F32))
    ph, plo = split2(jnp.swapaxes(jnp.concatenate(rows, axis=0), 0, 1))
    p_to = iota((64, 128), 1) % par

    def some(i, acc):
        high, low = [], []
        for u in range(turn):
            delta = i * turn + u - (par - 1)
            dy = far_ref[1] + 2.0 * delta.astype(F32)
            gap = jnp.where(jnp.abs(delta) <= 1, jnp.inf, 0.0)
            gh, gl = split2(lax.rsqrt(dy * dy + far_ref[0] + jnp.minimum(far_ref[2], gap)))
            high.append(gh)
            low.append(gl)
        gh = jnp.concatenate(high, axis=0)
        got = bdot(gh, ph) + (bdot(jnp.concatenate(low, axis=0), ph) + bdot(gh, plo))
        for u in range(turn):
            delta = i * turn + u - (par - 1)
            moved = pltpu.roll(got[64 * u : 64 * u + 64], (delta + 128) % 128, 1)
            source = p_to - delta
            acc = acc + jnp.where((source >= 0) & (source < par), moved, 0.0)
        return acc

    return lax.fori_loop(0, (2 * par - 1) // turn, some, jnp.zeros((64, 128), F32))


def child_table(table_ref):
    lane, row = iota((64, 512), 1), iota((64, 512), 0)
    table = 1.0
    for bit, w in (((lane // 128) % 2, 16), (lane // 256, 4), ((lane // 64) % 2, 1)):
        table = table * cheb_pair(bit.astype(F32) - 0.5 + 0.5 * node((lane // w) % 4), node((row // w) % 4))
    table_ref[...] = table


def tree_kernel(
    n_seg, n_x, per, off_ref, str_ref, cell_ref, count_ref, fill_ref, win_ref, loc_ref,
    rec_ref, mul_ref, table_ref, mwin_ref, pm_ref, pq_ref, part_ref, share_ref, grid_ref, base_ref, near_x_ref, far_ref,
    send, mrecv, precv, swap_send, swap_recv, share_recv, own_sem,
):
    n_ex = 2 * n_x
    seg, ex = lax.axis_index("space"), lax.axis_index("exp")
    x, core = ex // 2, ex % 2
    prev, after = (seg + n_seg - 1) % n_seg, (seg + 1) % n_seg
    ring = [((x + d) % n_x) * 2 + core for d in range(n_x)]
    mates = [((x + d) % n_x) * 2 + 1 - core for d in range(n_x)]
    order = [1, n_x - 1] + list(range(2, n_x - 1))
    mate = mates[0]
    others = [ring[d] for d in order] + [mates[d] for d in [0] + order]
    there = seg // per
    mine = ex == there
    par = mul_ref.shape[0] // 2 * n_ex // 8
    barrier = pltpu.get_barrier_semaphore()
    sent = []

    def hello(to_seg, to_ex):
        pl.semaphore_signal(barrier, 1, device_id=mesh_at(to_seg, to_ex), device_id_type=pl.DeviceIdType.MESH)

    def not_self(i):
        return jnp.logical_not(mine & (seg % per == i))

    for o in others:
        hello(seg, o)
    hello(prev, ex)
    hello(after, ex)
    for i in range(per):

        @pl.when(not_self(i))
        def _():
            hello(ex * per + i, there)

    particles(seg, ex, off_ref, str_ref, cell_ref, count_ref, fill_ref, rec_ref, mul_ref)
    grid_ref[...] = jnp.zeros(grid_ref.shape, F32)
    loc_ref[...] = jnp.zeros(loc_ref.shape, F32)
    m2l_tables(base_ref, near_x_ref)
    far_tables(seg, ex, per, far_ref)
    child_table(table_ref)
    pl.semaphore_wait(barrier, len(others) + 2 + jnp.where(mine, per - 1, per))

    def push(src, dst, recv, to_seg, to_ex):
        copy = remote(src, dst, send.at[len(sent)], recv, to_seg, to_ex)
        copy.start()
        sent.append(copy)

    def push_m(src, part, who, to_seg, to_ex):
        push(src, mwin_ref.at[part, who], mrecv.at[part, who], to_seg, to_ex)

    def push_p(src, part, who, to_seg, to_ex):
        push(src, win_ref.at[part, who], precv.at[part, who], to_seg, to_ex)

    def got_m(part, who):
        remote(mul_ref, mwin_ref.at[part, who], send.at[0], mrecv.at[part, who], seg, mate).wait_recv()

    def got_p(part, who):
        remote(rec_ref, win_ref.at[part, who], send.at[0], precv.at[part, who], seg, mate).wait_recv()

    for o in others:
        push_m(mul_ref, 1, ex, seg, o)
    push_m(mul_ref, 0, ex, after, ex)
    push_m(mul_ref, 2, ex, prev, ex)
    for d in order:
        push_p(rec_ref, 1, ex, seg, ring[d])
    push_p(rec_ref, 0, ex, after, ex)
    push_p(rec_ref, 2, ex, prev, ex)
    push_p(rec_ref, 1, ex, seg, mate)
    keep = pltpu.make_async_copy(rec_ref, win_ref.at[1, ex], own_sem)
    keep.start()
    mwin_ref[1, ex] = mul_ref[...]
    for d in order:
        got_m(1, ring[d])
        push_m(mwin_ref.at[1, ring[d]], 0, ring[d], after, ex)
        push_m(mwin_ref.at[1, ring[d]], 2, ring[d], prev, ex)
    for d in range(n_x):
        got_m(1, mates[d])
    g01, g2 = sorted_block(mwin_ref, 1, True)
    pm_ref[...] = parent_moments(g01, g2)
    store_rows(grid_ref, 1, g01, g2)

    def pass_on(d):
        got_p(1, ring[d])
        push_p(win_ref.at[1, ring[d]], 0, ring[d], after, ex)
        push_p(win_ref.at[1, ring[d]], 2, ring[d], prev, ex)
        push_p(win_ref.at[1, ring[d]], 1, ring[d], seg, mate)

    def swap(i):
        return remote(pm_ref, pq_ref.at[seg % per], swap_send.at[i], swap_recv.at[seg % per], ex * per + i, there)

    for i in range(per):

        @pl.when(not_self(i))
        def _():
            swap(i).start()

    @pl.when(mine)
    def _():
        pq_ref[seg % per] = pm_ref[...]

    for d in order:
        pass_on(d)
    m2l_segment(1, par, grid_ref, base_ref, near_x_ref, loc_ref)
    for d in [0] + order:
        for part in (0, 2):
            got_m(part, ring[d])
            push_m(mwin_ref.at[part, ring[d]], part, ring[d], seg, mate)

    def pass_mate(d):
        for part in (0, 2):
            got_p(part, ring[d])
            push_p(win_ref.at[part, ring[d]], part, ring[d], seg, mate)

    pass_mate(0)
    for d in range(n_x):
        for part in (0, 2):
            got_m(part, mates[d])
    for part, guard in ((0, seg > 0), (2, seg < n_seg - 1)):
        g01, g2 = sorted_block(mwin_ref, part, guard)
        store_rows(grid_ref, part, g01, g2)

    def sides(i, carry):
        m2l_segment(2 * i, par, grid_ref, base_ref, near_x_ref, loc_ref)
        return carry

    lax.fori_loop(0, 2, sides, 0)
    pass_mate(order[0])
    pass_mate(order[1])
    for i in range(per):

        @pl.when(not_self(i))
        def _():
            remote(pm_ref, pq_ref.at[i], swap_send.at[i], swap_recv.at[i], ex * per + i, there).wait_recv()
            swap(i).wait_send()

    part_ref[...] = far_sum(pq_ref, far_ref)
    for d in order[2:]:
        pass_mate(d)
    for o in others:
        push(part_ref, share_ref.at[ex], share_recv.at[ex], seg, o)
    share_ref[ex] = part_ref[...]
    for d in range(n_x):
        for part in range(3):
            got_p(part, mates[d])
    for o in others:
        remote(part_ref, share_ref.at[o], send.at[0], share_recv.at[o], seg, o).wait_recv()
    parent = share_ref[0]
    for i in range(1, n_ex):
        parent = parent + share_ref[i]
    loc_ref[...] += dot3(jnp.swapaxes(parent, 0, 1)[: 3 * par, :], table_ref[...])
    keep.wait()
    for copy in sent:
        copy.wait_send()


def near_field(seg, ex, leaf, near_ref, many_ref, spot_ref, box_ref, bufs, cols_ref, near_out_ref):
    count, size = near_ref.shape[0], 128
    slots = (box_ref.shape[0] - 8) // 18
    start = (seg - 1) * slots
    row8 = iota((8, size), 0)
    first, second = row8 < 3, (row8 >= 3) & (row8 < 6)
    none = jnp.zeros((8, size), F32)
    keep = jnp.where(row8 < 6, 1.0, 0.0)
    block = 32

    def frame(t):
        c = spot_ref[t]
        spot = (2 * seg + ((c >> 1) & 1), c >> 2, c & 1)
        mx, my, mz = (jnp.where(row8 == a, m.astype(F32) + 0.5, 0.0) for a, m in enumerate(spot))
        return mx + my + mz

    def local(rows, middle):
        near = jnp.where(first, rows - middle, 0.0)
        return near + pltpu.roll(near, 3, 0)

    def target_side(t, middle):
        here = local(box_ref[pl.ds((slots + ex * leaf + t) * 6, 8), :], middle)
        xh, xm, xl = split3(-2.0 * here)
        length = 0.5 * jnp.sum(here * here, axis=0, keepdims=True) + SMOOTH
        nh, nm, nl = split3(length)
        norm = jnp.where(row8 == 3, nh, jnp.where(row8 == 4, nm, nl))
        cross = jnp.where(first, xh, jnp.where(second, xm, 0.0))
        last = jnp.where(first, xh, jnp.where(second, xl, 0.0))
        tail = jnp.where(first, 1.0, jnp.where(second, norm, 0.0))
        side = jnp.concatenate([cross, cross, last, keep, tail] + [none] * 11, axis=0)
        return jnp.swapaxes(side, 0, 1).astype(BF16)[:, 0:48]

    def pair(t, k0, middle, side, many, buf):
        r2_ref, load_ref = buf
        feats = []
        for k in (k0, k0 + 1):
            rows = box_ref[pl.ds((near_ref[k, t] - start) * 6, 8), :]
            y = local(rows, middle)
            yh, ym, yl = split3(y)
            sh, sm, sl = split3(y * y)
            feat = [yh, ym, jnp.where(first, yl, yh), jnp.where(first, sh, sm), jnp.where(first, sl, 1.0), none]
            feats.append(jnp.concatenate(feat, axis=0).astype(BF16))
            load_ref[k] = rows * jnp.where(k < many, 1.0, 0.0).astype(F32)
        r2_ref[:, size * k0 : size * k0 + 2 * size] = bdot(side, jnp.concatenate(feats, axis=1))

    def gather_rows(n, buf):
        r2_ref, load_ref = buf
        at = block * n
        acc = [jnp.zeros((block, size), F32) for _ in range(3)]
        for k in range(count):
            g = lax.rsqrt(r2_ref[at : at + block, size * k : size * k + size])
            for c in range(3):
                acc[c] = acc[c] + g * load_ref[k, 3 + c : 4 + c, :]
        lane = iota((block, size), 1)
        s0, s1, s2 = (jnp.sum(x, axis=1, keepdims=True) for x in acc)
        cols_ref[at : at + block, :] = jnp.where(lane == 0, s0, jnp.where(lane == 1, s1, s2))

    def store(t):
        result = jnp.swapaxes(cols_ref[...], 0, 1)
        for c in range(3):
            near_out_ref[c, pl.ds(t, 1), :] = result[c : c + 1, :]

    def work(t_next, next_buf, t_now, now_buf):
        jobs = list(range(size // block)) if now_buf is not None else []
        steps = count // 2
        if next_buf is not None:
            middle = frame(t_next)
            side = target_side(t_next, middle)
            many = many_ref[t_next]
        for p in range(steps):
            if next_buf is not None:
                pair(t_next, 2 * p, middle, side, many, next_buf)
            while jobs and (size // block - len(jobs)) * steps < (p + 1) * (size // block):
                gather_rows(jobs.pop(0), now_buf)
        if now_buf is not None:
            store(t_now)

    def run(turns):
        work(0, bufs[0], None, None)

        def two(i, carry):
            t = 2 * i
            work(t + 1, bufs[1], t, bufs[0])
            work(jnp.minimum(t + 2, leaf - 1), bufs[0], t + 1, bufs[1])
            return carry

        lax.fori_loop(0, turns, two, 0)

    return run


def leaf_far(cell_ref, off_ref, loc_ref):
    leaf, size = off_ref.shape[1], off_ref.shape[2]
    par = loc_ref.shape[0] // 3
    cell = column(cell_ref[...], leaf).astype(jnp.int32)
    chosen = jnp.where((cell >> 3) == iota((leaf, par), 1), 1.0, 0.0).astype(BF16)
    child = cell & 7
    lane = iota((leaf, 128), 1)
    expansion = []
    for c in range(3):
        wide = pick_exact(chosen, loc_ref[c * par : (c + 1) * par, :])
        kept = jnp.zeros((leaf, 128), F32)
        for i in range(4):
            kept = kept + jnp.where(lane // 64 + 2 * i == child, wide[:, 128 * i : 128 * i + 128], 0.0)
        expansion.append(kept + pltpu.roll(kept, 64, 1))
    far = [jnp.zeros((leaf, size), F32) for _ in range(3)]

    def visit(a, w):
        for c in range(3):
            far[c] = far[c] + expansion[c][:, a : a + 1] * w

    weights_loop([off_ref[a] for a in range(3)], visit)
    return far


def final_kernel(
    near_ref, many_ref, count_ref, spot_ref, fill_ref, off_ref, cell_ref, win_ref, loc_ref, out_ref,
    box_ref, r2a_ref, r2b_ref, load_a_ref, load_b_ref, cols_ref, sum_ref, sem,
):
    leaf, size = off_ref.shape[1], off_ref.shape[2]
    seg, ex = lax.axis_index("space"), lax.axis_index("exp")
    rows = win_ref.shape[0]
    fetch = pltpu.make_async_copy(win_ref, box_ref.at[0:rows], sem)
    fetch.start()
    box_ref[rows:, :] = jnp.zeros((8, size), F32)
    sum_ref[...] = jnp.zeros(sum_ref.shape, F32)
    fetch.wait()
    bufs = ((r2a_ref, load_a_ref), (r2b_ref, load_b_ref))
    turns = jnp.clip(count_ref[0] - ex * leaf, 0, leaf)
    near_field(seg, ex, leaf, near_ref, many_ref, spot_ref, box_ref, bufs, cols_ref, sum_ref)((turns + 1) // 2)
    far = leaf_far(cell_ref, off_ref, loc_ref)
    live = (iota((leaf, size), 1).astype(F32) < column(fill_ref[...], leaf)) & (iota((leaf, size), 0) < turns)
    for c in range(3):
        out_ref[c] = jnp.where(live, (far[c] + sum_ref[c]) * SCALE, 0.0)


def shape(*dims):
    return jax.ShapeDtypeStruct(dims, F32)


def tree_call(n_seg, n_ex, offsets, strength, cell_row, count, fill_row):
    n_x, per = n_ex // 2, n_seg // n_ex
    leaf, size = offsets.shape[1], offsets.shape[2]
    par = leaf * n_ex // 8
    dma = pltpu.SemaphoreType.DMA
    return pl.pallas_call(
        lambda *refs: tree_kernel(n_seg, n_x, per, *refs),
        out_shape=(shape(3, n_ex, leaf * 6, size), shape(3 * par, 512)),
        in_specs=[VMEM, VMEM, VMEM, SMEM, VMEM],
        out_specs=(ANY, VMEM),
        scratch_shapes=[
            pltpu.VMEM((leaf * 6, size), F32),
            pltpu.VMEM((leaf * 2, size), F32),
            pltpu.VMEM((64, 512), F32),
            pltpu.VMEM((3, n_ex, leaf * 2, size), F32),
            pltpu.VMEM((2 * par, 128), F32),
            pltpu.VMEM((per, 2 * par, 128), F32),
            pltpu.VMEM((64, 128), F32),
            pltpu.VMEM((n_ex, 64, 128), F32),
            pltpu.VMEM((6, 3, par + 16, 256), F32),
            pltpu.VMEM((3, 256, 512), F32),
            pltpu.VMEM((2, 256, 512), F32),
            pltpu.VMEM((3, 64, per * 64), F32),
            dma((14 * n_x + 5,)),
            dma((3, n_ex)),
            dma((3, n_ex)),
            dma((per,)),
            dma((per,)),
            dma((n_ex,)),
            dma,
        ],
        compiler_params=pltpu.CompilerParams(collective_id=0, has_side_effects=True, vmem_limit_bytes=BIG),
    )(offsets, strength, cell_row, count, fill_row)


def near_scratch(rows, count, leaf, size):
    return [
        pltpu.VMEM((rows + 8, size), F32),
        pltpu.VMEM((size, count * size), F32),
        pltpu.VMEM((size, count * size), F32),
        pltpu.VMEM((count, 8, size), F32),
        pltpu.VMEM((count, 8, size), F32),
        pltpu.VMEM((size, size), F32),
        pltpu.VMEM((3, leaf, size), F32),
    ]


def final_call(near, many, count, spot, fill_row, offsets, cell_row, window, loc):
    leaf, size = offsets.shape[1], offsets.shape[2]
    return pl.pallas_call(
        final_kernel,
        out_shape=shape(3, leaf, size),
        in_specs=[SMEM, SMEM, SMEM, SMEM, VMEM, VMEM, VMEM, ANY, VMEM],
        out_specs=VMEM,
        scratch_shapes=near_scratch(window.shape[0], near.shape[0], leaf, size) + [pltpu.SemaphoreType.DMA],
        compiler_params=pltpu.CompilerParams(vmem_limit_bytes=BIG),
    )(near, many, count, spot, fill_row, offsets, cell_row, window, loc)


def solution(mesh):
    n_seg, n_ex = mesh.shape["space"], mesh.shape["exp"]

    def body(offsets, strength, leaf_cell, leaf_count, leaf_fill, near_list, near_count):
        leaf, size = offsets.shape[1], offsets.shape[2]
        cell_row = leaf_cell.reshape(1, leaf)
        fill_row = leaf_fill.reshape(1, leaf)
        window, loc = tree_call(n_seg, n_ex, offsets, strength, cell_row, leaf_count, fill_row)
        window = window.reshape(3 * n_ex * leaf * 6, size)
        return final_call(near_list, near_count, leaf_count, leaf_cell, fill_row, offsets, cell_row, window, loc)

    in_specs = (
        P(None, ("space", "exp"), None),
        P(None, ("space", "exp"), None),
        P(("space", "exp")),
        P("space"),
        P(("space", "exp")),
        P(None, ("space", "exp")),
        P(("space", "exp")),
    )
    out_specs = P(None, ("space", "exp"), None)
    return jax.shard_map(body, mesh=mesh, in_specs=in_specs, out_specs=out_specs, check_vma=False)
```

```python
import math

import jax
import jax.numpy as jnp
from jax import lax
from jax.experimental import pallas as pl
from jax.experimental.pallas import tpu as pltpu
from jax.sharding import PartitionSpec as P

NODES = [math.cos((2 * k + 1) * math.pi / 8) for k in range(4)]
SMOOTH = 0.01
SCALE = 1.0 / (4.0 * math.pi)
F32 = jnp.float32
BF16 = jnp.bfloat16
VMEM = pl.BlockSpec(memory_space=pltpu.VMEM)
SMEM = pl.BlockSpec(memory_space=pltpu.SMEM)
ANY = pl.BlockSpec(memory_space=pl.ANY)
BIG = 60 * 1024 * 1024
NN = (((1,), (0,)), ((), ()))
NT = (((1,), (1,)), ((), ()))


def iota(shape, axis):
    return lax.broadcasted_iota(jnp.int32, shape, axis)


def split2(x):
    hi = x.astype(BF16)
    return hi, (x - hi.astype(F32)).astype(BF16)


def split3(x):
    hi = x.astype(BF16).astype(F32)
    rest = x - hi
    mid = rest.astype(BF16).astype(F32)
    return hi, mid, rest - mid


def bdot(a, b, dims=NN):
    return lax.dot_general(a, b, dims, preferred_element_type=F32)


def dot3(a, b, dims=NN):
    ah, al = a if isinstance(a, tuple) else split2(a)
    bh, bl = b if isinstance(b, tuple) else split2(b)
    return bdot(ah, bh, dims) + (bdot(al, bh, dims) + bdot(ah, bl, dims))


def pick_exact(one_hot, x):
    hi = x.astype(BF16)
    rest = x - hi.astype(F32)
    mid = rest.astype(BF16)
    low = (rest - mid.astype(F32)).astype(BF16)
    return bdot(one_hot, hi) + (bdot(one_hot, mid) + bdot(one_hot, low))


def node(k):
    return jnp.where(
        k == 0, NODES[0], jnp.where(k == 1, NODES[1], jnp.where(k == 2, NODES[2], NODES[3]))
    ).astype(F32)


def cheb(u):
    return u, 2.0 * u * u - 1.0, (4.0 * u * u - 3.0) * u


def factors(u):
    t1, t2, t3 = cheb(u)
    out = []
    for t in NODES:
        out.append(0.25 + t1 * (0.5 * t) + t2 * (0.5 * (2 * t * t - 1)) + t3 * (0.5 * (4 * t**3 - 3 * t)))
    return out


def cheb_pair(u, t):
    u1, u2, u3 = cheb(u)
    t1, t2, t3 = cheb(t)
    return 0.25 + 0.5 * (u1 * t1 + u2 * t2 + u3 * t3)


def column(row, count):
    spread = jnp.where(iota((count, count), 0) == iota((count, count), 1), row.astype(F32), 0.0)
    return jnp.sum(spread, axis=1, keepdims=True)


def weights_loop(offs, visit):
    fx, fy, fz = (factors(o) for o in offs)
    for i in range(4):
        for j in range(4):
            fxy = fx[i] * fy[j]
            for k in range(4):
                visit(16 * i + 4 * j + k, fxy * fz[k])


def particles(seg, ex, off_ref, str_ref, cell_ref, count_ref, fill_ref, rec_ref, mul_ref):
    leaf, size = off_ref.shape[1], off_ref.shape[2]
    cell_f = column(cell_ref[...], leaf)
    fill = column(fill_ref[...], leaf)
    cell = cell_f.astype(jnp.int32)
    slot = ex * leaf + iota((leaf, size), 0)
    alive = (slot < count_ref[0]) & (iota((leaf, size), 1).astype(F32) < fill)
    centre = (
        2 * seg + ((cell >> 1) & 1),
        cell >> 2,
        cell & 1,
    )
    offs = [off_ref[a] for a in range(3)]
    charge = []
    for a in range(3):
        pos = (centre[a].astype(F32) + 0.5) + 0.5 * offs[a]
        rec_ref[pl.ds(a, leaf, 6), :] = pos
        q = jnp.where(alive, str_ref[a], 0.0)
        rec_ref[pl.ds(3 + a, leaf, 6), :] = q
        charge.append(q)
    lane = iota((leaf, size), 1)
    acc = [jnp.zeros((leaf, size), F32), jnp.where(lane >= 64, cell_f, 0.0)]

    def visit(a, w):
        for c in range(3):
            total = jnp.sum(charge[c] * w, axis=1, keepdims=True)
            at = a + 64 * (c % 2)
            acc[c // 2] = jnp.where(lane == at, total, acc[c // 2])

    weights_loop(offs, visit)
    mul_ref[0:leaf, :] = acc[0]
    mul_ref[leaf : 2 * leaf, :] = acc[1]


def mesh_at(seg, ex):
    return {"space": seg, "exp": ex}


def remote(src, dst, send, recv, seg, ex):
    return pltpu.make_async_remote_copy(
        src_ref=src, dst_ref=dst, send_sem=send, recv_sem=recv,
        device_id=mesh_at(seg, ex), device_id_type=pl.DeviceIdType.MESH,
    )


def sorted_block(mul_ref, part, guard):
    n_ex, leaf = mul_ref.shape[1], mul_ref.shape[2] // 2
    slots = n_ex * leaf
    par = slots // 8
    m01 = mul_ref[part, :, 0:leaf, :].reshape(slots, 128)
    m2c = mul_ref[part, :, leaf : 2 * leaf, :].reshape(slots, 128)
    cells = jnp.swapaxes(m2c, 0, 1)[64:65, :]
    row = iota((slots, slots), 0)
    wanted = ((row % par) * 8 + row // par).astype(F32)
    one_hot = jnp.where((wanted == cells) & guard, 1.0, 0.0).astype(BF16)
    return pick_exact(one_hot, m01), pick_exact(one_hot, m2c)


def parent_moments(g01, g2):
    par = g01.shape[0] // 8
    total = jnp.zeros((2 * par, 128), F32)
    lane_b = iota((128, 128), 1)
    row_a = iota((128, 128), 0)
    bx, by, bz = (node((lane_b // w) % 4) for w in (16, 4, 1))
    ax, ay, az = (node((row_a // w) % 4) for w in (16, 4, 1))
    sx, sy, sz = ([cheb_pair(bit - 0.5 + 0.5 * a, b) for bit in (0, 1)] for a, b in ((ax, bx), (ay, by), (az, bz)))
    same = (lane_b // 64) == (row_a // 64)
    for h in range(8):
        table = jnp.where(same, sx[(h // 2) % 2] * sy[h // 4] * sz[h % 2], 0.0)
        lhs = jnp.concatenate([g01[h * par : (h + 1) * par], g2[h * par : (h + 1) * par]], axis=0)
        total = total + dot3(lhs, table)
    return total


def store_rows(grid_ref, j, g01, g2):
    par = g01.shape[0] // 8
    for odd in range(2):
        for c in range(3):
            src = g01 if c < 2 else g2
            lo = 64 * (c % 2)
            grid_ref[j * 2 + odd, c, 8 : 8 + par, :] = jnp.concatenate(
                [src[(4 * odd + r) * par : (4 * odd + r + 1) * par, lo : lo + 64] for r in range(4)], axis=1
            )


def m2l_tables(base_ref, near_x_ref):
    lane, row = iota((256, 512), 1), iota((256, 512), 0)
    ux = ((lane // 128) % 2).astype(F32) + 0.5 * node((lane // 16) % 4)
    vx = (row // 128).astype(F32) + 0.5 * node((row // 16) % 4)
    uz = ((lane // 64) % 2).astype(F32) + 0.5 * node(lane % 4)
    vz = ((row // 64) % 2).astype(F32) + 0.5 * node(row % 4)
    base_ref[1] = (uz - vz) * (uz - vz) + SMOOTH
    base_ref[2] = ux - vx
    near_x_ref[1] = ((row // 128) - (lane // 128) % 2).astype(F32)


def m2l_segment(j, par, grid_ref, base_ref, near_x_ref, loc_ref):
    lane1 = iota((1, 512), 1)
    up1 = (lane1 // 256).astype(F32)
    uy = up1 + 0.5 * node((lane1 // 4) % 4)
    vy = 0.5 * node((iota((256, 1), 0) // 4) % 4)
    shift = 2.0 * jnp.asarray(j, jnp.int32).astype(F32) - 2.0
    dx = base_ref[2] - shift
    base_ref[0] = dx * dx + base_ref[1]
    near_x_ref[0] = jnp.where(jnp.abs(near_x_ref[1] + shift) < 1.5, jnp.inf, 0.0)
    for odd in range(2):
        for i in range(3):
            height = 2 * i + odd - 2
            lhs = jnp.concatenate([grid_ref[j * 2 + odd, c, 7 + i : 7 + i + par, :] for c in range(3)], axis=0)
            near_y = jnp.where(jnp.abs(height - up1) < 1.5, jnp.inf, 0.0)
            dy = (uy - height) - vy
            g = lax.rsqrt(dy * dy + base_ref[0] + jnp.minimum(near_x_ref[0], near_y))
            loc_ref[...] += dot3(lhs, g)


def far_tables(seg, ex, per, far_ref):
    wide = per * 64
    lane, row = iota((64, wide), 1), iota((64, wide), 0)
    step = (seg - ex * per - lane // 64).astype(F32)
    dx = 2.0 * step + node(row // 16) - node((lane // 16) % 4)
    dz = node(row % 4) - node(lane % 4)
    far_ref[0] = dx * dx + (dz * dz + SMOOTH)
    far_ref[1] = node((row // 4) % 4) - node((lane // 4) % 4)
    far_ref[2] = jnp.where(jnp.abs(step) < 1.5, jnp.inf, 0.0)


def far_sum(pq_ref, far_ref):
    per = pq_ref.shape[0]
    par = pq_ref.shape[1] // 2
    wide = per * 64
    turn = 7 if (2 * par - 1) % 7 == 0 else 1
    rows = []
    for c in range(3):
        r0, l0 = par * (c // 2), 64 * (c % 2)
        rows.append(jnp.concatenate([pq_ref[q, r0 : r0 + par, l0 : l0 + 64] for q in range(per)], axis=1))
    rows.append(jnp.zeros((128 - 3 * par, wide), F32))
    ph, plo = split2(jnp.swapaxes(jnp.concatenate(rows, axis=0), 0, 1))
    p_to = iota((64, 128), 1) % par

    def some(i, acc):
        high, low = [], []
        for u in range(turn):
            delta = i * turn + u - (par - 1)
            dy = far_ref[1] + 2.0 * delta.astype(F32)
            gap = jnp.where(jnp.abs(delta) <= 1, jnp.inf, 0.0)
            gh, gl = split2(lax.rsqrt(dy * dy + far_ref[0] + jnp.minimum(far_ref[2], gap)))
            high.append(gh)
            low.append(gl)
        gh = jnp.concatenate(high, axis=0)
        got = bdot(gh, ph) + (bdot(jnp.concatenate(low, axis=0), ph) + bdot(gh, plo))
        for u in range(turn):
            delta = i * turn + u - (par - 1)
            moved = pltpu.roll(got[64 * u : 64 * u + 64], (delta + 128) % 128, 1)
            source = p_to - delta
            acc = acc + jnp.where((source >= 0) & (source < par), moved, 0.0)
        return acc

    return lax.fori_loop(0, (2 * par - 1) // turn, some, jnp.zeros((64, 128), F32))


def child_table(table_ref):
    lane, row = iota((64, 512), 1), iota((64, 512), 0)
    table = 1.0
    for bit, w in (((lane // 128) % 2, 16), (lane // 256, 4), ((lane // 64) % 2, 1)):
        table = table * cheb_pair(bit.astype(F32) - 0.5 + 0.5 * node((lane // w) % 4), node((row // w) % 4))
    table_ref[...] = table


def tree_kernel(
    n_seg, n_x, per, off_ref, str_ref, cell_ref, count_ref, fill_ref, near_ref, many_ref, spot_ref, out_ref,
    loc_ref, rec_ref, mul_ref, table_ref, mwin_ref, pm_ref, pq_ref, part_ref, share_ref, grid_ref, base_ref,
    near_x_ref, far_ref, box_ref, r2a_ref, r2b_ref, load_a_ref, load_b_ref, cols_ref, sum_ref,
    send, mrecv, precv, swap_send, swap_recv, share_recv, own_sem,
):
    n_ex = 2 * n_x
    seg, ex = lax.axis_index("space"), lax.axis_index("exp")
    x, core = ex // 2, ex % 2
    prev, after = (seg + n_seg - 1) % n_seg, (seg + 1) % n_seg
    ring = [((x + d) % n_x) * 2 + core for d in range(n_x)]
    mates = [((x + d) % n_x) * 2 + 1 - core for d in range(n_x)]
    order = [1, n_x - 1] + list(range(2, n_x - 1))
    mate = mates[0]
    others = [ring[d] for d in order] + [mates[d] for d in [0] + order]
    there = seg // per
    mine = ex == there
    par = mul_ref.shape[0] // 2 * n_ex // 8
    leaf, size = off_ref.shape[1], off_ref.shape[2]
    barrier = pltpu.get_barrier_semaphore()
    sent = []

    def box(part, who):
        return box_ref.at[pl.ds(pl.multiple_of((part * n_ex + who) * (leaf * 6), 8), leaf * 6)]

    def hello(to_seg, to_ex):
        pl.semaphore_signal(barrier, 1, device_id=mesh_at(to_seg, to_ex), device_id_type=pl.DeviceIdType.MESH)

    def not_self(i):
        return jnp.logical_not(mine & (seg % per == i))

    for o in others:
        hello(seg, o)
    hello(prev, ex)
    hello(after, ex)
    for i in range(per):

        @pl.when(not_self(i))
        def _():
            hello(ex * per + i, there)

    particles(seg, ex, off_ref, str_ref, cell_ref, count_ref, fill_ref, rec_ref, mul_ref)
    grid_ref[...] = jnp.zeros(grid_ref.shape, F32)
    loc_ref[...] = jnp.zeros(loc_ref.shape, F32)
    m2l_tables(base_ref, near_x_ref)
    far_tables(seg, ex, per, far_ref)
    child_table(table_ref)
    box_ref[18 * n_ex * leaf :, :] = jnp.zeros((8, size), F32)
    pl.semaphore_wait(barrier, len(others) + 2 + jnp.where(mine, per - 1, per))

    def push(src, dst, recv, to_seg, to_ex):
        copy = remote(src, dst, send.at[len(sent)], recv, to_seg, to_ex)
        copy.start()
        sent.append(copy)

    def push_m(src, part, who, to_seg, to_ex):
        push(src, mwin_ref.at[part, who], mrecv.at[part, who], to_seg, to_ex)

    def push_p(src, part, who, to_seg, to_ex):
        push(src, box(part, who), precv.at[part, who], to_seg, to_ex)

    def got_m(part, who):
        remote(mul_ref, mwin_ref.at[part, who], send.at[0], mrecv.at[part, who], seg, mate).wait_recv()

    def got_p(part, who):
        remote(rec_ref, box(part, who), send.at[0], precv.at[part, who], seg, mate).wait_recv()

    for o in others:
        push_m(mul_ref, 1, ex, seg, o)
    push_m(mul_ref, 0, ex, after, ex)
    push_m(mul_ref, 2, ex, prev, ex)
    for d in order:
        push_p(rec_ref, 1, ex, seg, ring[d])
    push_p(rec_ref, 0, ex, after, ex)
    push_p(rec_ref, 2, ex, prev, ex)
    push_p(rec_ref, 1, ex, seg, mate)
    keep = pltpu.make_async_copy(rec_ref, box(1, ex), own_sem)
    keep.start()
    mwin_ref[1, ex] = mul_ref[...]
    for d in order:
        got_m(1, ring[d])
        push_m(mwin_ref.at[1, ring[d]], 0, ring[d], after, ex)
        push_m(mwin_ref.at[1, ring[d]], 2, ring[d], prev, ex)
    for d in range(n_x):
        got_m(1, mates[d])
    g01, g2 = sorted_block(mwin_ref, 1, True)
    pm_ref[...] = parent_moments(g01, g2)
    store_rows(grid_ref, 1, g01, g2)

    def pass_on(d):
        got_p(1, ring[d])
        push_p(box(1, ring[d]), 0, ring[d], after, ex)
        push_p(box(1, ring[d]), 2, ring[d], prev, ex)
        push_p(box(1, ring[d]), 1, ring[d], seg, mate)

    def swap(i):
        return remote(pm_ref, pq_ref.at[seg % per], swap_send.at[i], swap_recv.at[seg % per], ex * per + i, there)

    for i in range(per):

        @pl.when(not_self(i))
        def _():
            swap(i).start()

    @pl.when(mine)
    def _():
        pq_ref[seg % per] = pm_ref[...]

    for d in order:
        pass_on(d)
    m2l_segment(1, par, grid_ref, base_ref, near_x_ref, loc_ref)
    for d in [0] + order:
        for part in (0, 2):
            got_m(part, ring[d])
            push_m(mwin_ref.at[part, ring[d]], part, ring[d], seg, mate)

    def pass_mate(d):
        for part in (0, 2):
            got_p(part, ring[d])
            push_p(box(part, ring[d]), part, ring[d], seg, mate)

    pass_mate(0)
    for d in range(n_x):
        for part in (0, 2):
            got_m(part, mates[d])
    for part, guard in ((0, seg > 0), (2, seg < n_seg - 1)):
        g01, g2 = sorted_block(mwin_ref, part, guard)
        store_rows(grid_ref, part, g01, g2)

    def sides(i, carry):
        m2l_segment(2 * i, par, grid_ref, base_ref, near_x_ref, loc_ref)
        return carry

    lax.fori_loop(0, 2, sides, 0)
    pass_mate(order[0])
    pass_mate(order[1])
    for i in range(per):

        @pl.when(not_self(i))
        def _():
            remote(pm_ref, pq_ref.at[i], swap_send.at[i], swap_recv.at[i], ex * per + i, there).wait_recv()
            swap(i).wait_send()

    part_ref[...] = far_sum(pq_ref, far_ref)
    for d in order[2:]:
        pass_mate(d)
    for o in others:
        push(part_ref, share_ref.at[ex], share_recv.at[ex], seg, o)
    share_ref[ex] = part_ref[...]
    for d in range(n_x):
        for part in range(3):
            got_p(part, mates[d])
    keep.wait()
    bufs = ((r2a_ref, load_a_ref), (r2b_ref, load_b_ref))
    near_field(seg, ex, leaf, n_ex * leaf, near_ref, many_ref, spot_ref, box_ref, bufs, cols_ref, sum_ref)(leaf // 2)
    for o in others:
        remote(part_ref, share_ref.at[o], send.at[0], share_recv.at[o], seg, o).wait_recv()
    parent = share_ref[0]
    for i in range(1, n_ex):
        parent = parent + share_ref[i]
    loc_ref[...] += dot3(jnp.swapaxes(parent, 0, 1)[: 3 * par, :], table_ref[...])
    far = leaf_far(cell_ref, off_ref, loc_ref)
    slot = ex * leaf + iota((leaf, size), 0)
    live = (iota((leaf, size), 1).astype(F32) < column(fill_ref[...], leaf)) & (slot < count_ref[0])
    for c in range(3):
        out_ref[c] = jnp.where(live, (far[c] + sum_ref[c]) * SCALE, 0.0)
    for copy in sent:
        copy.wait_send()


def near_field(seg, ex, leaf, slots, near_ref, many_ref, spot_ref, box_ref, bufs, cols_ref, near_out_ref):
    count, size = near_ref.shape[0], 128
    start = (seg - 1) * slots
    row8 = iota((8, size), 0)
    first, second = row8 < 3, (row8 >= 3) & (row8 < 6)
    none = jnp.zeros((8, size), F32)
    keep = jnp.where(row8 < 6, 1.0, 0.0)
    block = 32

    def frame(t):
        c = spot_ref[t]
        spot = (2 * seg + ((c >> 1) & 1), c >> 2, c & 1)
        mx, my, mz = (jnp.where(row8 == a, m.astype(F32) + 0.5, 0.0) for a, m in enumerate(spot))
        return mx + my + mz

    def local(rows, middle):
        near = jnp.where(first, rows - middle, 0.0)
        return near + pltpu.roll(near, 3, 0)

    def target_side(t, middle):
        here = local(box_ref[pl.ds((slots + ex * leaf + t) * 6, 8), :], middle)
        xh, xm, xl = split3(-2.0 * here)
        length = 0.5 * jnp.sum(here * here, axis=0, keepdims=True) + SMOOTH
        nh, nm, nl = split3(length)
        norm = jnp.where(row8 == 3, nh, jnp.where(row8 == 4, nm, nl))
        cross = jnp.where(first, xh, jnp.where(second, xm, 0.0))
        last = jnp.where(first, xh, jnp.where(second, xl, 0.0))
        tail = jnp.where(first, 1.0, jnp.where(second, norm, 0.0))
        side = jnp.concatenate([cross, cross, last, keep, tail] + [none] * 11, axis=0)
        return jnp.swapaxes(side, 0, 1).astype(BF16)[:, 0:48]

    def pair(t, k0, middle, side, many, buf):
        r2_ref, load_ref = buf
        feats = []
        for k in (k0, k0 + 1):
            rows = box_ref[pl.ds(jnp.clip(near_ref[k, t] - start, 0, 3 * slots - 1) * 6, 8), :]
            y = local(rows, middle)
            yh, ym, yl = split3(y)
            sh, sm, sl = split3(y * y)
            feat = [yh, ym, jnp.where(first, yl, yh), jnp.where(first, sh, sm), jnp.where(first, sl, 1.0), none]
            feats.append(jnp.concatenate(feat, axis=0).astype(BF16))
            load_ref[k] = rows * jnp.clip(many - k, 0, 1).astype(F32)
        r2_ref[:, size * k0 : size * k0 + 2 * size] = bdot(side, jnp.concatenate(feats, axis=1))

    def gather_rows(n, buf):
        r2_ref, load_ref = buf
        at = block * n
        acc = [jnp.zeros((block, size), F32) for _ in range(3)]
        for k in range(count):
            g = lax.rsqrt(r2_ref[at : at + block, size * k : size * k + size])
            for c in range(3):
                acc[c] = acc[c] + g * load_ref[k, 3 + c : 4 + c, :]
        lane = iota((block, size), 1)
        s0, s1, s2 = (jnp.sum(x, axis=1, keepdims=True) for x in acc)
        cols_ref[at : at + block, :] = jnp.where(lane == 0, s0, jnp.where(lane == 1, s1, s2))

    def store(t):
        result = jnp.swapaxes(cols_ref[...], 0, 1)
        for c in range(3):
            near_out_ref[c, pl.ds(t, 1), :] = result[c : c + 1, :]

    def work(t_next, next_buf, t_now, now_buf):
        jobs = list(range(size // block)) if now_buf is not None else []
        steps = count // 2
        if next_buf is not None:
            middle = frame(t_next)
            side = target_side(t_next, middle)
            many = many_ref[t_next]
        for p in range(steps):
            if next_buf is not None:
                pair(t_next, 2 * p, middle, side, many, next_buf)
            while jobs and (size // block - len(jobs)) * steps < (p + 1) * (size // block):
                gather_rows(jobs.pop(0), now_buf)
        if now_buf is not None:
            store(t_now)

    def run(turns):
        work(0, bufs[0], None, None)

        def two(i, carry):
            t = 2 * i
            work(t + 1, bufs[1], t, bufs[0])
            work((t + 2) % leaf, bufs[0], t + 1, bufs[1])
            return carry

        lax.fori_loop(0, turns, two, 0)

    return run


def leaf_far(cell_ref, off_ref, loc_ref):
    leaf, size = off_ref.shape[1], off_ref.shape[2]
    par = loc_ref.shape[0] // 3
    cell = column(cell_ref[...], leaf).astype(jnp.int32)
    chosen = jnp.where((cell >> 3) == iota((leaf, par), 1), 1.0, 0.0).astype(BF16)
    child = cell & 7
    lane = iota((leaf, 128), 1)
    expansion = []
    for c in range(3):
        wide = pick_exact(chosen, loc_ref[c * par : (c + 1) * par, :])
        kept = jnp.zeros((leaf, 128), F32)
        for i in range(4):
            kept = kept + jnp.where(lane // 64 + 2 * i == child, wide[:, 128 * i : 128 * i + 128], 0.0)
        expansion.append(kept + pltpu.roll(kept, 64, 1))
    far = [jnp.zeros((leaf, size), F32) for _ in range(3)]

    def visit(a, w):
        for c in range(3):
            far[c] = far[c] + expansion[c][:, a : a + 1] * w

    weights_loop([off_ref[a] for a in range(3)], visit)
    return far


def shape(*dims):
    return jax.ShapeDtypeStruct(dims, F32)


def tree_call(n_seg, n_ex, offsets, strength, cell_row, count, fill_row, near, many, spot):
    n_x, per = n_ex // 2, n_seg // n_ex
    leaf, size = offsets.shape[1], offsets.shape[2]
    par = leaf * n_ex // 8
    dma = pltpu.SemaphoreType.DMA
    return pl.pallas_call(
        lambda *refs: tree_kernel(n_seg, n_x, per, *refs),
        out_shape=shape(3, leaf, size),
        in_specs=[VMEM, VMEM, VMEM, SMEM, VMEM, SMEM, SMEM, SMEM],
        out_specs=VMEM,
        scratch_shapes=[
            pltpu.VMEM((3 * par, 512), F32),
            pltpu.VMEM((leaf * 6, size), F32),
            pltpu.VMEM((leaf * 2, size), F32),
            pltpu.VMEM((64, 512), F32),
            pltpu.VMEM((3, n_ex, leaf * 2, size), F32),
            pltpu.VMEM((2 * par, 128), F32),
            pltpu.VMEM((per, 2 * par, 128), F32),
            pltpu.VMEM((64, 128), F32),
            pltpu.VMEM((n_ex, 64, 128), F32),
            pltpu.VMEM((6, 3, par + 16, 256), F32),
            pltpu.VMEM((3, 256, 512), F32),
            pltpu.VMEM((2, 256, 512), F32),
            pltpu.VMEM((3, 64, per * 64), F32),
            *near_scratch(18 * n_ex * leaf, near.shape[0], leaf, size),
            dma((14 * n_x + 5,)),
            dma((3, n_ex)),
            dma((3, n_ex)),
            dma((per,)),
            dma((per,)),
            dma((n_ex,)),
            dma,
        ],
        compiler_params=pltpu.CompilerParams(collective_id=0, has_side_effects=True, vmem_limit_bytes=BIG),
    )(offsets, strength, cell_row, count, fill_row, near, many, spot)


def near_scratch(rows, count, leaf, size):
    return [
        pltpu.VMEM((rows + 8, size), F32),
        pltpu.VMEM((size, count * size), F32),
        pltpu.VMEM((size, count * size), F32),
        pltpu.VMEM((count, 8, size), F32),
        pltpu.VMEM((count, 8, size), F32),
        pltpu.VMEM((size, size), F32),
        pltpu.VMEM((3, leaf, size), F32),
    ]


def solution(mesh):
    n_seg, n_ex = mesh.shape["space"], mesh.shape["exp"]

    def body(offsets, strength, leaf_cell, leaf_count, leaf_fill, near_list, near_count):
        leaf, size = offsets.shape[1], offsets.shape[2]
        cell_row = leaf_cell.reshape(1, leaf)
        fill_row = leaf_fill.reshape(1, leaf)
        return tree_call(
            n_seg, n_ex, offsets, strength, cell_row, leaf_count, fill_row, near_list, near_count, leaf_cell
        )

    in_specs = (
        P(None, ("space", "exp"), None),
        P(None, ("space", "exp"), None),
        P(("space", "exp")),
        P("space"),
        P(("space", "exp")),
        P(None, ("space", "exp")),
        P(("space", "exp")),
    )
    out_specs = P(None, ("space", "exp"), None)
    return jax.shard_map(body, mesh=mesh, in_specs=in_specs, out_specs=out_specs, check_vma=False)
```

```python
import math

import jax
import jax.numpy as jnp
from jax import lax
from jax.experimental import pallas as pl
from jax.experimental.pallas import tpu as pltpu
from jax.sharding import PartitionSpec as P

NODES = [math.cos((2 * k + 1) * math.pi / 8) for k in range(4)]
SMOOTH = 0.01
SCALE = 1.0 / (4.0 * math.pi)
F32 = jnp.float32
BF16 = jnp.bfloat16
VMEM = pl.BlockSpec(memory_space=pltpu.VMEM)
SMEM = pl.BlockSpec(memory_space=pltpu.SMEM)
ANY = pl.BlockSpec(memory_space=pl.ANY)
BIG = 60 * 1024 * 1024
NN = (((1,), (0,)), ((), ()))
NT = (((1,), (1,)), ((), ()))


def iota(shape, axis):
    return lax.broadcasted_iota(jnp.int32, shape, axis)


def split2(x):
    hi = x.astype(BF16)
    return hi, (x - hi.astype(F32)).astype(BF16)


def split3(x):
    hi = x.astype(BF16).astype(F32)
    rest = x - hi
    mid = rest.astype(BF16).astype(F32)
    return hi, mid, rest - mid


def bdot(a, b, dims=NN):
    return lax.dot_general(a, b, dims, preferred_element_type=F32)


def dot3(a, b, dims=NN):
    ah, al = a if isinstance(a, tuple) else split2(a)
    bh, bl = b if isinstance(b, tuple) else split2(b)
    return bdot(ah, bh, dims) + (bdot(al, bh, dims) + bdot(ah, bl, dims))


def pick_exact(one_hot, x):
    hi = x.astype(BF16)
    rest = x - hi.astype(F32)
    mid = rest.astype(BF16)
    low = (rest - mid.astype(F32)).astype(BF16)
    return bdot(one_hot, hi) + (bdot(one_hot, mid) + bdot(one_hot, low))


def node(k):
    return jnp.where(
        k == 0, NODES[0], jnp.where(k == 1, NODES[1], jnp.where(k == 2, NODES[2], NODES[3]))
    ).astype(F32)


def cheb(u):
    return u, 2.0 * u * u - 1.0, (4.0 * u * u - 3.0) * u


def factors(u):
    t1, t2, t3 = cheb(u)
    out = []
    for t in NODES:
        out.append(0.25 + t1 * (0.5 * t) + t2 * (0.5 * (2 * t * t - 1)) + t3 * (0.5 * (4 * t**3 - 3 * t)))
    return out


def cheb_pair(u, t):
    u1, u2, u3 = cheb(u)
    t1, t2, t3 = cheb(t)
    return 0.25 + 0.5 * (u1 * t1 + u2 * t2 + u3 * t3)


def column(row, count):
    spread = jnp.where(iota((count, count), 0) == iota((count, count), 1), row.astype(F32), 0.0)
    return jnp.sum(spread, axis=1, keepdims=True)


def weights_loop(offs, visit):
    fx, fy, fz = (factors(o) for o in offs)
    for i in range(4):
        for j in range(4):
            fxy = fx[i] * fy[j]
            for k in range(4):
                visit(16 * i + 4 * j + k, fxy * fz[k])


def particles(seg, ex, off_ref, str_ref, cell_ref, count_ref, fill_ref, rec_ref, mul_ref):
    leaf, size = off_ref.shape[1], off_ref.shape[2]
    cell_f = column(cell_ref[...], leaf)
    fill = column(fill_ref[...], leaf)
    cell = cell_f.astype(jnp.int32)
    slot = ex * leaf + iota((leaf, size), 0)
    alive = (slot < count_ref[0]) & (iota((leaf, size), 1).astype(F32) < fill)
    centre = (
        2 * seg + ((cell >> 1) & 1),
        cell >> 2,
        cell & 1,
    )
    offs = [off_ref[a] for a in range(3)]
    charge = []
    for a in range(3):
        pos = (centre[a].astype(F32) + 0.5) + 0.5 * offs[a]
        rec_ref[pl.ds(a, leaf, 6), :] = pos
        q = jnp.where(alive, str_ref[a], 0.0)
        rec_ref[pl.ds(3 + a, leaf, 6), :] = q
        charge.append(q)
    lane = iota((leaf, size), 1)
    acc = [jnp.zeros((leaf, size), F32), jnp.where(lane >= 64, cell_f, 0.0)]

    def visit(a, w):
        for c in range(3):
            total = jnp.sum(charge[c] * w, axis=1, keepdims=True)
            at = a + 64 * (c % 2)
            acc[c // 2] = jnp.where(lane == at, total, acc[c // 2])

    weights_loop(offs, visit)
    mul_ref[0:leaf, :] = acc[0]
    mul_ref[leaf : 2 * leaf, :] = acc[1]


def mesh_at(seg, ex):
    return {"space": seg, "exp": ex}


def remote(src, dst, send, recv, seg, ex):
    return pltpu.make_async_remote_copy(
        src_ref=src, dst_ref=dst, send_sem=send, recv_sem=recv,
        device_id=mesh_at(seg, ex), device_id_type=pl.DeviceIdType.MESH,
    )


def sorted_block(mul_ref, part, guard):
    n_ex, leaf = mul_ref.shape[1], mul_ref.shape[2] // 2
    slots = n_ex * leaf
    par = slots // 8
    m01 = mul_ref[part, :, 0:leaf, :].reshape(slots, 128)
    m2c = mul_ref[part, :, leaf : 2 * leaf, :].reshape(slots, 128)
    cells = jnp.swapaxes(m2c, 0, 1)[64:65, :]
    row = iota((slots, slots), 0)
    wanted = ((row % par) * 8 + row // par).astype(F32)
    one_hot = jnp.where((wanted == cells) & guard, 1.0, 0.0).astype(BF16)
    return pick_exact(one_hot, m01), pick_exact(one_hot, m2c)


def parent_moments(g01, g2):
    par = g01.shape[0] // 8
    total = jnp.zeros((2 * par, 128), F32)
    lane_b = iota((128, 128), 1)
    row_a = iota((128, 128), 0)
    bx, by, bz = (node((lane_b // w) % 4) for w in (16, 4, 1))
    ax, ay, az = (node((row_a // w) % 4) for w in (16, 4, 1))
    sx, sy, sz = ([cheb_pair(bit - 0.5 + 0.5 * a, b) for bit in (0, 1)] for a, b in ((ax, bx), (ay, by), (az, bz)))
    same = (lane_b // 64) == (row_a // 64)
    for h in range(8):
        table = jnp.where(same, sx[(h // 2) % 2] * sy[h // 4] * sz[h % 2], 0.0)
        lhs = jnp.concatenate([g01[h * par : (h + 1) * par], g2[h * par : (h + 1) * par]], axis=0)
        total = total + dot3(lhs, table)
    return total


def store_rows(grid_ref, j, g01, g2):
    par = g01.shape[0] // 8
    for odd in range(2):
        for c in range(3):
            src = g01 if c < 2 else g2
            lo = 64 * (c % 2)
            grid_ref[j * 2 + odd, c, 8 : 8 + par, :] = jnp.concatenate(
                [src[(4 * odd + r) * par : (4 * odd + r + 1) * par, lo : lo + 64] for r in range(4)], axis=1
            )


def m2l_tables(base_ref, near_x_ref):
    lane, row = iota((256, 512), 1), iota((256, 512), 0)
    ux = ((lane // 128) % 2).astype(F32) + 0.5 * node((lane // 16) % 4)
    vx = (row // 128).astype(F32) + 0.5 * node((row // 16) % 4)
    uz = ((lane // 64) % 2).astype(F32) + 0.5 * node(lane % 4)
    vz = ((row // 64) % 2).astype(F32) + 0.5 * node(row % 4)
    base_ref[1] = (uz - vz) * (uz - vz) + SMOOTH
    base_ref[2] = ux - vx
    near_x_ref[1] = ((row // 128) - (lane // 128) % 2).astype(F32)


def m2l_segment(j, par, grid_ref, base_ref, near_x_ref, loc_ref):
    lane1 = iota((1, 512), 1)
    up1 = (lane1 // 256).astype(F32)
    uy = up1 + 0.5 * node((lane1 // 4) % 4)
    vy = 0.5 * node((iota((256, 1), 0) // 4) % 4)
    shift = 2.0 * jnp.asarray(j, jnp.int32).astype(F32) - 2.0
    dx = base_ref[2] - shift
    base_ref[0] = dx * dx + base_ref[1]
    near_x_ref[0] = jnp.where(jnp.abs(near_x_ref[1] + shift) < 1.5, jnp.inf, 0.0)
    for odd in range(2):
        for i in range(3):
            height = 2 * i + odd - 2
            lhs = jnp.concatenate([grid_ref[j * 2 + odd, c, 7 + i : 7 + i + par, :] for c in range(3)], axis=0)
            near_y = jnp.where(jnp.abs(height - up1) < 1.5, jnp.inf, 0.0)
            dy = (uy - height) - vy
            g = lax.rsqrt(dy * dy + base_ref[0] + jnp.minimum(near_x_ref[0], near_y))
            loc_ref[...] += dot3(lhs, g)


def far_tables(seg, ex, per, far_ref):
    wide = per * 64
    lane, row = iota((64, wide), 1), iota((64, wide), 0)
    step = (seg - ex * per - lane // 64).astype(F32)
    dx = 2.0 * step + node(row // 16) - node((lane // 16) % 4)
    dz = node(row % 4) - node(lane % 4)
    far_ref[0] = dx * dx + (dz * dz + SMOOTH)
    far_ref[1] = node((row // 4) % 4) - node((lane // 4) % 4)
    far_ref[2] = jnp.where(jnp.abs(step) < 1.5, jnp.inf, 0.0)


def far_sum(pq_ref, far_ref):
    per = pq_ref.shape[0]
    par = pq_ref.shape[1] // 2
    wide = per * 64
    turn = 7 if (2 * par - 1) % 7 == 0 else 1
    rows = []
    for c in range(3):
        r0, l0 = par * (c // 2), 64 * (c % 2)
        rows.append(jnp.concatenate([pq_ref[q, r0 : r0 + par, l0 : l0 + 64] for q in range(per)], axis=1))
    rows.append(jnp.zeros((128 - 3 * par, wide), F32))
    ph, plo = split2(jnp.swapaxes(jnp.concatenate(rows, axis=0), 0, 1))
    p_to = iota((64, 128), 1) % par

    def some(i, acc):
        high, low = [], []
        for u in range(turn):
            delta = i * turn + u - (par - 1)
            dy = far_ref[1] + 2.0 * delta.astype(F32)
            gap = jnp.where(jnp.abs(delta) <= 1, jnp.inf, 0.0)
            gh, gl = split2(lax.rsqrt(dy * dy + far_ref[0] + jnp.minimum(far_ref[2], gap)))
            high.append(gh)
            low.append(gl)
        gh = jnp.concatenate(high, axis=0)
        got = bdot(gh, ph) + (bdot(jnp.concatenate(low, axis=0), ph) + bdot(gh, plo))
        for u in range(turn):
            delta = i * turn + u - (par - 1)
            moved = pltpu.roll(got[64 * u : 64 * u + 64], (delta + 128) % 128, 1)
            source = p_to - delta
            acc = acc + jnp.where((source >= 0) & (source < par), moved, 0.0)
        return acc

    return lax.fori_loop(0, (2 * par - 1) // turn, some, jnp.zeros((64, 128), F32))


def child_table(table_ref):
    lane, row = iota((64, 512), 1), iota((64, 512), 0)
    table = 1.0
    for bit, w in (((lane // 128) % 2, 16), (lane // 256, 4), ((lane // 64) % 2, 1)):
        table = table * cheb_pair(bit.astype(F32) - 0.5 + 0.5 * node((lane // w) % 4), node((row // w) % 4))
    table_ref[...] = table


def tree_kernel(
    n_seg, n_x, per, off_ref, str_ref, cell_ref, count_ref, fill_ref, near_ref, many_ref, spot_ref, out_ref,
    loc_ref, rec_ref, mul_ref, table_ref, mwin_ref, pm_ref, pq_ref, part_ref, share_ref, grid_ref, base_ref,
    near_x_ref, far_ref, box_ref, r2a_ref, r2b_ref, load_a_ref, load_b_ref, cols_ref, sum_ref, side_ref,
    send, mrecv, precv, swap_send, swap_recv, share_recv, own_sem,
):
    n_ex = 2 * n_x
    seg, ex = lax.axis_index("space"), lax.axis_index("exp")
    x, core = ex // 2, ex % 2
    prev, after = (seg + n_seg - 1) % n_seg, (seg + 1) % n_seg
    ring = [((x + d) % n_x) * 2 + core for d in range(n_x)]
    mates = [((x + d) % n_x) * 2 + 1 - core for d in range(n_x)]
    order = [1, n_x - 1] + list(range(2, n_x - 1))
    mate = mates[0]
    others = [ring[d] for d in order] + [mates[d] for d in [0] + order]
    there = seg // per
    mine = ex == there
    par = mul_ref.shape[0] // 2 * n_ex // 8
    leaf, size = off_ref.shape[1], off_ref.shape[2]
    own_rec = rec_ref.at[0 : leaf * 6]
    barrier = pltpu.get_barrier_semaphore()
    sent = []

    def box(part, who):
        return box_ref.at[pl.ds(pl.multiple_of((part * n_ex + who) * (leaf * 6), 8), leaf * 6)]

    def hello(to_seg, to_ex):
        pl.semaphore_signal(barrier, 1, device_id=mesh_at(to_seg, to_ex), device_id_type=pl.DeviceIdType.MESH)

    def not_self(i):
        return jnp.logical_not(mine & (seg % per == i))

    for o in others:
        hello(seg, o)
    hello(prev, ex)
    hello(after, ex)
    for i in range(per):

        @pl.when(not_self(i))
        def _():
            hello(ex * per + i, there)

    particles(seg, ex, off_ref, str_ref, cell_ref, count_ref, fill_ref, rec_ref, mul_ref)
    grid_ref[...] = jnp.zeros(grid_ref.shape, F32)
    loc_ref[...] = jnp.zeros(loc_ref.shape, F32)
    m2l_tables(base_ref, near_x_ref)
    far_tables(seg, ex, per, far_ref)
    child_table(table_ref)
    rec_ref[leaf * 6 :, :] = jnp.zeros((8, size), F32)
    target_sides(seg, leaf, spot_ref, rec_ref, side_ref)
    box_ref[18 * n_ex * leaf :, :] = jnp.zeros((8, size), F32)
    pl.semaphore_wait(barrier, len(others) + 2 + jnp.where(mine, per - 1, per))

    def push(src, dst, recv, to_seg, to_ex):
        copy = remote(src, dst, send.at[len(sent)], recv, to_seg, to_ex)
        copy.start()
        sent.append(copy)

    def push_m(src, part, who, to_seg, to_ex):
        push(src, mwin_ref.at[part, who], mrecv.at[part, who], to_seg, to_ex)

    def push_p(src, part, who, to_seg, to_ex):
        push(src, box(part, who), precv.at[part, who], to_seg, to_ex)

    def got_m(part, who):
        remote(mul_ref, mwin_ref.at[part, who], send.at[0], mrecv.at[part, who], seg, mate).wait_recv()

    def got_p(part, who):
        remote(own_rec, box(part, who), send.at[0], precv.at[part, who], seg, mate).wait_recv()

    for o in others:
        push_m(mul_ref, 1, ex, seg, o)
    push_m(mul_ref, 0, ex, after, ex)
    push_m(mul_ref, 2, ex, prev, ex)
    for d in order:
        push_p(own_rec, 1, ex, seg, ring[d])
    push_p(own_rec, 0, ex, after, ex)
    push_p(own_rec, 2, ex, prev, ex)
    push_p(own_rec, 1, ex, seg, mate)
    keep = pltpu.make_async_copy(own_rec, box(1, ex), own_sem)
    keep.start()
    mwin_ref[1, ex] = mul_ref[...]
    for d in order:
        got_m(1, ring[d])
        push_m(mwin_ref.at[1, ring[d]], 0, ring[d], after, ex)
        push_m(mwin_ref.at[1, ring[d]], 2, ring[d], prev, ex)
    for d in range(n_x):
        got_m(1, mates[d])
    g01, g2 = sorted_block(mwin_ref, 1, True)
    pm_ref[...] = parent_moments(g01, g2)
    store_rows(grid_ref, 1, g01, g2)

    def pass_on(d):
        got_p(1, ring[d])
        push_p(box(1, ring[d]), 0, ring[d], after, ex)
        push_p(box(1, ring[d]), 2, ring[d], prev, ex)
        push_p(box(1, ring[d]), 1, ring[d], seg, mate)

    def swap(i):
        return remote(pm_ref, pq_ref.at[seg % per], swap_send.at[i], swap_recv.at[seg % per], ex * per + i, there)

    for i in range(per):

        @pl.when(not_self(i))
        def _():
            swap(i).start()

    @pl.when(mine)
    def _():
        pq_ref[seg % per] = pm_ref[...]

    for d in order:
        pass_on(d)
    m2l_segment(1, par, grid_ref, base_ref, near_x_ref, loc_ref)
    for d in [0] + order:
        for part in (0, 2):
            got_m(part, ring[d])
            push_m(mwin_ref.at[part, ring[d]], part, ring[d], seg, mate)

    def pass_mate(d):
        for part in (0, 2):
            got_p(part, ring[d])
            push_p(box(part, ring[d]), part, ring[d], seg, mate)

    pass_mate(0)
    for d in range(n_x):
        for part in (0, 2):
            got_m(part, mates[d])
    for part, guard in ((0, seg > 0), (2, seg < n_seg - 1)):
        g01, g2 = sorted_block(mwin_ref, part, guard)
        store_rows(grid_ref, part, g01, g2)

    def sides(i, carry):
        m2l_segment(2 * i, par, grid_ref, base_ref, near_x_ref, loc_ref)
        return carry

    lax.fori_loop(0, 2, sides, 0)
    for d in order:
        pass_mate(d)
    for i in range(per):

        @pl.when(not_self(i))
        def _():
            remote(pm_ref, pq_ref.at[i], swap_send.at[i], swap_recv.at[i], ex * per + i, there).wait_recv()
            swap(i).wait_send()

    part_ref[...] = far_sum(pq_ref, far_ref)
    for o in others:
        push(part_ref, share_ref.at[ex], share_recv.at[ex], seg, o)
    share_ref[ex] = part_ref[...]
    for d in range(n_x):
        for part in range(3):
            got_p(part, mates[d])
    keep.wait()
    bufs = ((r2a_ref, load_a_ref), (r2b_ref, load_b_ref))
    near_field(seg, leaf, n_ex * leaf, near_ref, many_ref, spot_ref, side_ref, box_ref, bufs, cols_ref, sum_ref)(leaf // 2)
    for o in others:
        remote(part_ref, share_ref.at[o], send.at[0], share_recv.at[o], seg, o).wait_recv()
    parent = share_ref[0]
    for i in range(1, n_ex):
        parent = parent + share_ref[i]
    loc_ref[...] += dot3(jnp.swapaxes(parent, 0, 1)[: 3 * par, :], table_ref[...])
    far = leaf_far(cell_ref, off_ref, loc_ref)
    slot = ex * leaf + iota((leaf, size), 0)
    live = (iota((leaf, size), 1).astype(F32) < column(fill_ref[...], leaf)) & (slot < count_ref[0])
    for c in range(3):
        out_ref[c] = jnp.where(live, (far[c] + sum_ref[c]) * SCALE, 0.0)
    for copy in sent:
        copy.wait_send()


def frame(seg, c):
    row8 = iota((8, 128), 0)
    spot = (2 * seg + ((c >> 1) & 1), c >> 2, c & 1)
    mx, my, mz = (jnp.where(row8 == a, m.astype(F32) + 0.5, 0.0) for a, m in enumerate(spot))
    return mx + my + mz


def local(rows, middle):
    near = jnp.where(iota((8, 128), 0) < 3, rows - middle, 0.0)
    return near + pltpu.roll(near, 3, 0)


def target_sides(seg, leaf, spot_ref, rec_ref, side_ref):
    row8 = iota((8, 128), 0)
    first, second = row8 < 3, (row8 >= 3) & (row8 < 6)
    none = jnp.zeros((8, 128), F32)
    keep = jnp.where(row8 < 6, 1.0, 0.0)

    def one(t):
        here = local(rec_ref[pl.ds(t * 6, 8), :], frame(seg, spot_ref[t]))
        xh, xm, xl = split3(-2.0 * here)
        length = 0.5 * jnp.sum(here * here, axis=0, keepdims=True) + SMOOTH
        nh, nm, nl = split3(length)
        norm = jnp.where(row8 == 3, nh, jnp.where(row8 == 4, nm, nl))
        cross = jnp.where(first, xh, jnp.where(second, xm, 0.0))
        last = jnp.where(first, xh, jnp.where(second, xl, 0.0))
        tail = jnp.where(first, 1.0, jnp.where(second, norm, 0.0))
        side = jnp.concatenate([cross, cross, last, keep, tail] + [none] * 11, axis=0)
        side_ref[t] = jnp.swapaxes(side, 0, 1).astype(BF16)

    def some(i, carry):
        for u in range(8):
            one(8 * i + u)
        return carry

    lax.fori_loop(0, leaf // 8, some, 0)


def near_field(seg, leaf, slots, near_ref, many_ref, spot_ref, side_ref, box_ref, bufs, cols_ref, near_out_ref):
    count, size = near_ref.shape[0], 128
    start = (seg - 1) * slots
    row8 = iota((8, size), 0)
    first, second = row8 < 3, (row8 >= 3) & (row8 < 6)
    none = jnp.zeros((8, size), F32)
    block = 32

    def pair(t, k0, middle, side, many, buf):
        r2_ref, load_ref = buf
        feats = []
        for k in (k0, k0 + 1):
            rows = box_ref[pl.ds(jnp.clip(near_ref[k, t] - start, 0, 3 * slots - 1) * 6, 8), :]
            y = local(rows, middle)
            yh, ym, yl = split3(y)
            sh, sm, sl = split3(y * y)
            feat = [yh, ym, jnp.where(first, yl, yh), jnp.where(first, sh, sm), jnp.where(first, sl, 1.0), none]
            feats.append(jnp.concatenate(feat, axis=0).astype(BF16))
            load_ref[k] = rows * jnp.clip(many - k, 0, 1).astype(F32)
        r2_ref[:, size * k0 : size * k0 + 2 * size] = bdot(side, jnp.concatenate(feats, axis=1))

    def gather_rows(n, buf):
        r2_ref, load_ref = buf
        at = block * n
        acc = [jnp.zeros((block, size), F32) for _ in range(3)]
        for k in range(count):
            g = lax.rsqrt(r2_ref[at : at + block, size * k : size * k + size])
            for c in range(3):
                acc[c] = acc[c] + g * load_ref[k, 3 + c : 4 + c, :]
        lane = iota((block, size), 1)
        s0, s1, s2 = (jnp.sum(x, axis=1, keepdims=True) for x in acc)
        cols_ref[at : at + block, :] = jnp.where(lane == 0, s0, jnp.where(lane == 1, s1, s2))

    def store(t):
        result = jnp.swapaxes(cols_ref[...], 0, 1)
        for c in range(3):
            near_out_ref[c, pl.ds(t, 1), :] = result[c : c + 1, :]

    def work(t_next, next_buf, t_now, now_buf):
        jobs = list(range(size // block)) if now_buf is not None else []
        steps = count // 2
        if next_buf is not None:
            middle = frame(seg, spot_ref[t_next])
            side = side_ref[t_next, :, 0:48]
            many = many_ref[t_next]
        for p in range(steps):
            if next_buf is not None:
                pair(t_next, 2 * p, middle, side, many, next_buf)
            while jobs and (size // block - len(jobs)) * steps < (p + 1) * (size // block):
                gather_rows(jobs.pop(0), now_buf)
        if now_buf is not None:
            store(t_now)

    def run(turns):
        work(0, bufs[0], None, None)

        def two(i, carry):
            t = 2 * i
            work(t + 1, bufs[1], t, bufs[0])
            work((t + 2) % leaf, bufs[0], t + 1, bufs[1])
            return carry

        lax.fori_loop(0, turns, two, 0)

    return run


def leaf_far(cell_ref, off_ref, loc_ref):
    leaf, size = off_ref.shape[1], off_ref.shape[2]
    par = loc_ref.shape[0] // 3
    cell = column(cell_ref[...], leaf).astype(jnp.int32)
    chosen = jnp.where((cell >> 3) == iota((leaf, par), 1), 1.0, 0.0).astype(BF16)
    child = cell & 7
    lane = iota((leaf, 128), 1)
    expansion = []
    for c in range(3):
        wide = pick_exact(chosen, loc_ref[c * par : (c + 1) * par, :])
        kept = jnp.zeros((leaf, 128), F32)
        for i in range(4):
            kept = kept + jnp.where(lane // 64 + 2 * i == child, wide[:, 128 * i : 128 * i + 128], 0.0)
        expansion.append(kept + pltpu.roll(kept, 64, 1))
    far = [jnp.zeros((leaf, size), F32) for _ in range(3)]

    def visit(a, w):
        for c in range(3):
            far[c] = far[c] + expansion[c][:, a : a + 1] * w

    weights_loop([off_ref[a] for a in range(3)], visit)
    return far


def shape(*dims):
    return jax.ShapeDtypeStruct(dims, F32)


def tree_call(n_seg, n_ex, offsets, strength, cell_row, count, fill_row, near, many, spot):
    n_x, per = n_ex // 2, n_seg // n_ex
    leaf, size = offsets.shape[1], offsets.shape[2]
    par = leaf * n_ex // 8
    dma = pltpu.SemaphoreType.DMA
    return pl.pallas_call(
        lambda *refs: tree_kernel(n_seg, n_x, per, *refs),
        out_shape=shape(3, leaf, size),
        in_specs=[VMEM, VMEM, VMEM, SMEM, VMEM, SMEM, SMEM, SMEM],
        out_specs=VMEM,
        scratch_shapes=[
            pltpu.VMEM((3 * par, 512), F32),
            pltpu.VMEM((leaf * 6 + 8, size), F32),
            pltpu.VMEM((leaf * 2, size), F32),
            pltpu.VMEM((64, 512), F32),
            pltpu.VMEM((3, n_ex, leaf * 2, size), F32),
            pltpu.VMEM((2 * par, 128), F32),
            pltpu.VMEM((per, 2 * par, 128), F32),
            pltpu.VMEM((64, 128), F32),
            pltpu.VMEM((n_ex, 64, 128), F32),
            pltpu.VMEM((6, 3, par + 16, 256), F32),
            pltpu.VMEM((3, 256, 512), F32),
            pltpu.VMEM((2, 256, 512), F32),
            pltpu.VMEM((3, 64, per * 64), F32),
            *near_scratch(18 * n_ex * leaf, near.shape[0], leaf, size),
            dma((14 * n_x + 5,)),
            dma((3, n_ex)),
            dma((3, n_ex)),
            dma((per,)),
            dma((per,)),
            dma((n_ex,)),
            dma,
        ],
        compiler_params=pltpu.CompilerParams(collective_id=0, has_side_effects=True, vmem_limit_bytes=BIG),
    )(offsets, strength, cell_row, count, fill_row, near, many, spot)


def near_scratch(rows, count, leaf, size):
    return [
        pltpu.VMEM((rows + 8, size), F32),
        pltpu.VMEM((size, count * size), F32),
        pltpu.VMEM((size, count * size), F32),
        pltpu.VMEM((count, 8, size), F32),
        pltpu.VMEM((count, 8, size), F32),
        pltpu.VMEM((size, size), F32),
        pltpu.VMEM((3, leaf, size), F32),
        pltpu.VMEM((leaf, size, size), BF16),
    ]


def solution(mesh):
    n_seg, n_ex = mesh.shape["space"], mesh.shape["exp"]

    def body(offsets, strength, leaf_cell, leaf_count, leaf_fill, near_list, near_count):
        leaf, size = offsets.shape[1], offsets.shape[2]
        cell_row = leaf_cell.reshape(1, leaf)
        fill_row = leaf_fill.reshape(1, leaf)
        return tree_call(
            n_seg, n_ex, offsets, strength, cell_row, leaf_count, fill_row, near_list, near_count, leaf_cell
        )

    in_specs = (
        P(None, ("space", "exp"), None),
        P(None, ("space", "exp"), None),
        P(("space", "exp")),
        P("space"),
        P(("space", "exp")),
        P(None, ("space", "exp")),
        P(("space", "exp")),
    )
    out_specs = P(None, ("space", "exp"), None)
    return jax.shard_map(body, mesh=mesh, in_specs=in_specs, out_specs=out_specs, check_vma=False)
```

```python
import math

import jax
import jax.numpy as jnp
from jax import lax
from jax.experimental import pallas as pl
from jax.experimental.pallas import tpu as pltpu
from jax.sharding import PartitionSpec as P

NODES = [math.cos((2 * k + 1) * math.pi / 8) for k in range(4)]
SMOOTH = 0.01
SCALE = 1.0 / (4.0 * math.pi)
F32 = jnp.float32
BF16 = jnp.bfloat16
VMEM = pl.BlockSpec(memory_space=pltpu.VMEM)
SMEM = pl.BlockSpec(memory_space=pltpu.SMEM)
ANY = pl.BlockSpec(memory_space=pl.ANY)
BIG = 60 * 1024 * 1024
NN = (((1,), (0,)), ((), ()))
NT = (((1,), (1,)), ((), ()))


def iota(shape, axis):
    return lax.broadcasted_iota(jnp.int32, shape, axis)


def split2(x):
    hi = x.astype(BF16)
    return hi, (x - hi.astype(F32)).astype(BF16)


def split3(x):
    hi = x.astype(BF16).astype(F32)
    rest = x - hi
    mid = rest.astype(BF16).astype(F32)
    return hi, mid, rest - mid


def bdot(a, b, dims=NN):
    return lax.dot_general(a, b, dims, preferred_element_type=F32)


def dot3(a, b, dims=NN):
    ah, al = a if isinstance(a, tuple) else split2(a)
    bh, bl = b if isinstance(b, tuple) else split2(b)
    return bdot(ah, bh, dims) + (bdot(al, bh, dims) + bdot(ah, bl, dims))


def pick_exact(one_hot, x):
    hi = x.astype(BF16)
    rest = x - hi.astype(F32)
    mid = rest.astype(BF16)
    low = (rest - mid.astype(F32)).astype(BF16)
    return bdot(one_hot, hi) + (bdot(one_hot, mid) + bdot(one_hot, low))


def node(k):
    return jnp.where(
        k == 0, NODES[0], jnp.where(k == 1, NODES[1], jnp.where(k == 2, NODES[2], NODES[3]))
    ).astype(F32)


def cheb(u):
    return u, 2.0 * u * u - 1.0, (4.0 * u * u - 3.0) * u


def factors(u):
    t1, t2, t3 = cheb(u)
    out = []
    for t in NODES:
        out.append(0.25 + t1 * (0.5 * t) + t2 * (0.5 * (2 * t * t - 1)) + t3 * (0.5 * (4 * t**3 - 3 * t)))
    return out


def cheb_pair(u, t):
    u1, u2, u3 = cheb(u)
    t1, t2, t3 = cheb(t)
    return 0.25 + 0.5 * (u1 * t1 + u2 * t2 + u3 * t3)


def column(row, count):
    spread = jnp.where(iota((count, count), 0) == iota((count, count), 1), row.astype(F32), 0.0)
    return jnp.sum(spread, axis=1, keepdims=True)


def weights_loop(offs, visit):
    fx, fy, fz = (factors(o) for o in offs)
    for i in range(4):
        for j in range(4):
            fxy = fx[i] * fy[j]
            for k in range(4):
                visit(16 * i + 4 * j + k, fxy * fz[k])


def particles(seg, ex, off_ref, str_ref, cell_ref, count_ref, fill_ref, rec_ref, mul_ref):
    leaf, size = off_ref.shape[1], off_ref.shape[2]
    cell_f = column(cell_ref[...], leaf)
    fill = column(fill_ref[...], leaf)
    cell = cell_f.astype(jnp.int32)
    slot = ex * leaf + iota((leaf, size), 0)
    alive = (slot < count_ref[0]) & (iota((leaf, size), 1).astype(F32) < fill)
    centre = (
        2 * seg + ((cell >> 1) & 1),
        cell >> 2,
        cell & 1,
    )
    offs = [off_ref[a] for a in range(3)]
    charge = []
    for a in range(3):
        pos = (centre[a].astype(F32) + 0.5) + 0.5 * offs[a]
        rec_ref[pl.ds(a, leaf, 6), :] = pos
        q = jnp.where(alive, str_ref[a], 0.0)
        rec_ref[pl.ds(3 + a, leaf, 6), :] = q
        charge.append(q)
    lane = iota((leaf, size), 1)
    acc = [jnp.zeros((leaf, size), F32), jnp.where(lane >= 64, cell_f, 0.0)]

    def visit(a, w):
        for c in range(3):
            total = jnp.sum(charge[c] * w, axis=1, keepdims=True)
            at = a + 64 * (c % 2)
            acc[c // 2] = jnp.where(lane == at, total, acc[c // 2])

    weights_loop(offs, visit)
    mul_ref[0:leaf, :] = acc[0]
    mul_ref[leaf : 2 * leaf, :] = acc[1]


def mesh_at(seg, ex):
    return {"space": seg, "exp": ex}


def remote(src, dst, send, recv, seg, ex):
    return pltpu.make_async_remote_copy(
        src_ref=src, dst_ref=dst, send_sem=send, recv_sem=recv,
        device_id=mesh_at(seg, ex), device_id_type=pl.DeviceIdType.MESH,
    )


def sorted_block(mul_ref, part, guard):
    n_ex, leaf = mul_ref.shape[1], mul_ref.shape[2] // 2
    slots = n_ex * leaf
    par = slots // 8
    m01 = mul_ref[part, :, 0:leaf, :].reshape(slots, 128)
    m2c = mul_ref[part, :, leaf : 2 * leaf, :].reshape(slots, 128)
    cells = jnp.swapaxes(m2c, 0, 1)[64:65, :]
    row = iota((slots, slots), 0)
    wanted = ((row % par) * 8 + row // par).astype(F32)
    one_hot = jnp.where((wanted == cells) & guard, 1.0, 0.0).astype(BF16)
    return pick_exact(one_hot, m01), pick_exact(one_hot, m2c)


def parent_moments(g01, g2):
    par = g01.shape[0] // 8
    total = jnp.zeros((2 * par, 128), F32)
    lane_b = iota((128, 128), 1)
    row_a = iota((128, 128), 0)
    bx, by, bz = (node((lane_b // w) % 4) for w in (16, 4, 1))
    ax, ay, az = (node((row_a // w) % 4) for w in (16, 4, 1))
    sx, sy, sz = ([cheb_pair(bit - 0.5 + 0.5 * a, b) for bit in (0, 1)] for a, b in ((ax, bx), (ay, by), (az, bz)))
    same = (lane_b // 64) == (row_a // 64)
    for h in range(8):
        table = jnp.where(same, sx[(h // 2) % 2] * sy[h // 4] * sz[h % 2], 0.0)
        lhs = jnp.concatenate([g01[h * par : (h + 1) * par], g2[h * par : (h + 1) * par]], axis=0)
        total = total + dot3(lhs, table)
    return total


def store_rows(grid_ref, j, g01, g2):
    par = g01.shape[0] // 8
    for odd in range(2):
        for c in range(3):
            src = g01 if c < 2 else g2
            lo = 64 * (c % 2)
            grid_ref[j * 2 + odd, c, 8 : 8 + par, :] = jnp.concatenate(
                [src[(4 * odd + r) * par : (4 * odd + r + 1) * par, lo : lo + 64] for r in range(4)], axis=1
            )


def m2l_tables(base_ref, near_x_ref):
    lane, row = iota((256, 512), 1), iota((256, 512), 0)
    ux = ((lane // 128) % 2).astype(F32) + 0.5 * node((lane // 16) % 4)
    vx = (row // 128).astype(F32) + 0.5 * node((row // 16) % 4)
    uz = ((lane // 64) % 2).astype(F32) + 0.5 * node(lane % 4)
    vz = ((row // 64) % 2).astype(F32) + 0.5 * node(row % 4)
    base_ref[1] = (uz - vz) * (uz - vz) + SMOOTH
    base_ref[2] = ux - vx
    near_x_ref[1] = ((row // 128) - (lane // 128) % 2).astype(F32)


def m2l_segment(j, par, grid_ref, base_ref, near_x_ref, loc_ref):
    lane1 = iota((1, 512), 1)
    up1 = (lane1 // 256).astype(F32)
    uy = up1 + 0.5 * node((lane1 // 4) % 4)
    vy = 0.5 * node((iota((256, 1), 0) // 4) % 4)
    shift = 2.0 * jnp.asarray(j, jnp.int32).astype(F32) - 2.0
    dx = base_ref[2] - shift
    base_ref[0] = dx * dx + base_ref[1]
    near_x_ref[0] = jnp.where(jnp.abs(near_x_ref[1] + shift) < 1.5, jnp.inf, 0.0)
    for odd in range(2):
        for i in range(3):
            height = 2 * i + odd - 2
            lhs = jnp.concatenate([grid_ref[j * 2 + odd, c, 7 + i : 7 + i + par, :] for c in range(3)], axis=0)
            near_y = jnp.where(jnp.abs(height - up1) < 1.5, jnp.inf, 0.0)
            dy = (uy - height) - vy
            g = lax.rsqrt(dy * dy + base_ref[0] + jnp.minimum(near_x_ref[0], near_y))
            loc_ref[...] += dot3(lhs, g)


def far_tables(seg, ex, per, far_ref):
    wide = per * 64
    lane, row = iota((64, wide), 1), iota((64, wide), 0)
    step = (seg - ex * per - lane // 64).astype(F32)
    dx = 2.0 * step + node(row // 16) - node((lane // 16) % 4)
    dz = node(row % 4) - node(lane % 4)
    far_ref[0] = dx * dx + (dz * dz + SMOOTH)
    far_ref[1] = node((row // 4) % 4) - node((lane // 4) % 4)
    far_ref[2] = jnp.where(jnp.abs(step) < 1.5, jnp.inf, 0.0)


def far_sum(pq_ref, far_ref):
    per = pq_ref.shape[0]
    par = pq_ref.shape[1] // 2
    wide = per * 64
    turn = 7 if (2 * par - 1) % 7 == 0 else 1
    rows = []
    for c in range(3):
        r0, l0 = par * (c // 2), 64 * (c % 2)
        rows.append(jnp.concatenate([pq_ref[q, r0 : r0 + par, l0 : l0 + 64] for q in range(per)], axis=1))
    rows.append(jnp.zeros((128 - 3 * par, wide), F32))
    ph, plo = split2(jnp.swapaxes(jnp.concatenate(rows, axis=0), 0, 1))
    p_to = iota((64, 128), 1) % par

    def some(i, acc):
        high, low = [], []
        for u in range(turn):
            delta = i * turn + u - (par - 1)
            dy = far_ref[1] + 2.0 * delta.astype(F32)
            gap = jnp.where(jnp.abs(delta) <= 1, jnp.inf, 0.0)
            gh, gl = split2(lax.rsqrt(dy * dy + far_ref[0] + jnp.minimum(far_ref[2], gap)))
            high.append(gh)
            low.append(gl)
        gh = jnp.concatenate(high, axis=0)
        got = bdot(gh, ph) + (bdot(jnp.concatenate(low, axis=0), ph) + bdot(gh, plo))
        for u in range(turn):
            delta = i * turn + u - (par - 1)
            moved = pltpu.roll(got[64 * u : 64 * u + 64], (delta + 128) % 128, 1)
            source = p_to - delta
            acc = acc + jnp.where((source >= 0) & (source < par), moved, 0.0)
        return acc

    return lax.fori_loop(0, (2 * par - 1) // turn, some, jnp.zeros((64, 128), F32))


def child_table(table_ref):
    lane, row = iota((64, 512), 1), iota((64, 512), 0)
    table = 1.0
    for bit, w in (((lane // 128) % 2, 16), (lane // 256, 4), ((lane // 64) % 2, 1)):
        table = table * cheb_pair(bit.astype(F32) - 0.5 + 0.5 * node((lane // w) % 4), node((row // w) % 4))
    table_ref[...] = table


def tree_kernel(
    n_seg, n_x, per, off_ref, str_ref, cell_ref, count_ref, fill_ref, near_ref, many_ref, spot_ref, out_ref,
    loc_ref, rec_ref, mul_ref, table_ref, mwin_ref, pm_ref, pq_ref, part_ref, share_ref, grid_ref, base_ref,
    near_x_ref, far_ref, box_ref, r2a_ref, r2b_ref, load_a_ref, load_b_ref, cols_ref, sum_ref, side_ref,
    send, mrecv, precv, swap_send, swap_recv, share_recv, own_sem,
):
    n_ex = 2 * n_x
    seg, ex = lax.axis_index("space"), lax.axis_index("exp")
    x, core = ex // 2, ex % 2
    prev, after = (seg + n_seg - 1) % n_seg, (seg + 1) % n_seg
    ring = [((x + d) % n_x) * 2 + core for d in range(n_x)]
    mates = [((x + d) % n_x) * 2 + 1 - core for d in range(n_x)]
    order = [1, n_x - 1] + list(range(2, n_x - 1))
    mate = mates[0]
    others = [ring[d] for d in order] + [mates[d] for d in [0] + order]
    there = seg // per
    mine = ex == there
    par = mul_ref.shape[0] // 2 * n_ex // 8
    leaf, size = off_ref.shape[1], off_ref.shape[2]
    own_rec = rec_ref.at[0 : leaf * 6]
    barrier = pltpu.get_barrier_semaphore()
    sent = []

    def box(part, who):
        return box_ref.at[pl.ds(pl.multiple_of((part * n_ex + who) * (leaf * 6), 8), leaf * 6)]

    def hello(to_seg, to_ex):
        pl.semaphore_signal(barrier, 1, device_id=mesh_at(to_seg, to_ex), device_id_type=pl.DeviceIdType.MESH)

    def not_self(i):
        return jnp.logical_not(mine & (seg % per == i))

    for o in others:
        hello(seg, o)
    hello(prev, ex)
    hello(after, ex)
    for i in range(per):

        @pl.when(not_self(i))
        def _():
            hello(ex * per + i, there)

    particles(seg, ex, off_ref, str_ref, cell_ref, count_ref, fill_ref, rec_ref, mul_ref)
    far_tables(seg, ex, per, far_ref)
    rec_ref[leaf * 6 :, :] = jnp.zeros((8, size), F32)
    box_ref[18 * n_ex * leaf :, :] = jnp.zeros((8, size), F32)
    pl.semaphore_wait(barrier, len(others) + 2 + jnp.where(mine, per - 1, per))

    def push(src, dst, recv, to_seg, to_ex):
        copy = remote(src, dst, send.at[len(sent)], recv, to_seg, to_ex)
        copy.start()
        sent.append(copy)

    def push_m(src, part, who, to_seg, to_ex):
        push(src, mwin_ref.at[part, who], mrecv.at[part, who], to_seg, to_ex)

    def push_p(src, part, who, to_seg, to_ex):
        push(src, box(part, who), precv.at[part, who], to_seg, to_ex)

    def got_m(part, who):
        remote(mul_ref, mwin_ref.at[part, who], send.at[0], mrecv.at[part, who], seg, mate).wait_recv()

    def got_p(part, who):
        remote(own_rec, box(part, who), send.at[0], precv.at[part, who], seg, mate).wait_recv()

    push_p(own_rec, 0, ex, after, ex)
    push_p(own_rec, 2, ex, prev, ex)
    for o in others:
        push_m(mul_ref, 1, ex, seg, o)
    push_m(mul_ref, 0, ex, after, ex)
    push_m(mul_ref, 2, ex, prev, ex)
    for d in order:
        push_p(own_rec, 1, ex, seg, ring[d])
    push_p(own_rec, 1, ex, seg, mate)
    keep = pltpu.make_async_copy(own_rec, box(1, ex), own_sem)
    keep.start()
    mwin_ref[1, ex] = mul_ref[...]
    grid_ref[...] = jnp.zeros(grid_ref.shape, F32)
    loc_ref[...] = jnp.zeros(loc_ref.shape, F32)
    m2l_tables(base_ref, near_x_ref)
    child_table(table_ref)
    target_sides(seg, leaf, spot_ref, rec_ref, side_ref)
    for d in order:
        got_m(1, ring[d])
        push_m(mwin_ref.at[1, ring[d]], 0, ring[d], after, ex)
        push_m(mwin_ref.at[1, ring[d]], 2, ring[d], prev, ex)
    for d in range(n_x):
        got_m(1, mates[d])
    g01, g2 = sorted_block(mwin_ref, 1, True)
    pm_ref[...] = parent_moments(g01, g2)
    store_rows(grid_ref, 1, g01, g2)

    def pass_on(d):
        got_p(1, ring[d])
        push_p(box(1, ring[d]), 0, ring[d], after, ex)
        push_p(box(1, ring[d]), 2, ring[d], prev, ex)
        push_p(box(1, ring[d]), 1, ring[d], seg, mate)

    def swap(i):
        return remote(pm_ref, pq_ref.at[seg % per], swap_send.at[i], swap_recv.at[seg % per], ex * per + i, there)

    for i in range(per):

        @pl.when(not_self(i))
        def _():
            swap(i).start()

    @pl.when(mine)
    def _():
        pq_ref[seg % per] = pm_ref[...]

    for d in order:
        pass_on(d)
    m2l_segment(1, par, grid_ref, base_ref, near_x_ref, loc_ref)
    for d in [0] + order:
        for part in (0, 2):
            got_m(part, ring[d])
            push_m(mwin_ref.at[part, ring[d]], part, ring[d], seg, mate)

    def pass_mate(d):
        for part in (0, 2):
            got_p(part, ring[d])
            push_p(box(part, ring[d]), part, ring[d], seg, mate)

    pass_mate(0)
    for d in range(n_x):
        for part in (0, 2):
            got_m(part, mates[d])
    for part, guard in ((0, seg > 0), (2, seg < n_seg - 1)):
        g01, g2 = sorted_block(mwin_ref, part, guard)
        store_rows(grid_ref, part, g01, g2)

    def sides(i, carry):
        m2l_segment(2 * i, par, grid_ref, base_ref, near_x_ref, loc_ref)
        return carry

    lax.fori_loop(0, 2, sides, 0)
    for d in order:
        pass_mate(d)
    for d in range(n_x):
        for part in range(3):
            got_p(part, mates[d])
    keep.wait()
    bufs = ((r2a_ref, load_a_ref), (r2b_ref, load_b_ref))
    near = near_field(
        seg, leaf, n_ex * leaf, near_ref, many_ref, spot_ref, side_ref, box_ref, bufs, cols_ref, sum_ref
    )
    near(0, leaf // 4)
    for i in range(per):

        @pl.when(not_self(i))
        def _():
            remote(pm_ref, pq_ref.at[i], swap_send.at[i], swap_recv.at[i], ex * per + i, there).wait_recv()
            swap(i).wait_send()

    part_ref[...] = far_sum(pq_ref, far_ref)
    share_ref[ex] = part_ref[...]
    for o in others:
        push(part_ref, share_ref.at[ex], share_recv.at[ex], seg, o)
    near(leaf // 4, leaf // 2)
    for o in others:
        remote(part_ref, share_ref.at[o], send.at[0], share_recv.at[o], seg, o).wait_recv()
    parent = share_ref[0]
    for i in range(1, n_ex):
        parent = parent + share_ref[i]
    loc_ref[...] += dot3(jnp.swapaxes(parent, 0, 1)[: 3 * par, :], table_ref[...])
    far = leaf_far(cell_ref, off_ref, loc_ref)
    slot = ex * leaf + iota((leaf, size), 0)
    live = (iota((leaf, size), 1).astype(F32) < column(fill_ref[...], leaf)) & (slot < count_ref[0])
    for c in range(3):
        out_ref[c] = jnp.where(live, (far[c] + sum_ref[c]) * SCALE, 0.0)
    for copy in sent:
        copy.wait_send()


def frame(seg, c):
    row8 = iota((8, 128), 0)
    spot = (2 * seg + ((c >> 1) & 1), c >> 2, c & 1)
    mx, my, mz = (jnp.where(row8 == a, m.astype(F32) + 0.5, 0.0) for a, m in enumerate(spot))
    return mx + my + mz


def local(rows, middle):
    near = jnp.where(iota((8, 128), 0) < 3, rows - middle, 0.0)
    return near + pltpu.roll(near, 3, 0)


def target_sides(seg, leaf, spot_ref, rec_ref, side_ref):
    row8 = iota((8, 128), 0)
    first, second = row8 < 3, (row8 >= 3) & (row8 < 6)
    none = jnp.zeros((8, 128), F32)
    keep = jnp.where(row8 < 6, 1.0, 0.0)

    def one(t):
        here = local(rec_ref[pl.ds(t * 6, 8), :], frame(seg, spot_ref[t]))
        xh, xm, xl = split3(-2.0 * here)
        length = 0.5 * jnp.sum(here * here, axis=0, keepdims=True) + SMOOTH
        nh, nm, nl = split3(length)
        norm = jnp.where(row8 == 3, nh, jnp.where(row8 == 4, nm, nl))
        cross = jnp.where(first, xh, jnp.where(second, xm, 0.0))
        last = jnp.where(first, xh, jnp.where(second, xl, 0.0))
        tail = jnp.where(first, 1.0, jnp.where(second, norm, 0.0))
        side = jnp.concatenate([cross, cross, last, keep, tail] + [none] * 11, axis=0)
        side_ref[t] = jnp.swapaxes(side, 0, 1).astype(BF16)

    def some(i, carry):
        for u in range(8):
            one(8 * i + u)
        return carry

    lax.fori_loop(0, leaf // 8, some, 0)


def near_field(seg, leaf, slots, near_ref, many_ref, spot_ref, side_ref, box_ref, bufs, cols_ref, near_out_ref):
    count, size = near_ref.shape[0], 128
    start = (seg - 1) * slots
    row8 = iota((8, size), 0)
    first, second = row8 < 3, (row8 >= 3) & (row8 < 6)
    none = jnp.zeros((8, size), F32)
    block = 32

    def pair(t, k0, middle, side, many, buf):
        r2_ref, load_ref = buf
        feats = []
        for k in (k0, k0 + 1):
            rows = box_ref[pl.ds(jnp.clip(near_ref[k, t] - start, 0, 3 * slots - 1) * 6, 8), :]
            y = local(rows, middle)
            yh, ym, yl = split3(y)
            sh, sm, sl = split3(y * y)
            feat = [yh, ym, jnp.where(first, yl, yh), jnp.where(first, sh, sm), jnp.where(first, sl, 1.0), none]
            feats.append(jnp.concatenate(feat, axis=0).astype(BF16))
            load_ref[k] = rows * jnp.clip(many - k, 0, 1).astype(F32)
        r2_ref[:, size * k0 : size * k0 + 2 * size] = bdot(side, jnp.concatenate(feats, axis=1))

    def gather_rows(n, buf):
        r2_ref, load_ref = buf
        at = block * n
        acc = [jnp.zeros((block, size), F32) for _ in range(3)]
        for k in range(count):
            g = lax.rsqrt(r2_ref[at : at + block, size * k : size * k + size])
            for c in range(3):
                acc[c] = acc[c] + g * load_ref[k, 3 + c : 4 + c, :]
        lane = iota((block, size), 1)
        s0, s1, s2 = (jnp.sum(x, axis=1, keepdims=True) for x in acc)
        cols_ref[at : at + block, :] = jnp.where(lane == 0, s0, jnp.where(lane == 1, s1, s2))

    def store(t):
        result = jnp.swapaxes(cols_ref[...], 0, 1)
        for c in range(3):
            near_out_ref[c, pl.ds(t, 1), :] = result[c : c + 1, :]

    def work(t_next, next_buf, t_now, now_buf):
        jobs = list(range(size // block)) if now_buf is not None else []
        steps = count // 2
        if next_buf is not None:
            middle = frame(seg, spot_ref[t_next])
            side = side_ref[t_next, :, 0:48]
            many = many_ref[t_next]
        for p in range(steps):
            if next_buf is not None:
                pair(t_next, 2 * p, middle, side, many, next_buf)
            while jobs and (size // block - len(jobs)) * steps < (p + 1) * (size // block):
                gather_rows(jobs.pop(0), now_buf)
        if now_buf is not None:
            store(t_now)

    def run(low, high):
        if low == 0:
            work(0, bufs[0], None, None)

        def two(i, carry):
            t = 2 * i
            work(t + 1, bufs[1], t, bufs[0])
            work((t + 2) % leaf, bufs[0], t + 1, bufs[1])
            return carry

        lax.fori_loop(low, high, two, 0)

    return run


def leaf_far(cell_ref, off_ref, loc_ref):
    leaf, size = off_ref.shape[1], off_ref.shape[2]
    par = loc_ref.shape[0] // 3
    cell = column(cell_ref[...], leaf).astype(jnp.int32)
    chosen = jnp.where((cell >> 3) == iota((leaf, par), 1), 1.0, 0.0).astype(BF16)
    child = cell & 7
    lane = iota((leaf, 128), 1)
    expansion = []
    for c in range(3):
        wide = pick_exact(chosen, loc_ref[c * par : (c + 1) * par, :])
        kept = jnp.zeros((leaf, 128), F32)
        for i in range(4):
            kept = kept + jnp.where(lane // 64 + 2 * i == child, wide[:, 128 * i : 128 * i + 128], 0.0)
        expansion.append(kept + pltpu.roll(kept, 64, 1))
    far = [jnp.zeros((leaf, size), F32) for _ in range(3)]

    def visit(a, w):
        for c in range(3):
            far[c] = far[c] + expansion[c][:, a : a + 1] * w

    weights_loop([off_ref[a] for a in range(3)], visit)
    return far


def shape(*dims):
    return jax.ShapeDtypeStruct(dims, F32)


def tree_call(n_seg, n_ex, offsets, strength, cell_row, count, fill_row, near, many, spot):
    n_x, per = n_ex // 2, n_seg // n_ex
    leaf, size = offsets.shape[1], offsets.shape[2]
    par = leaf * n_ex // 8
    dma = pltpu.SemaphoreType.DMA
    return pl.pallas_call(
        lambda *refs: tree_kernel(n_seg, n_x, per, *refs),
        out_shape=shape(3, leaf, size),
        in_specs=[VMEM, VMEM, VMEM, SMEM, VMEM, SMEM, SMEM, SMEM],
        out_specs=VMEM,
        scratch_shapes=[
            pltpu.VMEM((3 * par, 512), F32),
            pltpu.VMEM((leaf * 6 + 8, size), F32),
            pltpu.VMEM((leaf * 2, size), F32),
            pltpu.VMEM((64, 512), F32),
            pltpu.VMEM((3, n_ex, leaf * 2, size), F32),
            pltpu.VMEM((2 * par, 128), F32),
            pltpu.VMEM((per, 2 * par, 128), F32),
            pltpu.VMEM((64, 128), F32),
            pltpu.VMEM((n_ex, 64, 128), F32),
            pltpu.VMEM((6, 3, par + 16, 256), F32),
            pltpu.VMEM((3, 256, 512), F32),
            pltpu.VMEM((2, 256, 512), F32),
            pltpu.VMEM((3, 64, per * 64), F32),
            *near_scratch(18 * n_ex * leaf, near.shape[0], leaf, size),
            dma((14 * n_x + 5,)),
            dma((3, n_ex)),
            dma((3, n_ex)),
            dma((per,)),
            dma((per,)),
            dma((n_ex,)),
            dma,
        ],
        compiler_params=pltpu.CompilerParams(collective_id=0, has_side_effects=True, vmem_limit_bytes=BIG),
    )(offsets, strength, cell_row, count, fill_row, near, many, spot)


def near_scratch(rows, count, leaf, size):
    return [
        pltpu.VMEM((rows + 8, size), F32),
        pltpu.VMEM((size, count * size), F32),
        pltpu.VMEM((size, count * size), F32),
        pltpu.VMEM((count, 8, size), F32),
        pltpu.VMEM((count, 8, size), F32),
        pltpu.VMEM((size, size), F32),
        pltpu.VMEM((3, leaf, size), F32),
        pltpu.VMEM((leaf, size, size), BF16),
    ]


def solution(mesh):
    n_seg, n_ex = mesh.shape["space"], mesh.shape["exp"]

    def body(offsets, strength, leaf_cell, leaf_count, leaf_fill, near_list, near_count):
        leaf, size = offsets.shape[1], offsets.shape[2]
        cell_row = leaf_cell.reshape(1, leaf)
        fill_row = leaf_fill.reshape(1, leaf)
        return tree_call(
            n_seg, n_ex, offsets, strength, cell_row, leaf_count, fill_row, near_list, near_count, leaf_cell
        )

    in_specs = (
        P(None, ("space", "exp"), None),
        P(None, ("space", "exp"), None),
        P(("space", "exp")),
        P("space"),
        P(("space", "exp")),
        P(None, ("space", "exp")),
        P(("space", "exp")),
    )
    out_specs = P(None, ("space", "exp"), None)
    return jax.shard_map(body, mesh=mesh, in_specs=in_specs, out_specs=out_specs, check_vma=False)
```

```python
import math

import jax
import jax.numpy as jnp
from jax import lax
from jax.experimental import pallas as pl
from jax.experimental.pallas import tpu as pltpu
from jax.sharding import PartitionSpec as P

NODES = [math.cos((2 * k + 1) * math.pi / 8) for k in range(4)]
SMOOTH = 0.01
SCALE = 1.0 / (4.0 * math.pi)
F32 = jnp.float32
BF16 = jnp.bfloat16
VMEM = pl.BlockSpec(memory_space=pltpu.VMEM)
SMEM = pl.BlockSpec(memory_space=pltpu.SMEM)
ANY = pl.BlockSpec(memory_space=pl.ANY)
BIG = 60 * 1024 * 1024
NN = (((1,), (0,)), ((), ()))
NT = (((1,), (1,)), ((), ()))


def iota(shape, axis):
    return lax.broadcasted_iota(jnp.int32, shape, axis)


def split2(x):
    hi = x.astype(BF16)
    return hi, (x - hi.astype(F32)).astype(BF16)


def split3(x):
    hi = x.astype(BF16).astype(F32)
    rest = x - hi
    mid = rest.astype(BF16).astype(F32)
    return hi, mid, rest - mid


def bdot(a, b, dims=NN):
    return lax.dot_general(a, b, dims, preferred_element_type=F32)


def dot3(a, b, dims=NN):
    ah, al = a if isinstance(a, tuple) else split2(a)
    bh, bl = b if isinstance(b, tuple) else split2(b)
    return bdot(ah, bh, dims) + (bdot(al, bh, dims) + bdot(ah, bl, dims))


def pick_exact(one_hot, x):
    hi = x.astype(BF16)
    rest = x - hi.astype(F32)
    mid = rest.astype(BF16)
    low = (rest - mid.astype(F32)).astype(BF16)
    return bdot(one_hot, hi) + (bdot(one_hot, mid) + bdot(one_hot, low))


def node(k):
    return jnp.where(
        k == 0, NODES[0], jnp.where(k == 1, NODES[1], jnp.where(k == 2, NODES[2], NODES[3]))
    ).astype(F32)


def cheb(u):
    return u, 2.0 * u * u - 1.0, (4.0 * u * u - 3.0) * u


def factors(u):
    t1, t2, t3 = cheb(u)
    out = []
    for t in NODES:
        out.append(0.25 + t1 * (0.5 * t) + t2 * (0.5 * (2 * t * t - 1)) + t3 * (0.5 * (4 * t**3 - 3 * t)))
    return out


def cheb_pair(u, t):
    u1, u2, u3 = cheb(u)
    t1, t2, t3 = cheb(t)
    return 0.25 + 0.5 * (u1 * t1 + u2 * t2 + u3 * t3)


def column(row, count):
    spread = jnp.where(iota((count, count), 0) == iota((count, count), 1), row.astype(F32), 0.0)
    return jnp.sum(spread, axis=1, keepdims=True)


def weights_loop(offs, visit):
    fx, fy, fz = (factors(o) for o in offs)
    for i in range(4):
        for j in range(4):
            fxy = fx[i] * fy[j]
            for k in range(4):
                visit(16 * i + 4 * j + k, fxy * fz[k])


def particles(seg, ex, off_ref, str_ref, cell_ref, count_ref, fill_ref, rec_ref, mul_ref):
    leaf, size = off_ref.shape[1], off_ref.shape[2]
    cell_f = column(cell_ref[...], leaf)
    fill = column(fill_ref[...], leaf)
    cell = cell_f.astype(jnp.int32)
    slot = ex * leaf + iota((leaf, size), 0)
    alive = (slot < count_ref[0]) & (iota((leaf, size), 1).astype(F32) < fill)
    centre = (
        2 * seg + ((cell >> 1) & 1),
        cell >> 2,
        cell & 1,
    )
    offs = [off_ref[a] for a in range(3)]
    charge = []
    for a in range(3):
        pos = (centre[a].astype(F32) + 0.5) + 0.5 * offs[a]
        rec_ref[pl.ds(a, leaf, 6), :] = pos
        q = jnp.where(alive, str_ref[a], 0.0)
        rec_ref[pl.ds(3 + a, leaf, 6), :] = q
        charge.append(q)
    lane = iota((leaf, size), 1)
    acc = [jnp.zeros((leaf, size), F32), jnp.where(lane >= 64, cell_f, 0.0)]

    def visit(a, w):
        for c in range(3):
            total = jnp.sum(charge[c] * w, axis=1, keepdims=True)
            at = a + 64 * (c % 2)
            acc[c // 2] = jnp.where(lane == at, total, acc[c // 2])

    weights_loop(offs, visit)
    mul_ref[0:leaf, :] = acc[0]
    mul_ref[leaf : 2 * leaf, :] = acc[1]


def mesh_at(seg, ex):
    return {"space": seg, "exp": ex}


def remote(src, dst, send, recv, seg, ex):
    return pltpu.make_async_remote_copy(
        src_ref=src, dst_ref=dst, send_sem=send, recv_sem=recv,
        device_id=mesh_at(seg, ex), device_id_type=pl.DeviceIdType.MESH,
    )


def sorted_block(mul_ref, part, guard):
    n_ex, leaf = mul_ref.shape[1], mul_ref.shape[2] // 2
    slots = n_ex * leaf
    par = slots // 8
    m01 = mul_ref[part, :, 0:leaf, :].reshape(slots, 128)
    m2c = mul_ref[part, :, leaf : 2 * leaf, :].reshape(slots, 128)
    cells = jnp.swapaxes(m2c, 0, 1)[64:65, :]
    row = iota((slots, slots), 0)
    wanted = ((row % par) * 8 + row // par).astype(F32)
    one_hot = jnp.where((wanted == cells) & guard, 1.0, 0.0).astype(BF16)
    return pick_exact(one_hot, m01), pick_exact(one_hot, m2c)


def parent_moments(g01, g2):
    par = g01.shape[0] // 8
    total = jnp.zeros((2 * par, 128), F32)
    lane_b = iota((128, 128), 1)
    row_a = iota((128, 128), 0)
    bx, by, bz = (node((lane_b // w) % 4) for w in (16, 4, 1))
    ax, ay, az = (node((row_a // w) % 4) for w in (16, 4, 1))
    sx, sy, sz = ([cheb_pair(bit - 0.5 + 0.5 * a, b) for bit in (0, 1)] for a, b in ((ax, bx), (ay, by), (az, bz)))
    same = (lane_b // 64) == (row_a // 64)
    for h in range(8):
        table = jnp.where(same, sx[(h // 2) % 2] * sy[h // 4] * sz[h % 2], 0.0)
        lhs = jnp.concatenate([g01[h * par : (h + 1) * par], g2[h * par : (h + 1) * par]], axis=0)
        total = total + dot3(lhs, table)
    return total


def store_rows(grid_ref, j, g01, g2):
    par = g01.shape[0] // 8
    for odd in range(2):
        for c in range(3):
            src = g01 if c < 2 else g2
            lo = 64 * (c % 2)
            grid_ref[j * 2 + odd, c, 8 : 8 + par, :] = jnp.concatenate(
                [src[(4 * odd + r) * par : (4 * odd + r + 1) * par, lo : lo + 64] for r in range(4)], axis=1
            )


def m2l_tables(base_ref, near_x_ref):
    lane, row = iota((256, 512), 1), iota((256, 512), 0)
    ux = ((lane // 128) % 2).astype(F32) + 0.5 * node((lane // 16) % 4)
    vx = (row // 128).astype(F32) + 0.5 * node((row // 16) % 4)
    uz = ((lane // 64) % 2).astype(F32) + 0.5 * node(lane % 4)
    vz = ((row // 64) % 2).astype(F32) + 0.5 * node(row % 4)
    base_ref[1] = (uz - vz) * (uz - vz) + SMOOTH
    base_ref[2] = ux - vx
    near_x_ref[1] = ((row // 128) - (lane // 128) % 2).astype(F32)


def m2l_segment(j, par, grid_ref, base_ref, near_x_ref, loc_ref):
    lane1 = iota((1, 512), 1)
    up1 = (lane1 // 256).astype(F32)
    uy = up1 + 0.5 * node((lane1 // 4) % 4)
    vy = 0.5 * node((iota((256, 1), 0) // 4) % 4)
    shift = 2.0 * jnp.asarray(j, jnp.int32).astype(F32) - 2.0
    dx = base_ref[2] - shift
    base_ref[0] = dx * dx + base_ref[1]
    near_x_ref[0] = jnp.where(jnp.abs(near_x_ref[1] + shift) < 1.5, jnp.inf, 0.0)
    for odd in range(2):
        for i in range(3):
            height = 2 * i + odd - 2
            lhs = jnp.concatenate([grid_ref[j * 2 + odd, c, 7 + i : 7 + i + par, :] for c in range(3)], axis=0)
            near_y = jnp.where(jnp.abs(height - up1) < 1.5, jnp.inf, 0.0)
            dy = (uy - height) - vy
            g = lax.rsqrt(dy * dy + base_ref[0] + jnp.minimum(near_x_ref[0], near_y))
            loc_ref[...] += dot3(lhs, g)


def far_tables(seg, ex, per, far_ref):
    wide = per * 64
    lane, row = iota((64, wide), 1), iota((64, wide), 0)
    step = (seg - ex * per - lane // 64).astype(F32)
    dx = 2.0 * step + node(row // 16) - node((lane // 16) % 4)
    dz = node(row % 4) - node(lane % 4)
    far_ref[0] = dx * dx + (dz * dz + SMOOTH)
    far_ref[1] = node((row // 4) % 4) - node((lane // 4) % 4)
    far_ref[2] = jnp.where(jnp.abs(step) < 1.5, jnp.inf, 0.0)


def far_sum(pq_ref, far_ref):
    per = pq_ref.shape[0]
    par = pq_ref.shape[1] // 2
    wide = per * 64
    turn = 7 if (2 * par - 1) % 7 == 0 else 1
    rows = []
    for c in range(3):
        r0, l0 = par * (c // 2), 64 * (c % 2)
        rows.append(jnp.concatenate([pq_ref[q, r0 : r0 + par, l0 : l0 + 64] for q in range(per)], axis=1))
    rows.append(jnp.zeros((128 - 3 * par, wide), F32))
    ph, plo = split2(jnp.swapaxes(jnp.concatenate(rows, axis=0), 0, 1))
    p_to = iota((64, 128), 1) % par

    def some(i, acc):
        high, low = [], []
        for u in range(turn):
            delta = i * turn + u - (par - 1)
            dy = far_ref[1] + 2.0 * delta.astype(F32)
            gap = jnp.where(jnp.abs(delta) <= 1, jnp.inf, 0.0)
            gh, gl = split2(lax.rsqrt(dy * dy + far_ref[0] + jnp.minimum(far_ref[2], gap)))
            high.append(gh)
            low.append(gl)
        gh = jnp.concatenate(high, axis=0)
        got = bdot(gh, ph) + (bdot(jnp.concatenate(low, axis=0), ph) + bdot(gh, plo))
        for u in range(turn):
            delta = i * turn + u - (par - 1)
            moved = pltpu.roll(got[64 * u : 64 * u + 64], (delta + 128) % 128, 1)
            source = p_to - delta
            acc = acc + jnp.where((source >= 0) & (source < par), moved, 0.0)
        return acc

    return lax.fori_loop(0, (2 * par - 1) // turn, some, jnp.zeros((64, 128), F32))


def child_table(table_ref):
    lane, row = iota((64, 512), 1), iota((64, 512), 0)
    table = 1.0
    for bit, w in (((lane // 128) % 2, 16), (lane // 256, 4), ((lane // 64) % 2, 1)):
        table = table * cheb_pair(bit.astype(F32) - 0.5 + 0.5 * node((lane // w) % 4), node((row // w) % 4))
    table_ref[...] = table


def tree_kernel(
    n_seg, n_x, per, off_ref, str_ref, cell_ref, count_ref, fill_ref, near_ref, many_ref, spot_ref, out_ref,
    loc_ref, rec_ref, mul_ref, table_ref, mwin_ref, pm_ref, pq_ref, part_ref, share_ref, grid_ref, base_ref,
    near_x_ref, far_ref, box_ref, r2a_ref, r2b_ref, load_a_ref, load_b_ref, cols_ref, sum_ref, side_ref,
    send, mrecv, precv, swap_send, swap_recv, share_recv, own_sem,
):
    n_ex = 2 * n_x
    seg, ex = lax.axis_index("space"), lax.axis_index("exp")
    x, core = ex // 2, ex % 2
    prev, after = (seg + n_seg - 1) % n_seg, (seg + 1) % n_seg
    ring = [((x + d) % n_x) * 2 + core for d in range(n_x)]
    mates = [((x + d) % n_x) * 2 + 1 - core for d in range(n_x)]
    order = [1, n_x - 1] + list(range(2, n_x - 1))
    mate = mates[0]
    others = [ring[d] for d in order] + [mates[d] for d in [0] + order]
    there = seg // per
    mine = ex == there
    par = mul_ref.shape[0] // 2 * n_ex // 8
    leaf, size = off_ref.shape[1], off_ref.shape[2]
    own_rec = rec_ref.at[0 : leaf * 6]
    barrier = pltpu.get_barrier_semaphore()
    sent = []

    def box(part, who):
        return box_ref.at[pl.ds(pl.multiple_of((part * n_ex + who) * (leaf * 6), 8), leaf * 6)]

    def hello(to_seg, to_ex):
        pl.semaphore_signal(barrier, 1, device_id=mesh_at(to_seg, to_ex), device_id_type=pl.DeviceIdType.MESH)

    def not_self(i):
        return jnp.logical_not(mine & (seg % per == i))

    for o in others:
        hello(seg, o)
    hello(prev, ex)
    hello(after, ex)
    for i in range(per):

        @pl.when(not_self(i))
        def _():
            hello(ex * per + i, there)

    particles(seg, ex, off_ref, str_ref, cell_ref, count_ref, fill_ref, rec_ref, mul_ref)
    far_tables(seg, ex, per, far_ref)
    rec_ref[leaf * 6 :, :] = jnp.zeros((8, size), F32)
    box_ref[18 * n_ex * leaf :, :] = jnp.zeros((8, size), F32)
    pl.semaphore_wait(barrier, len(others) + 2 + jnp.where(mine, per - 1, per))

    def push(src, dst, recv, to_seg, to_ex):
        copy = remote(src, dst, send.at[len(sent)], recv, to_seg, to_ex)
        copy.start()
        sent.append(copy)

    def push_m(src, part, who, to_seg, to_ex):
        push(src, mwin_ref.at[part, who], mrecv.at[part, who], to_seg, to_ex)

    def push_p(src, part, who, to_seg, to_ex):
        push(src, box(part, who), precv.at[part, who], to_seg, to_ex)

    def got_m(part, who):
        remote(mul_ref, mwin_ref.at[part, who], send.at[0], mrecv.at[part, who], seg, mate).wait_recv()

    def got_p(part, who):
        remote(own_rec, box(part, who), send.at[0], precv.at[part, who], seg, mate).wait_recv()

    for o in others:
        push_m(mul_ref, 1, ex, seg, o)
    push_m(mul_ref, 0, ex, after, ex)
    push_m(mul_ref, 2, ex, prev, ex)
    for d in order:
        push_p(own_rec, 1, ex, seg, ring[d])
    push_p(own_rec, 0, ex, after, ex)
    push_p(own_rec, 2, ex, prev, ex)
    push_p(own_rec, 1, ex, seg, mate)
    keep = pltpu.make_async_copy(own_rec, box(1, ex), own_sem)
    keep.start()
    mwin_ref[1, ex] = mul_ref[...]
    grid_ref[...] = jnp.zeros(grid_ref.shape, F32)
    loc_ref[...] = jnp.zeros(loc_ref.shape, F32)
    m2l_tables(base_ref, near_x_ref)
    child_table(table_ref)
    target_sides(seg, leaf, spot_ref, rec_ref, side_ref)
    for d in order:
        got_m(1, ring[d])
        push_m(mwin_ref.at[1, ring[d]], 0, ring[d], after, ex)
        push_m(mwin_ref.at[1, ring[d]], 2, ring[d], prev, ex)
    for d in range(n_x):
        got_m(1, mates[d])
    g01, g2 = sorted_block(mwin_ref, 1, True)
    pm_ref[...] = parent_moments(g01, g2)
    store_rows(grid_ref, 1, g01, g2)

    def pass_on(d):
        got_p(1, ring[d])
        push_p(box(1, ring[d]), 0, ring[d], after, ex)
        push_p(box(1, ring[d]), 2, ring[d], prev, ex)
        push_p(box(1, ring[d]), 1, ring[d], seg, mate)

    def swap(i):
        return remote(pm_ref, pq_ref.at[seg % per], swap_send.at[i], swap_recv.at[seg % per], ex * per + i, there)

    for i in range(per):

        @pl.when(not_self(i))
        def _():
            swap(i).start()

    @pl.when(mine)
    def _():
        pq_ref[seg % per] = pm_ref[...]

    for d in order:
        pass_on(d)
    m2l_segment(1, par, grid_ref, base_ref, near_x_ref, loc_ref)
    for d in [0] + order:
        for part in (0, 2):
            got_m(part, ring[d])
            push_m(mwin_ref.at[part, ring[d]], part, ring[d], seg, mate)

    def pass_mate(d):
        for part in (0, 2):
            got_p(part, ring[d])
            push_p(box(part, ring[d]), part, ring[d], seg, mate)

    pass_mate(0)
    for d in range(n_x):
        for part in (0, 2):
            got_m(part, mates[d])
    for part, guard in ((0, seg > 0), (2, seg < n_seg - 1)):
        g01, g2 = sorted_block(mwin_ref, part, guard)
        store_rows(grid_ref, part, g01, g2)

    def sides(i, carry):
        m2l_segment(2 * i, par, grid_ref, base_ref, near_x_ref, loc_ref)
        return carry

    lax.fori_loop(0, 2, sides, 0)
    for d in order:
        pass_mate(d)
    for i in range(per):

        @pl.when(not_self(i))
        def _():
            remote(pm_ref, pq_ref.at[i], swap_send.at[i], swap_recv.at[i], ex * per + i, there).wait_recv()
            swap(i).wait_send()

    part_ref[...] = far_sum(pq_ref, far_ref)
    for o in others:
        push(part_ref, share_ref.at[ex], share_recv.at[ex], seg, o)
    share_ref[ex] = part_ref[...]
    for d in range(n_x):
        for part in range(3):
            got_p(part, mates[d])
    keep.wait()
    bufs = ((r2a_ref, load_a_ref), (r2b_ref, load_b_ref))
    near_field(seg, leaf, n_ex * leaf, near_ref, many_ref, spot_ref, side_ref, box_ref, bufs, cols_ref, sum_ref)(leaf // 2)
    for o in others:
        remote(part_ref, share_ref.at[o], send.at[0], share_recv.at[o], seg, o).wait_recv()
    parent = share_ref[0]
    for i in range(1, n_ex):
        parent = parent + share_ref[i]
    loc_ref[...] += dot3(jnp.swapaxes(parent, 0, 1)[: 3 * par, :], table_ref[...])
    far = leaf_far(cell_ref, off_ref, loc_ref)
    slot = ex * leaf + iota((leaf, size), 0)
    live = (iota((leaf, size), 1).astype(F32) < column(fill_ref[...], leaf)) & (slot < count_ref[0])
    for c in range(3):
        out_ref[c] = jnp.where(live, (far[c] + sum_ref[c]) * SCALE, 0.0)
    for copy in sent:
        copy.wait_send()


def frame(seg, c):
    row8 = iota((8, 128), 0)
    spot = (2 * seg + ((c >> 1) & 1), c >> 2, c & 1)
    mx, my, mz = (jnp.where(row8 == a, m.astype(F32) + 0.5, 0.0) for a, m in enumerate(spot))
    return mx + my + mz


def local(rows, middle):
    near = jnp.where(iota((8, 128), 0) < 3, rows - middle, 0.0)
    return near + pltpu.roll(near, 3, 0)


def target_sides(seg, leaf, spot_ref, rec_ref, side_ref):
    row8 = iota((8, 128), 0)
    first, second = row8 < 3, (row8 >= 3) & (row8 < 6)
    none = jnp.zeros((8, 128), F32)
    keep = jnp.where(row8 < 6, 1.0, 0.0)

    def one(t):
        here = local(rec_ref[pl.ds(t * 6, 8), :], frame(seg, spot_ref[t]))
        xh, xm, xl = split3(-2.0 * here)
        length = 0.5 * jnp.sum(here * here, axis=0, keepdims=True) + SMOOTH
        nh, nm, nl = split3(length)
        norm = jnp.where(row8 == 3, nh, jnp.where(row8 == 4, nm, nl))
        cross = jnp.where(first, xh, jnp.where(second, xm, 0.0))
        last = jnp.where(first, xh, jnp.where(second, xl, 0.0))
        tail = jnp.where(first, 1.0, jnp.where(second, norm, 0.0))
        side = jnp.concatenate([cross, cross, last, keep, tail] + [none] * 11, axis=0)
        side_ref[t] = jnp.swapaxes(side, 0, 1).astype(BF16)

    def some(i, carry):
        for u in range(8):
            one(8 * i + u)
        return carry

    lax.fori_loop(0, leaf // 8, some, 0)


def near_field(seg, leaf, slots, near_ref, many_ref, spot_ref, side_ref, box_ref, bufs, cols_ref, near_out_ref):
    count, size = near_ref.shape[0], 128
    start = (seg - 1) * slots
    row8 = iota((8, size), 0)
    first, second = row8 < 3, (row8 >= 3) & (row8 < 6)
    none = jnp.zeros((8, size), F32)
    block = 32

    def pair(t, k0, middle, side, many, buf):
        r2_ref, load_ref = buf
        feats = []
        for k in (k0, k0 + 1):
            rows = box_ref[pl.ds(jnp.clip(near_ref[k, t] - start, 0, 3 * slots - 1) * 6, 8), :]
            y = local(rows, middle)
            yh, ym, yl = split3(y)
            sh, sm, sl = split3(y * y)
            feat = [yh, ym, jnp.where(first, yl, yh), jnp.where(first, sh, sm), jnp.where(first, sl, 1.0), none]
            feats.append(jnp.concatenate(feat, axis=0).astype(BF16))
            load_ref[k] = rows * jnp.clip(many - k, 0, 1).astype(F32)
        r2_ref[:, size * k0 : size * k0 + 2 * size] = bdot(side, jnp.concatenate(feats, axis=1))

    def gather_rows(n, buf):
        r2_ref, load_ref = buf
        at = block * n
        acc = [jnp.zeros((block, size), F32) for _ in range(3)]
        for k in range(count):
            g = lax.rsqrt(r2_ref[at : at + block, size * k : size * k + size])
            for c in range(3):
                acc[c] = acc[c] + g * load_ref[k, 3 + c : 4 + c, :]
        lane = iota((block, size), 1)
        s0, s1, s2 = (jnp.sum(x, axis=1, keepdims=True) for x in acc)
        cols_ref[at : at + block, :] = jnp.where(lane == 0, s0, jnp.where(lane == 1, s1, s2))

    def store(t):
        result = jnp.swapaxes(cols_ref[...], 0, 1)
        for c in range(3):
            near_out_ref[c, pl.ds(t, 1), :] = result[c : c + 1, :]

    def work(t_next, next_buf, t_now, now_buf):
        jobs = list(range(size // block)) if now_buf is not None else []
        steps = count // 2
        if next_buf is not None:
            middle = frame(seg, spot_ref[t_next])
            side = side_ref[t_next, :, 0:48]
            many = many_ref[t_next]
        for p in range(steps):
            if next_buf is not None:
                pair(t_next, 2 * p, middle, side, many, next_buf)
            while jobs and (size // block - len(jobs)) * steps < (p + 1) * (size // block):
                gather_rows(jobs.pop(0), now_buf)
        if now_buf is not None:
            store(t_now)

    def run(turns):
        work(0, bufs[0], None, None)

        def two(i, carry):
            t = 2 * i
            work(t + 1, bufs[1], t, bufs[0])
            work((t + 2) % leaf, bufs[0], t + 1, bufs[1])
            return carry

        lax.fori_loop(0, turns, two, 0)

    return run


def leaf_far(cell_ref, off_ref, loc_ref):
    leaf, size = off_ref.shape[1], off_ref.shape[2]
    par = loc_ref.shape[0] // 3
    cell = column(cell_ref[...], leaf).astype(jnp.int32)
    chosen = jnp.where((cell >> 3) == iota((leaf, par), 1), 1.0, 0.0).astype(BF16)
    child = cell & 7
    lane = iota((leaf, 128), 1)
    expansion = []
    for c in range(3):
        wide = pick_exact(chosen, loc_ref[c * par : (c + 1) * par, :])
        kept = jnp.zeros((leaf, 128), F32)
        for i in range(4):
            kept = kept + jnp.where(lane // 64 + 2 * i == child, wide[:, 128 * i : 128 * i + 128], 0.0)
        expansion.append(kept + pltpu.roll(kept, 64, 1))
    far = [jnp.zeros((leaf, size), F32) for _ in range(3)]

    def visit(a, w):
        for c in range(3):
            far[c] = far[c] + expansion[c][:, a : a + 1] * w

    weights_loop([off_ref[a] for a in range(3)], visit)
    return far


def shape(*dims):
    return jax.ShapeDtypeStruct(dims, F32)


def tree_call(n_seg, n_ex, offsets, strength, cell_row, count, fill_row, near, many, spot):
    n_x, per = n_ex // 2, n_seg // n_ex
    leaf, size = offsets.shape[1], offsets.shape[2]
    par = leaf * n_ex // 8
    dma = pltpu.SemaphoreType.DMA
    return pl.pallas_call(
        lambda *refs: tree_kernel(n_seg, n_x, per, *refs),
        out_shape=shape(3, leaf, size),
        in_specs=[VMEM, VMEM, VMEM, SMEM, VMEM, SMEM, SMEM, SMEM],
        out_specs=VMEM,
        scratch_shapes=[
            pltpu.VMEM((3 * par, 512), F32),
            pltpu.VMEM((leaf * 6 + 8, size), F32),
            pltpu.VMEM((leaf * 2, size), F32),
            pltpu.VMEM((64, 512), F32),
            pltpu.VMEM((3, n_ex, leaf * 2, size), F32),
            pltpu.VMEM((2 * par, 128), F32),
            pltpu.VMEM((per, 2 * par, 128), F32),
            pltpu.VMEM((64, 128), F32),
            pltpu.VMEM((n_ex, 64, 128), F32),
            pltpu.VMEM((6, 3, par + 16, 256), F32),
            pltpu.VMEM((3, 256, 512), F32),
            pltpu.VMEM((2, 256, 512), F32),
            pltpu.VMEM((3, 64, per * 64), F32),
            *near_scratch(18 * n_ex * leaf, near.shape[0], leaf, size),
            dma((14 * n_x + 5,)),
            dma((3, n_ex)),
            dma((3, n_ex)),
            dma((per,)),
            dma((per,)),
            dma((n_ex,)),
            dma,
        ],
        compiler_params=pltpu.CompilerParams(collective_id=0, has_side_effects=True, vmem_limit_bytes=BIG),
    )(offsets, strength, cell_row, count, fill_row, near, many, spot)


def near_scratch(rows, count, leaf, size):
    return [
        pltpu.VMEM((rows + 8, size), F32),
        pltpu.VMEM((size, count * size), F32),
        pltpu.VMEM((size, count * size), F32),
        pltpu.VMEM((count, 8, size), F32),
        pltpu.VMEM((count, 8, size), F32),
        pltpu.VMEM((size, size), F32),
        pltpu.VMEM((3, leaf, size), F32),
        pltpu.VMEM((leaf, size, size), BF16),
    ]


def solution(mesh):
    n_seg, n_ex = mesh.shape["space"], mesh.shape["exp"]

    def body(offsets, strength, leaf_cell, leaf_count, leaf_fill, near_list, near_count):
        leaf, size = offsets.shape[1], offsets.shape[2]
        cell_row = leaf_cell.reshape(1, leaf)
        fill_row = leaf_fill.reshape(1, leaf)
        return tree_call(
            n_seg, n_ex, offsets, strength, cell_row, leaf_count, fill_row, near_list, near_count, leaf_cell
        )

    in_specs = (
        P(None, ("space", "exp"), None),
        P(None, ("space", "exp"), None),
        P(("space", "exp")),
        P("space"),
        P(("space", "exp")),
        P(None, ("space", "exp")),
        P(("space", "exp")),
    )
    out_specs = P(None, ("space", "exp"), None)
    return jax.shard_map(body, mesh=mesh, in_specs=in_specs, out_specs=out_specs, check_vma=False)
```

```python
import math

import jax
import jax.numpy as jnp
from jax import lax
from jax.experimental import pallas as pl
from jax.experimental.pallas import tpu as pltpu
from jax.sharding import PartitionSpec as P

NODES = [math.cos((2 * k + 1) * math.pi / 8) for k in range(4)]
SMOOTH = 0.01
SCALE = 1.0 / (4.0 * math.pi)
F32 = jnp.float32
BF16 = jnp.bfloat16
VMEM = pl.BlockSpec(memory_space=pltpu.VMEM)
SMEM = pl.BlockSpec(memory_space=pltpu.SMEM)
ANY = pl.BlockSpec(memory_space=pl.ANY)
BIG = 60 * 1024 * 1024
NN = (((1,), (0,)), ((), ()))
NT = (((1,), (1,)), ((), ()))


def iota(shape, axis):
    return lax.broadcasted_iota(jnp.int32, shape, axis)


def split2(x):
    hi = x.astype(BF16)
    return hi, (x - hi.astype(F32)).astype(BF16)


def split3(x):
    hi = x.astype(BF16).astype(F32)
    rest = x - hi
    mid = rest.astype(BF16).astype(F32)
    return hi, mid, rest - mid


def bdot(a, b, dims=NN):
    return lax.dot_general(a, b, dims, preferred_element_type=F32)


def dot3(a, b, dims=NN):
    ah, al = a if isinstance(a, tuple) else split2(a)
    bh, bl = b if isinstance(b, tuple) else split2(b)
    return bdot(ah, bh, dims) + (bdot(al, bh, dims) + bdot(ah, bl, dims))


def pick_exact(one_hot, x):
    hi = x.astype(BF16)
    rest = x - hi.astype(F32)
    mid = rest.astype(BF16)
    low = (rest - mid.astype(F32)).astype(BF16)
    return bdot(one_hot, hi) + (bdot(one_hot, mid) + bdot(one_hot, low))


def node(k):
    return jnp.where(
        k == 0, NODES[0], jnp.where(k == 1, NODES[1], jnp.where(k == 2, NODES[2], NODES[3]))
    ).astype(F32)


def cheb(u):
    return u, 2.0 * u * u - 1.0, (4.0 * u * u - 3.0) * u


def factors(u):
    t1, t2, t3 = cheb(u)
    out = []
    for t in NODES:
        out.append(0.25 + t1 * (0.5 * t) + t2 * (0.5 * (2 * t * t - 1)) + t3 * (0.5 * (4 * t**3 - 3 * t)))
    return out


def cheb_pair(u, t):
    u1, u2, u3 = cheb(u)
    t1, t2, t3 = cheb(t)
    return 0.25 + 0.5 * (u1 * t1 + u2 * t2 + u3 * t3)


def column(row, count):
    spread = jnp.where(iota((count, count), 0) == iota((count, count), 1), row.astype(F32), 0.0)
    return jnp.sum(spread, axis=1, keepdims=True)


def weights_loop(offs, visit):
    fx, fy, fz = (factors(o) for o in offs)
    for i in range(4):
        for j in range(4):
            fxy = fx[i] * fy[j]
            for k in range(4):
                visit(16 * i + 4 * j + k, fxy * fz[k])


def particles(seg, ex, off_ref, str_ref, cell_ref, count_ref, fill_ref, rec_ref, mul_ref):
    leaf, size = off_ref.shape[1], off_ref.shape[2]
    cell_f = column(cell_ref[...], leaf)
    fill = column(fill_ref[...], leaf)
    cell = cell_f.astype(jnp.int32)
    slot = ex * leaf + iota((leaf, size), 0)
    alive = (slot < count_ref[0]) & (iota((leaf, size), 1).astype(F32) < fill)
    centre = (
        2 * seg + ((cell >> 1) & 1),
        cell >> 2,
        cell & 1,
    )
    offs = [off_ref[a] for a in range(3)]
    charge = []
    for a in range(3):
        pos = (centre[a].astype(F32) + 0.5) + 0.5 * offs[a]
        rec_ref[pl.ds(a, leaf, 6), :] = pos
        q = jnp.where(alive, str_ref[a], 0.0)
        rec_ref[pl.ds(3 + a, leaf, 6), :] = q
        charge.append(q)
    lane = iota((leaf, size), 1)
    acc = [jnp.zeros((leaf, size), F32), jnp.where(lane >= 64, cell_f, 0.0)]

    def visit(a, w):
        for c in range(3):
            total = jnp.sum(charge[c] * w, axis=1, keepdims=True)
            at = a + 64 * (c % 2)
            acc[c // 2] = jnp.where(lane == at, total, acc[c // 2])

    weights_loop(offs, visit)
    mul_ref[0:leaf, :] = acc[0]
    mul_ref[leaf : 2 * leaf, :] = acc[1]


def mesh_at(seg, ex):
    return {"space": seg, "exp": ex}


def remote(src, dst, send, recv, seg, ex):
    return pltpu.make_async_remote_copy(
        src_ref=src, dst_ref=dst, send_sem=send, recv_sem=recv,
        device_id=mesh_at(seg, ex), device_id_type=pl.DeviceIdType.MESH,
    )


def sorted_block(mul_ref, part, guard):
    n_ex, leaf = mul_ref.shape[1], mul_ref.shape[2] // 2
    slots = n_ex * leaf
    par = slots // 8
    m01 = mul_ref[part, :, 0:leaf, :].reshape(slots, 128)
    m2c = mul_ref[part, :, leaf : 2 * leaf, :].reshape(slots, 128)
    cells = jnp.swapaxes(m2c, 0, 1)[64:65, :]
    row = iota((slots, slots), 0)
    wanted = ((row % par) * 8 + row // par).astype(F32)
    one_hot = jnp.where((wanted == cells) & guard, 1.0, 0.0).astype(BF16)
    return pick_exact(one_hot, m01), pick_exact(one_hot, m2c)


def parent_moments(g01, g2):
    par = g01.shape[0] // 8
    total = jnp.zeros((2 * par, 128), F32)
    lane_b = iota((128, 128), 1)
    row_a = iota((128, 128), 0)
    bx, by, bz = (node((lane_b // w) % 4) for w in (16, 4, 1))
    ax, ay, az = (node((row_a // w) % 4) for w in (16, 4, 1))
    sx, sy, sz = ([cheb_pair(bit - 0.5 + 0.5 * a, b) for bit in (0, 1)] for a, b in ((ax, bx), (ay, by), (az, bz)))
    same = (lane_b // 64) == (row_a // 64)
    for h in range(8):
        table = jnp.where(same, sx[(h // 2) % 2] * sy[h // 4] * sz[h % 2], 0.0)
        lhs = jnp.concatenate([g01[h * par : (h + 1) * par], g2[h * par : (h + 1) * par]], axis=0)
        total = total + dot3(lhs, table)
    return total


def store_rows(grid_ref, j, g01, g2):
    par = g01.shape[0] // 8
    for odd in range(2):
        for c in range(3):
            src = g01 if c < 2 else g2
            lo = 64 * (c % 2)
            grid_ref[j * 2 + odd, c, 8 : 8 + par, :] = jnp.concatenate(
                [src[(4 * odd + r) * par : (4 * odd + r + 1) * par, lo : lo + 64] for r in range(4)], axis=1
            )


def m2l_tables(base_ref, near_x_ref):
    lane, row = iota((256, 512), 1), iota((256, 512), 0)
    ux = ((lane // 128) % 2).astype(F32) + 0.5 * node((lane // 16) % 4)
    vx = (row // 128).astype(F32) + 0.5 * node((row // 16) % 4)
    uz = ((lane // 64) % 2).astype(F32) + 0.5 * node(lane % 4)
    vz = ((row // 64) % 2).astype(F32) + 0.5 * node(row % 4)
    base_ref[1] = (uz - vz) * (uz - vz) + SMOOTH
    base_ref[2] = ux - vx
    near_x_ref[1] = ((row // 128) - (lane // 128) % 2).astype(F32)


def m2l_segment(j, par, grid_ref, base_ref, near_x_ref, loc_ref):
    lane1 = iota((1, 512), 1)
    up1 = (lane1 // 256).astype(F32)
    uy = up1 + 0.5 * node((lane1 // 4) % 4)
    vy = 0.5 * node((iota((256, 1), 0) // 4) % 4)
    shift = 2.0 * jnp.asarray(j, jnp.int32).astype(F32) - 2.0
    dx = base_ref[2] - shift
    base_ref[0] = dx * dx + base_ref[1]
    near_x_ref[0] = jnp.where(jnp.abs(near_x_ref[1] + shift) < 1.5, jnp.inf, 0.0)
    for odd in range(2):
        for i in range(3):
            height = 2 * i + odd - 2
            lhs = jnp.concatenate([grid_ref[j * 2 + odd, c, 7 + i : 7 + i + par, :] for c in range(3)], axis=0)
            near_y = jnp.where(jnp.abs(height - up1) < 1.5, jnp.inf, 0.0)
            dy = (uy - height) - vy
            g = lax.rsqrt(dy * dy + base_ref[0] + jnp.minimum(near_x_ref[0], near_y))
            loc_ref[...] += dot3(lhs, g)


def far_tables(seg, ex, per, far_ref):
    wide = per * 64
    lane, row = iota((64, wide), 1), iota((64, wide), 0)
    step = (seg - ex * per - lane // 64).astype(F32)
    dx = 2.0 * step + node(row // 16) - node((lane // 16) % 4)
    dz = node(row % 4) - node(lane % 4)
    far_ref[0] = dx * dx + (dz * dz + SMOOTH)
    far_ref[1] = node((row // 4) % 4) - node((lane // 4) % 4)
    far_ref[2] = jnp.where(jnp.abs(step) < 1.5, jnp.inf, 0.0)


def far_sum(pq_ref, far_ref):
    per = pq_ref.shape[0]
    par = pq_ref.shape[1] // 2
    wide = per * 64
    turn = 7 if (2 * par - 1) % 7 == 0 else 1
    rows = []
    for c in range(3):
        r0, l0 = par * (c // 2), 64 * (c % 2)
        rows.append(jnp.concatenate([pq_ref[q, r0 : r0 + par, l0 : l0 + 64] for q in range(per)], axis=1))
    rows.append(jnp.zeros((128 - 3 * par, wide), F32))
    ph, plo = split2(jnp.swapaxes(jnp.concatenate(rows, axis=0), 0, 1))
    p_to = iota((64, 128), 1) % par

    def some(i, acc):
        high, low = [], []
        for u in range(turn):
            delta = i * turn + u - (par - 1)
            dy = far_ref[1] + 2.0 * delta.astype(F32)
            gap = jnp.where(jnp.abs(delta) <= 1, jnp.inf, 0.0)
            gh, gl = split2(lax.rsqrt(dy * dy + far_ref[0] + jnp.minimum(far_ref[2], gap)))
            high.append(gh)
            low.append(gl)
        gh = jnp.concatenate(high, axis=0)
        got = bdot(gh, ph) + (bdot(jnp.concatenate(low, axis=0), ph) + bdot(gh, plo))
        for u in range(turn):
            delta = i * turn + u - (par - 1)
            moved = pltpu.roll(got[64 * u : 64 * u + 64], (delta + 128) % 128, 1)
            source = p_to - delta
            acc = acc + jnp.where((source >= 0) & (source < par), moved, 0.0)
        return acc

    return lax.fori_loop(0, (2 * par - 1) // turn, some, jnp.zeros((64, 128), F32))


def child_table(table_ref):
    lane, row = iota((64, 512), 1), iota((64, 512), 0)
    table = 1.0
    for bit, w in (((lane // 128) % 2, 16), (lane // 256, 4), ((lane // 64) % 2, 1)):
        table = table * cheb_pair(bit.astype(F32) - 0.5 + 0.5 * node((lane // w) % 4), node((row // w) % 4))
    table_ref[...] = table


def tree_kernel(
    n_seg, n_x, per, off_ref, str_ref, cell_ref, count_ref, fill_ref, near_ref, many_ref, spot_ref, out_ref,
    loc_ref, rec_ref, mul_ref, table_ref, mwin_ref, pm_ref, pq_ref, part_ref, share_ref, grid_ref, base_ref,
    near_x_ref, far_ref, box_ref, r2a_ref, r2b_ref, load_a_ref, load_b_ref, cols_ref, sum_ref, side_ref,
    send, mrecv, precv, swap_send, swap_recv, share_recv, own_sem,
):
    n_ex = 2 * n_x
    seg, ex = lax.axis_index("space"), lax.axis_index("exp")
    x, core = ex // 2, ex % 2
    prev, after = (seg + n_seg - 1) % n_seg, (seg + 1) % n_seg
    ring = [((x + d) % n_x) * 2 + core for d in range(n_x)]
    mates = [((x + d) % n_x) * 2 + 1 - core for d in range(n_x)]
    order = [1, n_x - 1] + list(range(2, n_x - 1))
    mate = mates[0]
    others = [ring[d] for d in order] + [mates[d] for d in [0] + order]
    there = seg // per
    mine = ex == there
    par = mul_ref.shape[0] // 2 * n_ex // 8
    leaf, size = off_ref.shape[1], off_ref.shape[2]
    own_rec = rec_ref.at[0 : leaf * 6]
    barrier = pltpu.get_barrier_semaphore()
    sent = []

    def box(part, who):
        return box_ref.at[pl.ds(pl.multiple_of((part * n_ex + who) * (leaf * 6), 8), leaf * 6)]

    def hello(to_seg, to_ex):
        pl.semaphore_signal(barrier, 1, device_id=mesh_at(to_seg, to_ex), device_id_type=pl.DeviceIdType.MESH)

    def not_self(i):
        return jnp.logical_not(mine & (seg % per == i))

    for o in others:
        hello(seg, o)
    hello(prev, ex)
    hello(after, ex)
    for i in range(per):

        @pl.when(not_self(i))
        def _():
            hello(ex * per + i, there)

    particles(seg, ex, off_ref, str_ref, cell_ref, count_ref, fill_ref, rec_ref, mul_ref)
    grid_ref[...] = jnp.zeros(grid_ref.shape, F32)
    loc_ref[...] = jnp.zeros(loc_ref.shape, F32)
    m2l_tables(base_ref, near_x_ref)
    far_tables(seg, ex, per, far_ref)
    child_table(table_ref)
    rec_ref[leaf * 6 :, :] = jnp.zeros((8, size), F32)
    target_sides(seg, leaf, spot_ref, rec_ref, side_ref)
    box_ref[18 * n_ex * leaf :, :] = jnp.zeros((8, size), F32)
    pl.semaphore_wait(barrier, len(others) + 2 + jnp.where(mine, per - 1, per))

    def push(src, dst, recv, to_seg, to_ex):
        copy = remote(src, dst, send.at[len(sent)], recv, to_seg, to_ex)
        copy.start()
        sent.append(copy)

    def push_m(src, part, who, to_seg, to_ex):
        push(src, mwin_ref.at[part, who], mrecv.at[part, who], to_seg, to_ex)

    def push_p(src, part, who, to_seg, to_ex):
        push(src, box(part, who), precv.at[part, who], to_seg, to_ex)

    def got_m(part, who):
        remote(mul_ref, mwin_ref.at[part, who], send.at[0], mrecv.at[part, who], seg, mate).wait_recv()

    def got_p(part, who):
        remote(own_rec, box(part, who), send.at[0], precv.at[part, who], seg, mate).wait_recv()

    for o in others:
        push_m(mul_ref, 1, ex, seg, o)
    push_m(mul_ref, 0, ex, after, ex)
    push_m(mul_ref, 2, ex, prev, ex)
    for d in order:
        push_p(own_rec, 1, ex, seg, ring[d])
    push_p(own_rec, 0, ex, after, ex)
    push_p(own_rec, 2, ex, prev, ex)
    push_p(own_rec, 1, ex, seg, mate)
    keep = pltpu.make_async_copy(own_rec, box(1, ex), own_sem)
    keep.start()
    mwin_ref[1, ex] = mul_ref[...]
    for d in order:
        got_m(1, ring[d])
        push_m(mwin_ref.at[1, ring[d]], 0, ring[d], after, ex)
        push_m(mwin_ref.at[1, ring[d]], 2, ring[d], prev, ex)
    for d in range(n_x):
        got_m(1, mates[d])
    g01, g2 = sorted_block(mwin_ref, 1, True)
    pm_ref[...] = parent_moments(g01, g2)
    store_rows(grid_ref, 1, g01, g2)

    def pass_on(d):
        got_p(1, ring[d])
        push_p(box(1, ring[d]), 0, ring[d], after, ex)
        push_p(box(1, ring[d]), 2, ring[d], prev, ex)
        push_p(box(1, ring[d]), 1, ring[d], seg, mate)

    def swap(i):
        return remote(pm_ref, pq_ref.at[seg % per], swap_send.at[i], swap_recv.at[seg % per], ex * per + i, there)

    for i in range(per):

        @pl.when(not_self(i))
        def _():
            swap(i).start()

    @pl.when(mine)
    def _():
        pq_ref[seg % per] = pm_ref[...]

    for d in order:
        pass_on(d)
    m2l_segment(1, par, grid_ref, base_ref, near_x_ref, loc_ref)
    for d in [0] + order:
        for part in (0, 2):
            got_m(part, ring[d])
            push_m(mwin_ref.at[part, ring[d]], part, ring[d], seg, mate)

    def pass_mate(d):
        for part in (0, 2):
            got_p(part, ring[d])
            push_p(box(part, ring[d]), part, ring[d], seg, mate)

    pass_mate(0)
    for d in range(n_x):
        for part in (0, 2):
            got_m(part, mates[d])
    for part, guard in ((0, seg > 0), (2, seg < n_seg - 1)):
        g01, g2 = sorted_block(mwin_ref, part, guard)
        store_rows(grid_ref, part, g01, g2)

    def sides(i, carry):
        m2l_segment(2 * i, par, grid_ref, base_ref, near_x_ref, loc_ref)
        return carry

    lax.fori_loop(0, 2, sides, 0)
    for d in order:
        pass_mate(d)
    for i in range(per):

        @pl.when(not_self(i))
        def _():
            remote(pm_ref, pq_ref.at[i], swap_send.at[i], swap_recv.at[i], ex * per + i, there).wait_recv()
            swap(i).wait_send()

    part_ref[...] = far_sum(pq_ref, far_ref)
    for o in others:
        push(part_ref, share_ref.at[ex], share_recv.at[ex], seg, o)
    share_ref[ex] = part_ref[...]
    for d in range(n_x):
        for part in range(3):
            got_p(part, mates[d])
    keep.wait()
    bufs = ((r2a_ref, load_a_ref), (r2b_ref, load_b_ref))
    near_field(seg, leaf, n_ex * leaf, near_ref, many_ref, spot_ref, side_ref, box_ref, bufs, cols_ref, sum_ref)(leaf // 2)
    for o in others:
        remote(part_ref, share_ref.at[o], send.at[0], share_recv.at[o], seg, o).wait_recv()
    parent = share_ref[0]
    for i in range(1, n_ex):
        parent = parent + share_ref[i]
    loc_ref[...] += dot3(jnp.swapaxes(parent, 0, 1)[: 3 * par, :], table_ref[...])
    far = leaf_far(cell_ref, off_ref, loc_ref)
    slot = ex * leaf + iota((leaf, size), 0)
    live = (iota((leaf, size), 1).astype(F32) < column(fill_ref[...], leaf)) & (slot < count_ref[0])
    for c in range(3):
        out_ref[c] = jnp.where(live, far[c] + sum_ref[c], 0.0)
    for copy in sent:
        copy.wait_send()


def frame(seg, c):
    row8 = iota((8, 128), 0)
    spot = (2 * seg + ((c >> 1) & 1), c >> 2, c & 1)
    mx, my, mz = (jnp.where(row8 == a, m.astype(F32) + 0.5, 0.0) for a, m in enumerate(spot))
    return mx + my + mz


def local(rows, middle):
    near = jnp.where(iota((8, 128), 0) < 3, rows - middle, 0.0)
    return near + pltpu.roll(near, 3, 0)


def target_sides(seg, leaf, spot_ref, rec_ref, side_ref):
    row8 = iota((8, 128), 0)
    first, second = row8 < 3, (row8 >= 3) & (row8 < 6)
    none = jnp.zeros((8, 128), F32)
    keep = jnp.where(row8 < 6, 1.0, 0.0)

    def one(t):
        here = local(rec_ref[pl.ds(t * 6, 8), :], frame(seg, spot_ref[t]))
        xh, xm, xl = split3(-2.0 * here)
        length = 0.5 * jnp.sum(here * here, axis=0, keepdims=True) + SMOOTH
        nh, nm, nl = split3(length)
        norm = jnp.where(row8 == 3, nh, jnp.where(row8 == 4, nm, nl))
        cross = jnp.where(first, xh, jnp.where(second, xm, 0.0))
        last = jnp.where(first, xh, jnp.where(second, xl, 0.0))
        tail = jnp.where(first, 1.0, jnp.where(second, norm, 0.0))
        side = jnp.concatenate([cross, cross, last, keep, tail] + [none] * 11, axis=0)
        side_ref[t] = jnp.swapaxes(side, 0, 1).astype(BF16)

    def some(i, carry):
        for u in range(8):
            one(8 * i + u)
        return carry

    lax.fori_loop(0, leaf // 8, some, 0)


def near_field(seg, leaf, slots, near_ref, many_ref, spot_ref, side_ref, box_ref, bufs, cols_ref, near_out_ref):
    count, size = near_ref.shape[0], 128
    start = (seg - 1) * slots
    row8 = iota((8, size), 0)
    first, second = row8 < 3, (row8 >= 3) & (row8 < 6)
    none = jnp.zeros((8, size), F32)
    block = 32

    def pair(t, k0, middle, side, many, buf):
        r2_ref, load_ref = buf
        feats = []
        for k in (k0, k0 + 1):
            rows = box_ref[pl.ds(jnp.clip(near_ref[k, t] - start, 0, 3 * slots - 1) * 6, 8), :]
            y = local(rows, middle)
            yh, ym, yl = split3(y)
            sh, sm, sl = split3(y * y)
            feat = [yh, ym, jnp.where(first, yl, yh), jnp.where(first, sh, sm), jnp.where(first, sl, 1.0), none]
            feats.append(jnp.concatenate(feat, axis=0).astype(BF16))
            load_ref[k] = rows * jnp.clip(many - k, 0, 1).astype(F32)
        r2_ref[:, size * k0 : size * k0 + 2 * size] = bdot(side, jnp.concatenate(feats, axis=1))

    def gather_rows(n, buf):
        r2_ref, load_ref = buf
        at = block * n
        acc = [jnp.zeros((block, size), F32) for _ in range(3)]
        for k in range(count):
            g = lax.rsqrt(r2_ref[at : at + block, size * k : size * k + size])
            for c in range(3):
                acc[c] = acc[c] + g * load_ref[k, 3 + c : 4 + c, :]
        lane = iota((block, size), 1)
        s0, s1, s2 = (jnp.sum(x, axis=1, keepdims=True) for x in acc)
        cols_ref[at : at + block, :] = jnp.where(lane == 0, s0, jnp.where(lane == 1, s1, s2))

    def store(t):
        result = jnp.swapaxes(cols_ref[...], 0, 1)
        for c in range(3):
            near_out_ref[c, pl.ds(t, 1), :] = result[c : c + 1, :]

    def work(t_next, next_buf, t_now, now_buf):
        jobs = list(range(size // block)) if now_buf is not None else []
        steps = count // 2
        if next_buf is not None:
            middle = frame(seg, spot_ref[t_next])
            side = side_ref[t_next, :, 0:48]
            many = many_ref[t_next]
        for p in range(steps):
            if next_buf is not None:
                pair(t_next, 2 * p, middle, side, many, next_buf)
            while jobs and (size // block - len(jobs)) * steps < (p + 1) * (size // block):
                gather_rows(jobs.pop(0), now_buf)
        if now_buf is not None:
            store(t_now)

    def run(turns):
        work(0, bufs[0], None, None)

        def two(i, carry):
            t = 2 * i
            work(t + 1, bufs[1], t, bufs[0])
            work((t + 2) % leaf, bufs[0], t + 1, bufs[1])
            return carry

        lax.fori_loop(0, turns, two, 0)

    return run


def leaf_far(cell_ref, off_ref, loc_ref):
    leaf, size = off_ref.shape[1], off_ref.shape[2]
    par = loc_ref.shape[0] // 3
    cell = column(cell_ref[...], leaf).astype(jnp.int32)
    chosen = jnp.where((cell >> 3) == iota((leaf, par), 1), 1.0, 0.0).astype(BF16)
    child = cell & 7
    lane = iota((leaf, 128), 1)
    expansion = []
    for c in range(3):
        wide = pick_exact(chosen, loc_ref[c * par : (c + 1) * par, :])
        kept = jnp.zeros((leaf, 128), F32)
        for i in range(4):
            kept = kept + jnp.where(lane // 64 + 2 * i == child, wide[:, 128 * i : 128 * i + 128], 0.0)
        expansion.append(kept + pltpu.roll(kept, 64, 1))
    far = [jnp.zeros((leaf, size), F32) for _ in range(3)]

    def visit(a, w):
        for c in range(3):
            far[c] = far[c] + expansion[c][:, a : a + 1] * w

    weights_loop([off_ref[a] for a in range(3)], visit)
    return far


def shape(*dims):
    return jax.ShapeDtypeStruct(dims, F32)


def tree_call(n_seg, n_ex, offsets, strength, cell_row, count, fill_row, near, many, spot):
    n_x, per = n_ex // 2, n_seg // n_ex
    leaf, size = offsets.shape[1], offsets.shape[2]
    par = leaf * n_ex // 8
    dma = pltpu.SemaphoreType.DMA
    return pl.pallas_call(
        lambda *refs: tree_kernel(n_seg, n_x, per, *refs),
        out_shape=shape(3, leaf, size),
        in_specs=[VMEM, VMEM, VMEM, SMEM, VMEM, SMEM, SMEM, SMEM],
        out_specs=VMEM,
        scratch_shapes=[
            pltpu.VMEM((3 * par, 512), F32),
            pltpu.VMEM((leaf * 6 + 8, size), F32),
            pltpu.VMEM((leaf * 2, size), F32),
            pltpu.VMEM((64, 512), F32),
            pltpu.VMEM((3, n_ex, leaf * 2, size), F32),
            pltpu.VMEM((2 * par, 128), F32),
            pltpu.VMEM((per, 2 * par, 128), F32),
            pltpu.VMEM((64, 128), F32),
            pltpu.VMEM((n_ex, 64, 128), F32),
            pltpu.VMEM((6, 3, par + 16, 256), F32),
            pltpu.VMEM((3, 256, 512), F32),
            pltpu.VMEM((2, 256, 512), F32),
            pltpu.VMEM((3, 64, per * 64), F32),
            *near_scratch(18 * n_ex * leaf, near.shape[0], leaf, size),
            dma((14 * n_x + 5,)),
            dma((3, n_ex)),
            dma((3, n_ex)),
            dma((per,)),
            dma((per,)),
            dma((n_ex,)),
            dma,
        ],
        compiler_params=pltpu.CompilerParams(collective_id=0, has_side_effects=True, vmem_limit_bytes=BIG),
    )(offsets, strength, cell_row, count, fill_row, near, many, spot)


def near_scratch(rows, count, leaf, size):
    return [
        pltpu.VMEM((rows + 8, size), F32),
        pltpu.VMEM((size, count * size), F32),
        pltpu.VMEM((size, count * size), F32),
        pltpu.VMEM((count, 8, size), F32),
        pltpu.VMEM((count, 8, size), F32),
        pltpu.VMEM((size, size), F32),
        pltpu.VMEM((3, leaf, size), F32),
        pltpu.VMEM((leaf, size, size), BF16),
    ]


def solution(mesh):
    n_seg, n_ex = mesh.shape["space"], mesh.shape["exp"]

    def body(offsets, strength, leaf_cell, leaf_count, leaf_fill, near_list, near_count):
        leaf, size = offsets.shape[1], offsets.shape[2]
        cell_row = leaf_cell.reshape(1, leaf)
        fill_row = leaf_fill.reshape(1, leaf)
        total = tree_call(
            n_seg, n_ex, offsets, strength, cell_row, leaf_count, fill_row, near_list, near_count, leaf_cell
        )
        return total * SCALE

    in_specs = (
        P(None, ("space", "exp"), None),
        P(None, ("space", "exp"), None),
        P(("space", "exp")),
        P("space"),
        P(("space", "exp")),
        P(None, ("space", "exp")),
        P(("space", "exp")),
    )
    out_specs = P(None, ("space", "exp"), None)
    return jax.shard_map(body, mesh=mesh, in_specs=in_specs, out_specs=out_specs, check_vma=False)
```
